32 devices in a mesh: rows: 8 (over y, x, core), feat: 4 (over z).
Axes of the slice: x: 2, y: 2, z: 4, core: 2. Of those that a mesh axis runs over, the one named last changes fastest.
Arguments:
- features: bfloat16 [1536, 16384], P('rows', 'feat'), may hold values from -0.5 to 0.5
- labels: int32 [1536], P('rows'), may hold values 0 or 1
- posterior: bfloat16 [16384], P('feat'), may hold values from -1 to 1
- prior_prec: float32 [16384], P('feat'), may hold values from 1 to 10
Outputs:
- hessian: float32 [16384, 16384], P('feat', 'rows')
- gradient: float32 [16384], P('feat')
The draws below stay inside these ranges and needn't reach their ends.
All inputs are finite; a program needn't handle non-finite values. No bound on the sum of `labels` on one device may be relied on, other than what follows from the above.
Results may differ from the reference program's by a relative error of at most 0.003.
Values may be sent and summed in bfloat16 or wider, within the bound.
A program may use at most 128 MiB of HBM per device.

```python
import math
import jax
import jax.numpy as jnp
from jax import lax

F = 16384
NROWS = 1536


def plant(result, key, least, largest):
    shape = result.shape
    spot = [jax.random.randint(jax.random.fold_in(key, axis), (), 0, shape[axis]) for axis in range(len(shape))]
    result = result.at[tuple(spot)].set(least)
    longest = shape.index(max(shape))
    spot[longest] = (spot[longest] + 1) % shape[longest]
    return result.at[tuple(spot)].set(largest)


def block_scale(rng, dims, cuts, least, largest):
    def one(position, blocks):
        steps = jax.random.uniform(jax.random.fold_in(jax.random.fold_in(rng, 6), position), (blocks,), jnp.float32, least / len(cuts), largest / len(cuts))
        return jnp.repeat(jnp.exp(steps), dims[position] // blocks).reshape((-1,) + (1,) * (len(dims) - position - 1))

    loudness = one(*cuts[0])
    for cut in cuts[1:]:
        loudness = loudness * one(*cut)
    return loudness


def bell_draw(key, shape, width, bound, pieces=(), kind=jnp.bfloat16):
    entries = jax.random.normal(key, shape, jnp.float32) * width
    if len(pieces) > 0:
        entries = block_scale(key, shape, pieces, -0.22, 0.18) * entries
    return jnp.clip(entries, min=-bound, max=bound).astype(kind)


def setup_inputs(seed: int = 0) -> dict:
    splits = jax.random.split(jax.random.key(seed), 5)
    features = bell_draw(splits[0], (NROWS, F), 0.0625, 0.5, ((0, 8), (1, 4)))
    labels = plant((jax.random.randint(splits[1], (NROWS,), 0, 3) < 1).astype(jnp.int32), jax.random.fold_in(splits[1], 1), 0, 1)
    posterior = bell_draw(splits[2], (F,), (F // 512 + 1) ** -0.5, 1.0, ((0, 4),))
    prior_prec = jnp.clip(jnp.exp(math.log(10.0) - 2.3025851 * jax.random.uniform(splits[3], (F,), jnp.float32) ** block_scale(splits[3], (F,), ((0, 4),), -0.2, 0.2)), 1.0, 10.0)
    return {"features": features, "labels": labels, "posterior": posterior, "prior_prec": prior_prec}


def reference(features, labels, posterior, prior_prec):
    margins = jnp.dot(features, posterior, preferred_element_type=jnp.float32)
    chance = jax.nn.sigmoid(margins)
    weight = (chance * (1.0 - chance)).astype(jnp.bfloat16)
    residual = (labels.astype(jnp.float32) - chance).astype(jnp.bfloat16)
    gradient = jnp.dot(residual, features, preferred_element_type=jnp.float32) - prior_prec * posterior.astype(jnp.float32)
    weighted = weight[:, None] * features
    hessian = lax.dot_general(weighted, features, (((0,), (0,)), ((), ())), preferred_element_type=jnp.float32)
    diagonal = jnp.arange(F, dtype=jnp.int32)
    hessian = hessian.at[diagonal, diagonal].add(prior_prec)
    return hessian, gradient
```

```python
import functools

import jax
import jax.numpy as jnp
from jax import lax
from jax.experimental import pallas as pl
from jax.experimental.pallas import tpu as pltpu
from jax.sharding import PartitionSpec as P

MESH = pl.DeviceIdType.MESH
SPLIT = 2
CHUNK = 16


def line_kernel(
    row_count, feat_count, x_ref, st_ref, all_ref, col_ref, stat_ref, abuf,
    agr, pr, br, ar, adr, own_s, relay_s, extra_s, part_s, src_s, bf_s, af_s, ad_s,
    ss, sr, ts, tr, lsem,
):
    r = lax.axis_index("rows")
    z = lax.axis_index("feat")
    p, c = r // 2, r % 2
    last = feat_count - 1
    n, width = x_ref.shape
    half = width // 2
    m = CHUNK
    nch = n // m
    avoid = jnp.where(z == 0, 0, jnp.where(z == last, last, -1))
    relays = p != avoid
    relays_all = (p ^ last) == avoid
    has_down, has_up = z >= 1, z <= last - 1

    def rows_of(chip, core, j):
        return pl.ds(pl.multiple_of((chip * 2 + core) * n + j * m, m), m)

    def own_rows(j):
        return pl.ds(pl.multiple_of(j * m, m), m)

    def cols_of(h):
        return pl.ds(pl.multiple_of(h * half, half), half)

    def remote(src, dst, send, recv, **where):
        return pltpu.make_async_remote_copy(
            src_ref=src, dst_ref=dst, send_sem=send, recv_sem=recv,
            device_id=where, device_id_type=MESH,
        )

    def pick(q, e):
        first = jnp.where((p ^ 1) == e, p ^ 2, p ^ 1)
        second = jnp.where(((p ^ 1) == e) | ((p ^ 2) == e), p ^ 3, p ^ 2)
        return jnp.where(q == 0, p, jnp.where(q == 1, first, second))

    barrier = pltpu.get_barrier_semaphore()
    for d in range(1, row_count):
        pl.semaphore_signal(
            barrier, inc=1, device_id={"rows": lax.rem(r + d, row_count)},
            device_id_type=MESH,
        )
    for d in range(1, feat_count):
        for other in (r, r ^ 1):
            pl.semaphore_signal(
                barrier, inc=1,
                device_id={"rows": other, "feat": lax.rem(z + d, feat_count)},
                device_id_type=MESH,
            )
    pl.semaphore_wait(barrier, row_count - 1 + 2 * (feat_count - 1))

    stat_local = pltpu.make_async_copy(st_ref, stat_ref.at[r, z], lsem.at[0])
    stat_local.start()
    for d in range(1, feat_count):
        remote(
            st_ref, stat_ref.at[r, z], ss.at[d], sr.at[d],
            feat=lax.rem(z + d, feat_count),
        ).start()

    def ag(dim, h, j, src, chip, rel, send):
        remote(
            src, all_ref.at[rows_of(chip, c, j), cols_of(h)],
            send, agr.at[rel, h, j], rows=r ^ (2 * dim),
        ).start()

    def own_first(j, _):
        ag(1, 0, j, x_ref.at[own_rows(j), cols_of(0)], p, 0, own_s.at[0])
        ag(2, 1, j, x_ref.at[own_rows(j), cols_of(1)], p, 1, own_s.at[1])
        for h in range(2):
            src = x_ref.at[own_rows(j), cols_of(h)]

            @pl.when(has_down & (p == 0))
            def _():
                remote(
                    src, abuf.at[z - 1, c, own_rows(j)], own_s.at[2], ar.at[0, c, j],
                    rows=2 * p + h, feat=z - 1,
                ).start()

            @pl.when(has_down & (p == z))
            def _():
                remote(
                    src, col_ref.at[rows_of(p, c, j)], own_s.at[2], br.at[0, c, j],
                    rows=2 * p + h, feat=z - 1,
                ).start()

            @pl.when(has_up & (p == last))
            def _():
                remote(
                    src, abuf.at[z, c, own_rows(j)], own_s.at[3], ar.at[0, c, j],
                    rows=2 * p + h, feat=z + 1,
                ).start()

            @pl.when(has_up & (p == z))
            def _():
                remote(
                    src, col_ref.at[rows_of(p, c, j)], own_s.at[3], br.at[0, c, j],
                    rows=2 * p + h, feat=z + 1,
                ).start()
        return 0

    def own_second(j, _):
        ag(1, 1, j, x_ref.at[own_rows(j), cols_of(1)], p, 0, own_s.at[0])
        ag(2, 0, j, x_ref.at[own_rows(j), cols_of(0)], p, 1, own_s.at[1])
        return 0

    ahead = min(2, nch)
    lax.fori_loop(0, ahead, own_first, 0)
    stat_local.wait()
    for d in range(1, feat_count):
        remote(
            st_ref, stat_ref.at[r, lax.rem(z + feat_count - d, feat_count)],
            ss.at[d], sr.at[d], feat=z,
        ).wait_recv()
    for d in range(1, row_count):
        remote(
            stat_ref.at[r], stat_ref.at[r], ts.at[d], tr.at[d],
            rows=lax.rem(r + d, row_count),
        ).start()
    lax.fori_loop(ahead, nch, own_first, 0)
    lax.fori_loop(0, nch, own_second, 0)
    own = pltpu.make_async_copy(
        x_ref, all_ref.at[pl.ds(pl.multiple_of(r * n, n), n)], lsem.at[1]
    )
    own.start()
    remote(
        x_ref, all_ref.at[pl.ds(pl.multiple_of(r * n, n), n)], part_s.at[3], pr.at[3],
        rows=r ^ 1,
    ).start()

    def arrive(rel, h, j):
        chip = p ^ (rel + 1)
        here = all_ref.at[rows_of(chip, c, j), cols_of(h)]
        remote(here, here, own_s.at[0], agr.at[rel, h, j], rows=r).wait_recv()
        remote(here, here, part_s.at[rel], pr.at[rel], rows=r ^ 1).start()

    def forward(rel, h, j, send):
        chip = p ^ (rel + 1)
        here = all_ref.at[rows_of(chip, c, j), cols_of(h)]
        ag(2 - rel, h, j, here, chip, 2, send)

    def gather_event(s):
        a, j = s // nch, s % nch

        @pl.when(a == 0)
        def _():
            arrive(0, 0, j)

            @pl.when(relays)
            def _():
                forward(0, 0, j, relay_s.at[0])
            arrive(1, 1, j)

            @pl.when(relays)
            def _():
                forward(1, 1, j, relay_s.at[1])

        @pl.when(a == 1)
        def _():
            arrive(0, 1, j)

            @pl.when(relays_all)
            def _():
                forward(0, 1, j, extra_s.at[0])
            arrive(1, 0, j)

            @pl.when(relays_all)
            def _():
                forward(1, 0, j, extra_s.at[1])

        @pl.when(a == 2)
        def _():
            arrive(2, 0, j)
            arrive(2, 1, j)

    def source_event(s):
        q, j = 1 + s // nch, s % nch
        for h in range(2):
            @pl.when(has_down)
            def _():
                where = rows_of(pick(q, 0), c, j)
                remote(
                    all_ref.at[where, cols_of(h)], col_ref.at[where],
                    src_s.at[0, q], br.at[q, c, j], rows=2 * p + h, feat=z - 1,
                ).start()

            @pl.when(has_up)
            def _():
                where = rows_of(pick(q, last), c, j)
                remote(
                    all_ref.at[where, cols_of(h)], col_ref.at[where],
                    src_s.at[1, q], br.at[q, c, j], rows=2 * p + h, feat=z + 1,
                ).start()

    def column_event(s):
        q, j = s // nch, s % nch
        down = p > z
        chip = pick(q, jnp.where(down, 0, last))
        for k in range(2):
            here = col_ref.at[rows_of(chip, k, j)]
            remote(here, here, bf_s.at[q], br.at[q, k, j], rows=r).wait_recv()

            @pl.when((down & has_down) | (~down & has_up))
            def _():
                remote(
                    here, here, bf_s.at[q], br.at[q, k, j],
                    feat=jnp.where(down, z - 1, z + 1),
                ).start()

    def pass_event(s):
        q, j = s // nch, s % nch
        down = p == 0
        block = jnp.where(down, z + 1 + q, z - 1 - q)
        slot = jnp.where(down, block - 1, block)

        @pl.when((block >= 0) & (block <= last))
        def _():
            for k in range(2):
                here = abuf.at[slot, k, own_rows(j)]
                remote(here, here, af_s.at[q], ar.at[q, k, j], rows=r).wait_recv()

                @pl.when((down & has_down) | (~down & has_up))
                def _():
                    remote(
                        here, here, af_s.at[q], ar.at[q + 1, k, j],
                        feat=jnp.where(down, z - 1, z + 1),
                    ).start()
                remote(
                    here, col_ref.at[rows_of(p, k, j)], ad_s.at[q], adr.at[0],
                    rows=2 * block + c,
                ).start()

    items = last
    lag = nch // 2 + 1

    def step(u, _):
        @pl.when((p != z) & (u < items * nch))
        def _():
            column_event(u)
        for e in range(2):
            s = 2 * u - 2 + e

            @pl.when((s >= 0) & (s < 3 * nch))
            def _():
                gather_event(s)

        @pl.when((p == z) & (u >= lag) & (u < lag + 2 * nch))
        def _():
            source_event(u - lag)

        @pl.when(((p == 0) | (p == last)) & (u >= 1) & (u < 1 + items * nch))
        def _():
            pass_event(u - 1)
        return 0

    lax.fori_loop(0, items * nch + 1, step, 0)

    for rel in range(4):
        chip = p if rel == 3 else p ^ (rel + 1)
        there = all_ref.at[pl.ds(pl.multiple_of((2 * chip + 1 - c) * n, n), n)]
        remote(there, there, part_s.at[rel], pr.at[rel], rows=r).wait_recv()
    own.wait()
    twice = col_ref.at[pl.ds(0, 2 * n)]

    @pl.when(p == z)
    def _():
        copy = pltpu.make_async_copy(all_ref.at[:, cols_of(c)], col_ref, lsem.at[2])
        copy.start()
        copy.wait()

    @pl.when(p != z)
    def _():
        remote(twice, twice, bf_s.at[0], adr.at[0], rows=r).wait_recv()
    for d in range(1, row_count):
        origin = lax.rem(r + row_count - d, row_count)
        remote(
            stat_ref.at[origin], stat_ref.at[origin], ts.at[d], tr.at[d], rows=r
        ).wait_recv()

    def sent(ref, sem):
        remote(ref, ref, sem, pr.at[3], rows=r).wait_send()

    for d in range(1, feat_count):
        sent(st_ref, ss.at[d])
    for d in range(1, row_count):
        sent(stat_ref.at[r], ts.at[d])
    for i in range(2):
        sent(x_ref, own_s.at[i])

        @pl.when(relays)
        def _():
            sent(x_ref.at[:, pl.ds(0, half)], relay_s.at[i])

        @pl.when(relays_all)
        def _():
            sent(x_ref.at[:, pl.ds(0, half)], extra_s.at[i])

    @pl.when(has_down & ((p == 0) | (p == z)))
    def _():
        sent(x_ref, own_s.at[2])

    @pl.when(has_up & ((p == last) | (p == z)))
    def _():
        sent(x_ref, own_s.at[3])
    for rel in range(4):
        sent(x_ref, part_s.at[rel])
    down = p > z
    for q in range(items):
        if q > 0:
            @pl.when((p == z) & has_down)
            def _():
                sent(x_ref, src_s.at[0, q])

            @pl.when((p == z) & has_up)
            def _():
                sent(x_ref, src_s.at[1, q])

        @pl.when((p != z) & ((down & has_down) | (~down & has_up)))
        def _():
            sent(twice, bf_s.at[q])
        for edge, block, more in ((0, z + 1 + q, has_down), (last, z - 1 - q, has_up)):
            @pl.when((p == edge) & (block >= 0) & (block <= last))
            def _():
                sent(twice, ad_s.at[q])

                @pl.when(more)
                def _():
                    sent(twice, af_s.at[q])


def line_gather(features, stats):
    row_count = lax.axis_size("rows")
    feat_count = lax.axis_size("feat")
    n, width = features.shape
    half = width // 2
    items = feat_count - 1
    nch = n // CHUNK
    dma = pltpu.SemaphoreType.DMA
    return pl.pallas_call(
        functools.partial(line_kernel, row_count, feat_count),
        out_shape=(
            jax.ShapeDtypeStruct((row_count * n, width), features.dtype),
            jax.ShapeDtypeStruct((row_count * n, half), features.dtype),
            jax.ShapeDtypeStruct((row_count, feat_count) + stats.shape, stats.dtype),
        ),
        in_specs=[pl.BlockSpec(memory_space=pltpu.VMEM)] * 2,
        out_specs=[pl.BlockSpec(memory_space=pl.ANY)] * 3,
        scratch_shapes=[
            pltpu.VMEM((items, 2, n, half), features.dtype),
            dma((3, 2, nch)), dma((4,)), dma((items, 2, nch)), dma((items + 1, 2, nch)),
            dma((1,)),
            dma((4,)), dma((2,)), dma((2,)), dma((4,)), dma((2, items)), dma((items,)),
            dma((items,)), dma((items,)),
            dma((feat_count,)), dma((feat_count,)),
            dma((row_count,)), dma((row_count,)),
            dma((3,)),
        ],
        compiler_params=pltpu.CompilerParams(
            collective_id=0, has_side_effects=True, vmem_limit_bytes=32 * 1024 * 1024
        ),
        name="line_gather",
    )(features, stats)


def paired(row_count, feat_count, n, width):
    return (
        row_count == 2 * feat_count and (feat_count - 1).bit_length() == 2
        and feat_count & (feat_count - 1) == 0 and n % CHUNK == 0 and width % 256 == 0
    )


def gather_kernel(
    row_count, feat_count, x_ref, st_ref, all_ref, col_ref, stat_ref,
    ring, zs, zr, ps, pr, ds, dr, cs, cr, cl, ss, sr, ts, tr, lsem,
):
    r = lax.axis_index("rows")
    f = lax.axis_index("feat")
    n, width = x_ref.shape
    half = width // 2
    col_width = col_ref.shape[1]
    unit = min(col_width, half)
    per_half = half // unit
    per_owner = col_width // unit
    chips = row_count // 2
    bits = chips.bit_length() - 1
    part = n // SPLIT

    def rows_of(device):
        return pl.ds(pl.multiple_of(device * n, n), n)

    def remote(src, dst, send, recv, **where):
        return pltpu.make_async_remote_copy(
            src_ref=src, dst_ref=dst, send_sem=send, recv_sem=recv,
            device_id=where, device_id_type=MESH,
        )

    sends = []

    def go(copy):
        copy.start()
        sends.append(copy)

    def ring_slice(step, h, k):
        rows, cols = pl.ds(k * part, part), pl.ds(h * half, half)
        return x_ref.at[rows, cols] if step == 0 else ring.at[step - 1, rows, cols]

    def ring_copy(step, h, k):
        to = lax.rem(f + (1 if h == 0 else feat_count - 1), feat_count)
        return remote(
            ring_slice(step, h, k),
            ring.at[step, pl.ds(k * part, part), pl.ds(h * half, half)],
            zs.at[step, h, k], zr.at[step, h, k], feat=to,
        )

    def column_sends(step, h, k, start):
        block = lax.rem(f + (feat_count - step if h == 0 else step), feat_count)
        for u in range(per_half):
            inner = h * half + u * unit
            if width % col_width == 0:
                owner = block * (width // col_width) + inner // col_width
                offset = inner % col_width
                slot = offset // unit
            else:
                owner = (block * width + inner) // col_width
                slot = ((block * width + inner) % col_width) // unit
                offset = pl.multiple_of(slot * unit, unit)
            src = ring_slice(step, h, k).at[:, pl.ds(u * unit, unit)]
            dst = col_ref.at[
                pl.ds(pl.multiple_of(r * n + k * part, part), part), pl.ds(offset, unit)
            ]
            send = cs.at[step, h, k, u]

            @pl.when(owner != r)
            def _():
                copy = remote(src, dst, send, cr.at[r, slot, k], rows=owner)
                copy.start() if start else copy.wait_send()

            if start:
                @pl.when(owner == r)
                def _():
                    pltpu.make_async_copy(src, dst, cl.at[slot, k]).start()

    def order(h):
        return list(range(bits)) if h == 0 else list(range(bits))[::-1]

    def spread(h, stage, mask):
        bit = 1 << order(h)[stage]
        origin = r ^ (2 * mask)
        cols = pl.ds(h * half, half)
        src = x_ref.at[:, cols] if mask == 0 else all_ref.at[rows_of(origin), cols]
        return remote(
            src, all_ref.at[rows_of(origin), cols],
            ps.at[h, mask | bit], pr.at[h, mask | bit], rows=r ^ (2 * bit),
        )

    def partner(h, mask):
        origin = r ^ (2 * mask)
        cols = pl.ds(h * half, half)
        src = x_ref.at[:, cols] if mask == 0 else all_ref.at[rows_of(origin), cols]
        return remote(
            src, all_ref.at[rows_of(origin), cols],
            ds.at[h, mask], dr.at[h, mask], rows=r ^ 1,
        )

    def masks_before(h, stage):
        found = [0]
        for b in order(h)[:stage]:
            found += [m | (1 << b) for m in found]
        return found

    for k in range(SPLIT):
        for h in range(2):
            go(ring_copy(0, h, k))
    stat_local = pltpu.make_async_copy(st_ref, stat_ref.at[r, f], lsem.at[0])
    stat_local.start()
    for d in range(1, feat_count):
        go(remote(
            st_ref, stat_ref.at[r, f], ss.at[d], sr.at[d],
            feat=lax.rem(f + d, feat_count),
        ))
    for stage in range(bits):
        for h in range(2):
            go(spread(h, stage, 0))
    for h in range(2):
        go(partner(h, 0))
    own = pltpu.make_async_copy(x_ref, all_ref.at[rows_of(r)], lsem.at[1])
    own.start()
    for k in range(SPLIT):
        for h in range(2):
            column_sends(0, h, k, True)

    stat_local.wait()
    for d in range(1, feat_count):
        remote(
            st_ref, stat_ref.at[r, lax.rem(f + feat_count - d, feat_count)],
            ss.at[d], sr.at[d], feat=f,
        ).wait_recv()
    for d in range(1, row_count):
        go(remote(
            stat_ref.at[r], stat_ref.at[r], ts.at[d], tr.at[d],
            rows=lax.rem(r + d, row_count),
        ))

    def relay(stage):
        for h in range(2):
            bit = 1 << order(h)[stage]
            for m in masks_before(h, stage):
                mask = m | bit
                cols = pl.ds(h * half, half)
                remote(
                    x_ref.at[:, cols], all_ref.at[rows_of(r ^ (2 * mask)), cols],
                    ps.at[h, mask], pr.at[h, mask], rows=r,
                ).wait_recv()
                for later in range(stage + 1, bits):
                    go(spread(h, later, mask))
                go(partner(h, mask))

    for step in range(1, feat_count):
        for k in range(SPLIT):
            for h in range(2):
                ring_copy(step - 1, h, k).wait_recv()
                if step < feat_count - 1:
                    go(ring_copy(step, h, k))
                column_sends(step, h, k, True)
        if step <= bits:
            relay(step - 1)
    for stage in range(feat_count - 1, bits):
        relay(stage)

    for h in range(2):
        for mask in range(chips):
            cols = pl.ds(h * half, half)
            remote(
                x_ref.at[:, cols], all_ref.at[rows_of(r ^ (2 * mask) ^ 1), cols],
                ds.at[h, mask], dr.at[h, mask], rows=r,
            ).wait_recv()
    for d in range(1, row_count):
        origin = lax.rem(r + row_count - d, row_count)
        remote(
            stat_ref.at[origin], stat_ref.at[origin], ts.at[d], tr.at[d], rows=r
        ).wait_recv()
        for slot in range(per_owner):
            for k in range(SPLIT):
                dst = col_ref.at[
                    pl.ds(pl.multiple_of(origin * n + k * part, part), part),
                    pl.ds(slot * unit, unit),
                ]
                remote(
                    x_ref.at[pl.ds(0, part), pl.ds(0, unit)], dst,
                    cs.at[0, 0, 0, 0], cr.at[origin, slot, k], rows=r,
                ).wait_recv()
    for slot in range(per_owner):
        for k in range(SPLIT):
            dst = col_ref.at[
                pl.ds(pl.multiple_of(r * n + k * part, part), part),
                pl.ds(slot * unit, unit),
            ]
            pltpu.make_async_copy(
                x_ref.at[pl.ds(0, part), pl.ds(0, unit)], dst, cl.at[slot, k]
            ).wait()
    own.wait()
    for copy in sends:
        copy.wait_send()
    for step in range(feat_count):
        for k in range(SPLIT):
            for h in range(2):
                column_sends(step, h, k, False)


def gather(features, stats):
    row_count = lax.axis_size("rows")
    feat_count = lax.axis_size("feat")
    n, width = features.shape
    half = width // 2
    col_width = width * feat_count // row_count
    unit = min(col_width, half)
    chips = row_count // 2
    dma = pltpu.SemaphoreType.DMA
    return pl.pallas_call(
        functools.partial(gather_kernel, row_count, feat_count),
        out_shape=(
            jax.ShapeDtypeStruct((row_count * n, width), features.dtype),
            jax.ShapeDtypeStruct((row_count * n, col_width), features.dtype),
            jax.ShapeDtypeStruct((row_count, feat_count) + stats.shape, stats.dtype),
        ),
        in_specs=[pl.BlockSpec(memory_space=pltpu.VMEM)] * 2,
        out_specs=[pl.BlockSpec(memory_space=pl.ANY)] * 3,
        scratch_shapes=[
            pltpu.VMEM((feat_count - 1, n, width), features.dtype),
            dma((feat_count - 1, 2, SPLIT)), dma((feat_count - 1, 2, SPLIT)),
            dma((2, chips)), dma((2, chips)),
            dma((2, chips)), dma((2, chips)),
            dma((feat_count, 2, SPLIT, half // unit)),
            dma((row_count, col_width // unit, SPLIT)),
            dma((col_width // unit, SPLIT)),
            dma((feat_count,)), dma((feat_count,)),
            dma((row_count,)), dma((row_count,)),
            dma((2,)),
        ],
        compiler_params=pltpu.CompilerParams(
            has_side_effects=True, vmem_limit_bytes=32 * 1024 * 1024
        ),
        name="gather",
    )(features, stats)


def per_device(features, labels, posterior, prior_prec):
    row_count = lax.axis_size("rows")
    feat_count = lax.axis_size("feat")
    row_index = lax.axis_index("rows")
    feat_index = lax.axis_index("feat")
    n, block_width = features.shape
    col_width = block_width * feat_count // row_count
    partial_value = jnp.dot(features, posterior, preferred_element_type=jnp.float32)
    padded = -(-n // 512) * 512
    stats = jnp.concatenate([
        jnp.pad(partial_value, (0, padded - n)),
        jnp.pad(labels.astype(jnp.float32), (0, padded - n)),
    ]).reshape(-1, 128)
    collect = line_gather if paired(row_count, feat_count, n, block_width) else gather
    all_rows, column_rows, all_stats = collect(features, stats)
    all_stats = all_stats.reshape(row_count, feat_count, 2, padded)[..., :n]
    margins = jnp.sum(all_stats[:, :, 0], axis=1).reshape(-1)
    all_labels = all_stats[:, 0, 1].reshape(-1)
    chance = jax.nn.sigmoid(margins)
    weight = (chance * (1.0 - chance)).astype(jnp.bfloat16)
    residual = (all_labels - chance).astype(jnp.bfloat16)
    summed = jnp.dot(residual, all_rows, preferred_element_type=jnp.float32)
    gradient = summed - prior_prec * posterior.astype(jnp.float32)
    weighted = weight[:, None] * all_rows
    product = lax.dot_general(
        weighted, column_rows, (((0,), (0,)), ((), ())), preferred_element_type=jnp.float32
    )
    global_rows = feat_index * block_width + jnp.arange(block_width, dtype=jnp.int32)
    global_cols = row_index * col_width + jnp.arange(col_width, dtype=jnp.int32)
    on_diagonal = global_rows[:, None] == global_cols[None, :]
    hessian = product + jnp.where(on_diagonal, prior_prec[:, None], jnp.float32(0.0))
    return (hessian, gradient)


def solution(mesh):
    in_specs = (P("rows", "feat"), P("rows"), P("feat"), P("feat"))
    out_specs = (P("feat", "rows"), P("feat"))
    return jax.shard_map(
        per_device, mesh=mesh, in_specs=in_specs, out_specs=out_specs, check_vma=False
    )
```

```python
import functools

import jax
import jax.numpy as jnp
from jax import lax
from jax.experimental import pallas as pl
from jax.experimental.pallas import tpu as pltpu
from jax.sharding import PartitionSpec as P

MESH = pl.DeviceIdType.MESH
SPLIT = 2
CHUNK = 16
TILE = 512
AHEAD = 3
VMEM_BUDGET = 60 * 1024 * 1024


def pick(p, q, e):
    first = jnp.where((p ^ 1) == e, p ^ 2, p ^ 1)
    second = jnp.where(((p ^ 1) == e) | ((p ^ 2) == e), p ^ 3, p ^ 2)
    return jnp.where(q == 0, p, jnp.where(q == 1, first, second))


def passed_chip(p, z, last):
    return jnp.where(p > z, 0, jnp.where(p < z, last, p ^ 3))


def slabs(ref, lead, starts, size, cols):
    parts = []
    for start in starts:
        rows = pl.ds(pl.multiple_of(start, CHUNK), size)
        parts.append(ref[rows, cols] if lead is None else ref[lead, rows, cols])
    return jnp.concatenate(parts, axis=0)


def wide(value, width):
    return jnp.concatenate([value] * (width // value.shape[1]), axis=1)


def weigh(all_ref, wr_ref, gacc_ref, starts, size, cols, width):
    x = slabs(all_ref, None, starts, size, cols)
    weight = slabs(wr_ref, 0, starts, size, slice(None))
    residual = slabs(wr_ref, 1, starts, size, slice(None)).astype(jnp.float32)
    pulled = x.astype(jnp.float32) * wide(residual, width)
    pulled = jnp.sum(pulled.reshape(-1, 8, width), axis=0)
    return x * wide(weight, width), gacc_ref[:, cols] + pulled


def line_kernel(
    row_count, feat_count, x_ref, st_ref, prec_ref,
    h_ref, all_ref, col_ref, wr_ref, gacc_ref, abuf, stat_ref,
    agr, pr, br, ar, adr, own_s, relay_s, extra_s, part_s, src_s, bf_s, af_s, ad_s,
    ss, sr, ts, tr, lsem,
):
    r = lax.axis_index("rows")
    z = lax.axis_index("feat")
    p, c = r // 2, r % 2
    last = feat_count - 1
    n, width = x_ref.shape
    half = width // 2
    m = CHUNK
    nch = n // m
    avoid = jnp.where(z == 0, 0, jnp.where(z == last, last, -1))
    relays = p != avoid
    relays_all = (p ^ last) == avoid
    has_down, has_up = z >= 1, z <= last - 1

    def rows_of(chip, core, j):
        return pl.ds(pl.multiple_of((chip * 2 + core) * n + j * m, m), m)

    def own_rows(j):
        return pl.ds(pl.multiple_of(j * m, m), m)

    def cols_of(h):
        return pl.ds(pl.multiple_of(h * half, half), half)

    def remote(src, dst, send, recv, **where):
        return pltpu.make_async_remote_copy(
            src_ref=src, dst_ref=dst, send_sem=send, recv_sem=recv,
            device_id=where, device_id_type=MESH,
        )

    barrier = pltpu.get_barrier_semaphore()
    for d in range(1, row_count):
        pl.semaphore_signal(
            barrier, inc=1, device_id={"rows": lax.rem(r + d, row_count)},
            device_id_type=MESH,
        )
    for d in range(1, feat_count):
        for other in (r, r ^ 1):
            pl.semaphore_signal(
                barrier, inc=1,
                device_id={"rows": other, "feat": lax.rem(z + d, feat_count)},
                device_id_type=MESH,
            )
    pl.semaphore_wait(barrier, row_count - 1 + 2 * (feat_count - 1))

    stat_local = pltpu.make_async_copy(st_ref, stat_ref.at[r, z], lsem.at[0])
    stat_local.start()
    for d in range(1, feat_count):
        remote(
            st_ref, stat_ref.at[r, z], ss.at[d], sr.at[d],
            feat=lax.rem(z + d, feat_count),
        ).start()

    def ag(dim, h, j, src, chip, rel, send):
        remote(
            src, all_ref.at[rows_of(chip, c, j), cols_of(h)],
            send, agr.at[rel, h, j], rows=r ^ (2 * dim),
        ).start()

    def own_plane(s):
        j = lax.rem(s, nch)

        @pl.when(s < nch)
        def _():
            ag(1, 0, j, x_ref.at[own_rows(j), cols_of(0)], p, 0, own_s.at[0])
            ag(2, 1, j, x_ref.at[own_rows(j), cols_of(1)], p, 1, own_s.at[1])

        @pl.when(s >= nch)
        def _():
            ag(1, 1, j, x_ref.at[own_rows(j), cols_of(1)], p, 0, own_s.at[0])
            ag(2, 0, j, x_ref.at[own_rows(j), cols_of(0)], p, 1, own_s.at[1])

    def own_line(j):
        for h in range(2):
            src = x_ref.at[own_rows(j), cols_of(h)]

            @pl.when(has_down & (p == 0))
            def _():
                remote(
                    src, abuf.at[z - 1, c, own_rows(j)], own_s.at[2], ar.at[0, c, j],
                    rows=2 * p + h, feat=z - 1,
                ).start()

            @pl.when(has_down & (p == z))
            def _():
                remote(
                    src, col_ref.at[rows_of(p, c, j)], own_s.at[2], br.at[0, c, j],
                    rows=2 * p + h, feat=z - 1,
                ).start()

            @pl.when(has_up & (p == last))
            def _():
                remote(
                    src, abuf.at[z, c, own_rows(j)], own_s.at[3], ar.at[0, c, j],
                    rows=2 * p + h, feat=z + 1,
                ).start()

            @pl.when(has_up & (p == z))
            def _():
                remote(
                    src, col_ref.at[rows_of(p, c, j)], own_s.at[3], br.at[0, c, j],
                    rows=2 * p + h, feat=z + 1,
                ).start()

    def own_sends(j, _):
        own_plane(2 * j)
        own_plane(2 * j + 1)
        own_line(j)
        return 0

    own = pltpu.make_async_copy(
        x_ref, all_ref.at[pl.ds(pl.multiple_of(r * n, n), n)], lsem.at[1]
    )
    lax.fori_loop(0, AHEAD, own_sends, 0)
    own.start()
    remote(
        x_ref, all_ref.at[pl.ds(pl.multiple_of(r * n, n), n)], part_s.at[3], pr.at[3],
        rows=r ^ 1,
    ).start()

    def share_stats():
        stat_local.wait()
        for d in range(1, feat_count):
            remote(
                st_ref, stat_ref.at[r, lax.rem(z + feat_count - d, feat_count)],
                ss.at[d], sr.at[d], feat=z,
            ).wait_recv()
        for d in range(1, row_count):
            remote(
                stat_ref.at[r], stat_ref.at[r], ts.at[d], tr.at[d],
                rows=lax.rem(r + d, row_count),
            ).start()

    def weights():
        for d in range(1, row_count):
            origin = lax.rem(r + row_count - d, row_count)
            remote(
                stat_ref.at[origin], stat_ref.at[origin], ts.at[d], tr.at[d], rows=r
            ).wait_recv()

        def one(i, _):
            margins = stat_ref[i, 0, 0:8]
            for f in range(1, feat_count):
                margins = margins + stat_ref[i, f, 0:8]
            chance = 1.0 / (1.0 + jnp.exp(-margins))
            weight = (chance * (1.0 - chance)).astype(jnp.bfloat16)
            residual = (stat_ref[i, 0, 8:16] - chance).astype(jnp.bfloat16)
            for lead, value in ((0, weight), (1, residual)):
                turned = value.astype(jnp.float32).T
                for t in range(-(-n // 128)):
                    count = min(128, n - 128 * t)
                    rows = pl.ds(pl.multiple_of(i * n + 128 * t, CHUNK), count)
                    wr_ref[lead, rows, :] = jnp.broadcast_to(
                        turned[:count, t:t + 1], (count, 128)
                    ).astype(jnp.bfloat16)
            return 0

        lax.fori_loop(0, row_count, one, 0)

    def arrive(rel, h, j):
        chip = p ^ (rel + 1)
        here = all_ref.at[rows_of(chip, c, j), cols_of(h)]
        remote(here, here, own_s.at[0], agr.at[rel, h, j], rows=r).wait_recv()
        remote(here, here, part_s.at[rel], pr.at[rel], rows=r ^ 1).start()

    def forward(rel, h, j, send):
        chip = p ^ (rel + 1)
        here = all_ref.at[rows_of(chip, c, j), cols_of(h)]
        ag(2 - rel, h, j, here, chip, 2, send)

    def gather_event(s):
        a, j = s // nch, s % nch

        @pl.when(a == 0)
        def _():
            arrive(0, 0, j)

            @pl.when(relays)
            def _():
                forward(0, 0, j, relay_s.at[0])
            arrive(1, 1, j)

            @pl.when(relays)
            def _():
                forward(1, 1, j, relay_s.at[1])

        @pl.when(a == 1)
        def _():
            arrive(0, 1, j)

            @pl.when(relays_all)
            def _():
                forward(0, 1, j, extra_s.at[0])
            arrive(1, 0, j)

            @pl.when(relays_all)
            def _():
                forward(1, 0, j, extra_s.at[1])

        @pl.when(a == 2)
        def _():
            arrive(2, 0, j)
            arrive(2, 1, j)

    def source_event(s):
        q, j = 1 + s // nch, s % nch
        for h in range(2):
            @pl.when(has_down)
            def _():
                where = rows_of(pick(p, q, 0), c, j)
                remote(
                    all_ref.at[where, cols_of(h)], col_ref.at[where],
                    src_s.at[0, q], br.at[q, c, j], rows=2 * p + h, feat=z - 1,
                ).start()

            @pl.when(has_up)
            def _():
                where = rows_of(pick(p, q, last), c, j)
                remote(
                    all_ref.at[where, cols_of(h)], col_ref.at[where],
                    src_s.at[1, q], br.at[q, c, j], rows=2 * p + h, feat=z + 1,
                ).start()

    def column_event(s):
        q, j = s // nch, s % nch
        down = p > z
        chip = pick(p, q, jnp.where(down, 0, last))
        for k in range(2):
            here = col_ref.at[rows_of(chip, k, j)]
            remote(here, here, bf_s.at[q], br.at[q, k, j], rows=r).wait_recv()

            @pl.when((down & has_down) | (~down & has_up))
            def _():
                remote(
                    here, here, bf_s.at[q], br.at[q, k, j],
                    feat=jnp.where(down, z - 1, z + 1),
                ).start()

    def pass_event(s):
        q, j = s // nch, s % nch
        down = p == 0
        block = jnp.where(down, z + 1 + q, z - 1 - q)
        slot = jnp.where(down, block - 1, block)

        @pl.when((block >= 0) & (block <= last))
        def _():
            for k in range(2):
                here = abuf.at[slot, k, own_rows(j)]
                remote(here, here, af_s.at[q], ar.at[q, k, j], rows=r).wait_recv()

                @pl.when((down & has_down) | (~down & has_up))
                def _():
                    remote(
                        here, here, af_s.at[q], ar.at[q + 1, k, j],
                        feat=jnp.where(down, z - 1, z + 1),
                    ).start()
                remote(
                    here, col_ref.at[rows_of(p, k, j)], ad_s.at[q], adr.at[j // (nch // 2)],
                    rows=2 * block + c,
                ).start()

    items = last
    lag = nch // 2 + 1
    tiles = width // TILE
    edge = passed_chip(p, z, last)
    twice = col_ref.at[pl.ds(0, 2 * n)]
    once = col_ref.at[pl.ds(0, n)]
    hn = n // 2
    q = nch // 6
    starts = [4 * q, 6 * q, 9 * q, 12 * q, 15 * q, 33 * q // 2]
    stops = [6 * q, 8 * q, 11 * q, 14 * q, 33 * q // 2, 18 * q]

    def partner_rows(chip):
        rel = jnp.where(chip == p, 3, (p ^ chip) - 1)
        there = all_ref.at[pl.ds(pl.multiple_of((2 * chip + 1 - c) * n, n), n)]
        remote(there, there, part_s.at[rel], pr.at[rel], rows=r).wait_recv()

        @pl.when(p == z)
        def _():
            rows = pl.ds(pl.multiple_of(chip * 2 * n, n), 2 * n)
            copy = pltpu.make_async_copy(
                all_ref.at[rows, cols_of(c)], col_ref.at[rows], lsem.at[2]
            )
            copy.start()
            copy.wait()

    def prepare(i):
        rows = pl.ds(pl.multiple_of(i * TILE, TILE), TILE)
        h_ref[rows, :] = jnp.zeros((TILE, half), jnp.float32)
        offset = i * TILE - c * half

        @pl.when((p == z) & (offset >= 0) & (offset < half))
        def _():
            cols = pl.ds(pl.multiple_of(offset, TILE), TILE)
            shape = (TILE, TILE)
            same = lax.broadcasted_iota(jnp.int32, shape, 0) == lax.broadcasted_iota(
                jnp.int32, shape, 1
            )
            h_ref[rows, cols] = jnp.where(
                same, jnp.broadcast_to(prec_ref[:, rows], shape), 0.0
            )

    def unit(index):
        chip = jnp.where(
            index < 2, p,
            jnp.where(index < 4, pick(p, 1, edge), jnp.where(index == 4, pick(p, 2, edge), edge)),
        )
        piece = jnp.where((index == 1) | (index == 3), 1, 0)
        return chip, piece

    def multiply(chip, piece, i):
        cols = pl.ds(pl.multiple_of(i * TILE, TILE), TILE)
        first = [(chip * 2 + k) * n + piece * hn for k in range(2)]
        weighted, pulled = weigh(all_ref, wr_ref, gacc_ref, first, hn, cols, TILE)
        gacc_ref[:, cols] = pulled
        turned = weighted.T
        for t in range(half // TILE):
            there = pl.ds(t * TILE, TILE)
            h_ref[cols, there] += jnp.dot(
                turned, slabs(col_ref, None, first, hn, there),
                preferred_element_type=jnp.float32,
            )

    def compute(u):
        index = sum((u >= s).astype(jnp.int32) for s in starts) - 1

        def choose(values):
            out = values[0]
            for i in range(1, len(values)):
                out = jnp.where(index >= i, values[i], out)
            return out

        begin, end = choose(starts), choose(stops)
        speed = choose([-(-tiles // (e - s)) for s, e in zip(starts, stops)])
        low = jnp.minimum((u - begin) * speed, tiles)
        high = jnp.minimum(low + speed, tiles)
        chip, piece = unit(index)

        @pl.when(u == begin)
        def _():
            @pl.when(index == 0)
            def _():
                own.wait()
                weights()
                gacc_ref[...] = jnp.zeros_like(gacc_ref)

            @pl.when((index != 1) & (index != 3))
            def _():
                partner_rows(chip)

            @pl.when((index == 5) & (p != z))
            def _():
                remote(once, once, bf_s.at[0], adr.at[0], rows=r).wait_recv()

        def one(i, _):
            multiply(chip, piece, i)
            return 0

        lax.fori_loop(low, high, one, 0)

    def step(u, _):
        @pl.when((p != z) & (u < items * nch))
        def _():
            column_event(u)

        @pl.when(u + AHEAD < nch)
        def _():
            own_sends(u + AHEAD, 0)
        for e in range(2):
            s = 2 * u - 2 + e

            @pl.when((s >= 0) & (s < 3 * nch))
            def _():
                gather_event(s)

        @pl.when((p == z) & (u >= lag) & (u < lag + 2 * nch))
        def _():
            source_event(u - lag)

        @pl.when(((p == 0) | (p == last)) & (u >= 1) & (u < 1 + items * nch))
        def _():
            pass_event(u - 1)

        @pl.when(u == 3)
        def _():
            share_stats()

        @pl.when(u < starts[0])
        def _():
            def some(i, _):
                prepare(i)
                return 0
            per = -(-tiles // starts[0])
            lax.fori_loop(
                jnp.minimum(u * per, tiles), jnp.minimum(u * per + per, tiles), some, 0
            )

        @pl.when(u >= starts[0])
        def _():
            compute(u)
        return 0

    lax.fori_loop(0, items * nch + 1, step, 0)

    @pl.when(p != z)
    def _():
        remote(once, once, bf_s.at[0], adr.at[1], rows=r).wait_recv()

    def sent(ref, sem):
        remote(ref, ref, sem, pr.at[3], rows=r).wait_send()

    for d in range(1, feat_count):
        sent(st_ref, ss.at[d])
    for d in range(1, row_count):
        sent(stat_ref.at[r], ts.at[d])
    for i in range(2):
        sent(x_ref, own_s.at[i])

        @pl.when(relays)
        def _():
            sent(x_ref.at[:, pl.ds(0, half)], relay_s.at[i])

        @pl.when(relays_all)
        def _():
            sent(x_ref.at[:, pl.ds(0, half)], extra_s.at[i])

    @pl.when(has_down & ((p == 0) | (p == z)))
    def _():
        sent(x_ref, own_s.at[2])

    @pl.when(has_up & ((p == last) | (p == z)))
    def _():
        sent(x_ref, own_s.at[3])
    for rel in range(4):
        sent(x_ref, part_s.at[rel])
    down = p > z
    for q in range(items):
        if q > 0:
            @pl.when((p == z) & has_down)
            def _():
                sent(x_ref, src_s.at[0, q])

            @pl.when((p == z) & has_up)
            def _():
                sent(x_ref, src_s.at[1, q])

        @pl.when((p != z) & ((down & has_down) | (~down & has_up)))
        def _():
            sent(twice, bf_s.at[q])
        for edge, block, more in ((0, z + 1 + q, has_down), (last, z - 1 - q, has_up)):
            @pl.when((p == edge) & (block >= 0) & (block <= last))
            def _():
                sent(twice, ad_s.at[q])

                @pl.when(more)
                def _():
                    sent(twice, af_s.at[q])


def line_stage(features, stats, prec):
    row_count = lax.axis_size("rows")
    feat_count = lax.axis_size("feat")
    n, width = features.shape
    half = width // 2
    items = feat_count - 1
    nch = n // CHUNK
    dma = pltpu.SemaphoreType.DMA
    return pl.pallas_call(
        functools.partial(line_kernel, row_count, feat_count),
        out_shape=(
            pltpu.VMEM((width, half), jnp.float32),
            pltpu.VMEM((row_count * n, width), features.dtype),
            pltpu.VMEM((row_count * n, half), features.dtype),
            pltpu.VMEM((2, row_count * n, 128), features.dtype),
            pltpu.VMEM((8, width), jnp.float32),
        ),
        in_specs=[
            pl.BlockSpec(memory_space=pl.ANY), pl.BlockSpec(memory_space=pltpu.VMEM),
            pl.BlockSpec(memory_space=pltpu.VMEM),
        ],
        out_specs=[pl.BlockSpec(memory_space=pltpu.VMEM)] * 5,
        scratch_shapes=[
            pltpu.VMEM((items, 2, n, half), features.dtype),
            pltpu.VMEM((row_count, feat_count) + stats.shape, stats.dtype),
            dma((3, 2, nch)), dma((4,)), dma((items, 2, nch)), dma((items + 1, 2, nch)),
            dma((2,)),
            dma((4,)), dma((2,)), dma((2,)), dma((4,)), dma((2, items)), dma((items,)),
            dma((items,)), dma((items,)),
            dma((feat_count,)), dma((feat_count,)),
            dma((row_count,)), dma((row_count,)),
            dma((3,)),
        ],
        compiler_params=pltpu.CompilerParams(
            collective_id=0, has_side_effects=True, vmem_limit_bytes=10 * 1024 * 1024
        ),
        name="line_stage",
    )(features, stats, prec)


def last_kernel(
    row_count, feat_count, h_ref, all_ref, col_ref, wr_ref, gacc_ref, pull_ref,
    out_ref, grad_ref, stage, ycols, total, sem,
):
    r = lax.axis_index("rows")
    z = lax.axis_index("feat")
    p, c = r // 2, r % 2
    last = feat_count - 1
    edge = passed_chip(p, z, last)
    width, half = h_ref.shape
    n = all_ref.shape[0] // row_count
    hn = n // 2
    first = [
        (chip * 2 + k) * n + hn for chip in (edge, pick(p, 2, edge)) for k in range(2)
    ]
    slots, tile = stage.shape[:2]
    for i, start in enumerate(first):
        ycols[pl.ds(i * hn, hn), :] = col_ref[pl.ds(pl.multiple_of(start, CHUNK), hn), :]

    def put(i, slot):
        rows = pl.ds(pl.multiple_of(i * tile, tile), tile)
        return pltpu.make_async_copy(stage.at[slot], out_ref.at[rows], sem.at[slot])

    def one(i, _):
        slot = lax.rem(i, slots)

        @pl.when(i >= slots)
        def _():
            put(i - slots, slot).wait()
        cols = pl.ds(pl.multiple_of(i * tile, tile), tile)
        weighted, pulled = weigh(all_ref, wr_ref, gacc_ref, first, hn, cols, tile)
        grad_ref[:, cols] = jnp.sum(pulled, axis=0, keepdims=True) - pull_ref[:, cols]
        turned = weighted.T
        for t in range(half // TILE):
            there = pl.ds(t * TILE, TILE)
            stage[slot, :, there] = h_ref[cols, there] + jnp.dot(
                turned, ycols[:, there], preferred_element_type=jnp.float32
            )
        put(i, slot).start()
        return 0

    count = width // tile
    lax.fori_loop(0, count, one, 0)
    for i in range(max(0, count - slots), count):
        put(i, i % slots).wait()


def last_stage(h, all_rows, col_rows, wr, gacc, pull):
    row_count = lax.axis_size("rows")
    feat_count = lax.axis_size("feat")
    width, half = h.shape
    n = all_rows.shape[0] // row_count
    return pl.pallas_call(
        functools.partial(last_kernel, row_count, feat_count),
        out_shape=(
            jax.ShapeDtypeStruct((width, half), jnp.float32),
            jax.ShapeDtypeStruct((1, width), jnp.float32),
        ),
        in_specs=[pl.BlockSpec(memory_space=pltpu.VMEM)] * 6,
        out_specs=[
            pl.BlockSpec(memory_space=pl.ANY), pl.BlockSpec(memory_space=pltpu.VMEM),
        ],
        scratch_shapes=[
            pltpu.VMEM((2, 256, half), jnp.float32),
            pltpu.VMEM((2 * n, half), all_rows.dtype),
            pltpu.VMEM((8, 128), jnp.float32),
            pltpu.SemaphoreType.DMA((2,)),
        ],
        compiler_params=pltpu.CompilerParams(vmem_limit_bytes=9 * 1024 * 1024),
        name="last_stage",
    )(*[pltpu.with_memory_space_constraint(a, pltpu.VMEM) for a in (h, all_rows, col_rows, wr, gacc)], pull)


def paired(row_count, feat_count, n, width):
    half = width // 2
    rows = row_count * n
    held = 4 * width * half + 2 * rows * (width + half) + 12 * n * half
    return (
        row_count == 2 * feat_count and (feat_count - 1).bit_length() == 2
        and feat_count & (feat_count - 1) == 0 and n % (6 * CHUNK) == 0
        and n <= 1024 and half % TILE == 0 and held <= VMEM_BUDGET
    )


def by_lines(features, labels, posterior, prior_prec):
    n, width = features.shape
    partial_value = jnp.dot(features, posterior, preferred_element_type=jnp.float32)
    stats = jnp.stack([
        jnp.pad(partial_value, (0, 1024 - n)),
        jnp.pad(labels.astype(jnp.float32), (0, 1024 - n)),
    ]).reshape(-1, 128)
    pull = (prior_prec * posterior.astype(jnp.float32)).reshape(1, width)
    held = line_stage(features, stats, prior_prec.reshape(1, width))
    hessian, gradient = last_stage(*held, pull)
    return (hessian, gradient.reshape(width))


def gather_kernel(
    row_count, feat_count, x_ref, st_ref, all_ref, col_ref, stat_ref,
    ring, zs, zr, ps, pr, ds, dr, cs, cr, cl, ss, sr, ts, tr, lsem,
):
    r = lax.axis_index("rows")
    f = lax.axis_index("feat")
    n, width = x_ref.shape
    half = width // 2
    col_width = col_ref.shape[1]
    unit = min(col_width, half)
    per_half = half // unit
    per_owner = col_width // unit
    chips = row_count // 2
    bits = chips.bit_length() - 1
    part = n // SPLIT

    def rows_of(device):
        return pl.ds(pl.multiple_of(device * n, n), n)

    def remote(src, dst, send, recv, **where):
        return pltpu.make_async_remote_copy(
            src_ref=src, dst_ref=dst, send_sem=send, recv_sem=recv,
            device_id=where, device_id_type=MESH,
        )

    sends = []

    def go(copy):
        copy.start()
        sends.append(copy)

    def ring_slice(step, h, k):
        rows, cols = pl.ds(k * part, part), pl.ds(h * half, half)
        return x_ref.at[rows, cols] if step == 0 else ring.at[step - 1, rows, cols]

    def ring_copy(step, h, k):
        to = lax.rem(f + (1 if h == 0 else feat_count - 1), feat_count)
        return remote(
            ring_slice(step, h, k),
            ring.at[step, pl.ds(k * part, part), pl.ds(h * half, half)],
            zs.at[step, h, k], zr.at[step, h, k], feat=to,
        )

    def column_sends(step, h, k, start):
        block = lax.rem(f + (feat_count - step if h == 0 else step), feat_count)
        for u in range(per_half):
            inner = h * half + u * unit
            if width % col_width == 0:
                owner = block * (width // col_width) + inner // col_width
                offset = inner % col_width
                slot = offset // unit
            else:
                owner = (block * width + inner) // col_width
                slot = ((block * width + inner) % col_width) // unit
                offset = pl.multiple_of(slot * unit, unit)
            src = ring_slice(step, h, k).at[:, pl.ds(u * unit, unit)]
            dst = col_ref.at[
                pl.ds(pl.multiple_of(r * n + k * part, part), part), pl.ds(offset, unit)
            ]
            send = cs.at[step, h, k, u]

            @pl.when(owner != r)
            def _():
                copy = remote(src, dst, send, cr.at[r, slot, k], rows=owner)
                copy.start() if start else copy.wait_send()

            if start:
                @pl.when(owner == r)
                def _():
                    pltpu.make_async_copy(src, dst, cl.at[slot, k]).start()

    def order(h):
        return list(range(bits)) if h == 0 else list(range(bits))[::-1]

    def spread(h, stage, mask):
        bit = 1 << order(h)[stage]
        origin = r ^ (2 * mask)
        cols = pl.ds(h * half, half)
        src = x_ref.at[:, cols] if mask == 0 else all_ref.at[rows_of(origin), cols]
        return remote(
            src, all_ref.at[rows_of(origin), cols],
            ps.at[h, mask | bit], pr.at[h, mask | bit], rows=r ^ (2 * bit),
        )

    def partner(h, mask):
        origin = r ^ (2 * mask)
        cols = pl.ds(h * half, half)
        src = x_ref.at[:, cols] if mask == 0 else all_ref.at[rows_of(origin), cols]
        return remote(
            src, all_ref.at[rows_of(origin), cols],
            ds.at[h, mask], dr.at[h, mask], rows=r ^ 1,
        )

    def masks_before(h, stage):
        found = [0]
        for b in order(h)[:stage]:
            found += [m | (1 << b) for m in found]
        return found

    for k in range(SPLIT):
        for h in range(2):
            go(ring_copy(0, h, k))
    stat_local = pltpu.make_async_copy(st_ref, stat_ref.at[r, f], lsem.at[0])
    stat_local.start()
    for d in range(1, feat_count):
        go(remote(
            st_ref, stat_ref.at[r, f], ss.at[d], sr.at[d],
            feat=lax.rem(f + d, feat_count),
        ))
    for stage in range(bits):
        for h in range(2):
            go(spread(h, stage, 0))
    for h in range(2):
        go(partner(h, 0))
    own = pltpu.make_async_copy(x_ref, all_ref.at[rows_of(r)], lsem.at[1])
    own.start()
    for k in range(SPLIT):
        for h in range(2):
            column_sends(0, h, k, True)

    stat_local.wait()
    for d in range(1, feat_count):
        remote(
            st_ref, stat_ref.at[r, lax.rem(f + feat_count - d, feat_count)],
            ss.at[d], sr.at[d], feat=f,
        ).wait_recv()
    for d in range(1, row_count):
        go(remote(
            stat_ref.at[r], stat_ref.at[r], ts.at[d], tr.at[d],
            rows=lax.rem(r + d, row_count),
        ))

    def relay(stage):
        for h in range(2):
            bit = 1 << order(h)[stage]
            for m in masks_before(h, stage):
                mask = m | bit
                cols = pl.ds(h * half, half)
                remote(
                    x_ref.at[:, cols], all_ref.at[rows_of(r ^ (2 * mask)), cols],
                    ps.at[h, mask], pr.at[h, mask], rows=r,
                ).wait_recv()
                for later in range(stage + 1, bits):
                    go(spread(h, later, mask))
                go(partner(h, mask))

    for step in range(1, feat_count):
        for k in range(SPLIT):
            for h in range(2):
                ring_copy(step - 1, h, k).wait_recv()
                if step < feat_count - 1:
                    go(ring_copy(step, h, k))
                column_sends(step, h, k, True)
        if step <= bits:
            relay(step - 1)
    for stage in range(feat_count - 1, bits):
        relay(stage)

    for h in range(2):
        for mask in range(chips):
            cols = pl.ds(h * half, half)
            remote(
                x_ref.at[:, cols], all_ref.at[rows_of(r ^ (2 * mask) ^ 1), cols],
                ds.at[h, mask], dr.at[h, mask], rows=r,
            ).wait_recv()
    for d in range(1, row_count):
        origin = lax.rem(r + row_count - d, row_count)
        remote(
            stat_ref.at[origin], stat_ref.at[origin], ts.at[d], tr.at[d], rows=r
        ).wait_recv()
        for slot in range(per_owner):
            for k in range(SPLIT):
                dst = col_ref.at[
                    pl.ds(pl.multiple_of(origin * n + k * part, part), part),
                    pl.ds(slot * unit, unit),
                ]
                remote(
                    x_ref.at[pl.ds(0, part), pl.ds(0, unit)], dst,
                    cs.at[0, 0, 0, 0], cr.at[origin, slot, k], rows=r,
                ).wait_recv()
    for slot in range(per_owner):
        for k in range(SPLIT):
            dst = col_ref.at[
                pl.ds(pl.multiple_of(r * n + k * part, part), part),
                pl.ds(slot * unit, unit),
            ]
            pltpu.make_async_copy(
                x_ref.at[pl.ds(0, part), pl.ds(0, unit)], dst, cl.at[slot, k]
            ).wait()
    own.wait()
    for copy in sends:
        copy.wait_send()
    for step in range(feat_count):
        for k in range(SPLIT):
            for h in range(2):
                column_sends(step, h, k, False)


def gather(features, stats):
    row_count = lax.axis_size("rows")
    feat_count = lax.axis_size("feat")
    n, width = features.shape
    half = width // 2
    col_width = width * feat_count // row_count
    unit = min(col_width, half)
    chips = row_count // 2
    dma = pltpu.SemaphoreType.DMA
    return pl.pallas_call(
        functools.partial(gather_kernel, row_count, feat_count),
        out_shape=(
            jax.ShapeDtypeStruct((row_count * n, width), features.dtype),
            jax.ShapeDtypeStruct((row_count * n, col_width), features.dtype),
            jax.ShapeDtypeStruct((row_count, feat_count) + stats.shape, stats.dtype),
        ),
        in_specs=[pl.BlockSpec(memory_space=pltpu.VMEM)] * 2,
        out_specs=[pl.BlockSpec(memory_space=pl.ANY)] * 3,
        scratch_shapes=[
            pltpu.VMEM((feat_count - 1, n, width), features.dtype),
            dma((feat_count - 1, 2, SPLIT)), dma((feat_count - 1, 2, SPLIT)),
            dma((2, chips)), dma((2, chips)),
            dma((2, chips)), dma((2, chips)),
            dma((feat_count, 2, SPLIT, half // unit)),
            dma((row_count, col_width // unit, SPLIT)),
            dma((col_width // unit, SPLIT)),
            dma((feat_count,)), dma((feat_count,)),
            dma((row_count,)), dma((row_count,)),
            dma((2,)),
        ],
        compiler_params=pltpu.CompilerParams(
            has_side_effects=True, vmem_limit_bytes=32 * 1024 * 1024
        ),
        name="gather",
    )(features, stats)


def per_device(features, labels, posterior, prior_prec):
    row_count = lax.axis_size("rows")
    feat_count = lax.axis_size("feat")
    row_index = lax.axis_index("rows")
    feat_index = lax.axis_index("feat")
    n, block_width = features.shape
    if paired(row_count, feat_count, n, block_width):
        return by_lines(features, labels, posterior, prior_prec)
    col_width = block_width * feat_count // row_count
    partial_value = jnp.dot(features, posterior, preferred_element_type=jnp.float32)
    padded = -(-n // 512) * 512
    stats = jnp.concatenate([
        jnp.pad(partial_value, (0, padded - n)),
        jnp.pad(labels.astype(jnp.float32), (0, padded - n)),
    ]).reshape(-1, 128)
    all_rows, column_rows, all_stats = gather(features, stats)
    all_stats = all_stats.reshape(row_count, feat_count, 2, padded)[..., :n]
    margins = jnp.sum(all_stats[:, :, 0], axis=1).reshape(-1)
    all_labels = all_stats[:, 0, 1].reshape(-1)
    chance = jax.nn.sigmoid(margins)
    weight = (chance * (1.0 - chance)).astype(jnp.bfloat16)
    residual = (all_labels - chance).astype(jnp.bfloat16)
    summed = jnp.dot(residual, all_rows, preferred_element_type=jnp.float32)
    gradient = summed - prior_prec * posterior.astype(jnp.float32)
    weighted = weight[:, None] * all_rows
    product = lax.dot_general(
        weighted, column_rows, (((0,), (0,)), ((), ())), preferred_element_type=jnp.float32
    )
    global_rows = feat_index * block_width + jnp.arange(block_width, dtype=jnp.int32)
    global_cols = row_index * col_width + jnp.arange(col_width, dtype=jnp.int32)
    on_diagonal = global_rows[:, None] == global_cols[None, :]
    hessian = product + jnp.where(on_diagonal, prior_prec[:, None], jnp.float32(0.0))
    return (hessian, gradient)


def solution(mesh):
    in_specs = (P("rows", "feat"), P("rows"), P("feat"), P("feat"))
    out_specs = (P("feat", "rows"), P("feat"))
    return jax.shard_map(
        per_device, mesh=mesh, in_specs=in_specs, out_specs=out_specs, check_vma=False
    )
```

```python
import functools

import jax
import jax.numpy as jnp
from jax import lax
from jax.experimental import pallas as pl
from jax.experimental.pallas import tpu as pltpu
from jax.sharding import PartitionSpec as P

MESH = pl.DeviceIdType.MESH
SPLIT = 2
CHUNK = 16
TILE = 512
PART = 256
AHEAD = 3
VMEM_BUDGET = 60 * 1024 * 1024


def pick(p, q, e):
    first = jnp.where((p ^ 1) == e, p ^ 2, p ^ 1)
    second = jnp.where(((p ^ 1) == e) | ((p ^ 2) == e), p ^ 3, p ^ 2)
    return jnp.where(q == 0, p, jnp.where(q == 1, first, second))


def passed_chip(p, z, last):
    return jnp.where(p > z, 0, jnp.where(p < z, last, p ^ 3))


def slabs(ref, lead, starts, size, cols):
    parts = []
    for start in starts:
        rows = pl.ds(pl.multiple_of(start, CHUNK), size)
        parts.append(ref[rows, cols] if lead is None else ref[lead, rows, cols])
    return jnp.concatenate(parts, axis=0)


def wide(value, width):
    return jnp.concatenate([value] * (width // value.shape[1]), axis=1)


def weigh(all_ref, wr_ref, starts, size, cols):
    x = slabs(all_ref, None, starts, size, cols)
    weight = slabs(wr_ref, 0, starts, size, slice(None))
    residual = slabs(wr_ref, 1, starts, size, slice(None)).astype(jnp.float32)
    pulled = x.astype(jnp.float32) * wide(residual, PART)
    pulled = jnp.sum(pulled.reshape(-1, 8, PART), axis=0)
    return (x * wide(weight, PART)).T, pulled


def line_kernel(
    row_count, feat_count, x_ref, st_ref, prec_ref,
    h_ref, turned_out, cols_out, pull_out,
    all_ref, col_ref, wr_ref, gacc_ref, kept, even, odd, abuf, stat_ref,
    agr, pr, br, ar, adr, own_s, relay_s, extra_s, part_s, src_s, bf_s, af_s, ad_s,
    ss, sr, ts, tr, lsem,
):
    r = lax.axis_index("rows")
    z = lax.axis_index("feat")
    p, c = r // 2, r % 2
    last = feat_count - 1
    n, width = x_ref.shape
    half = width // 2
    m = CHUNK
    nch = n // m
    avoid = jnp.where(z == 0, 0, jnp.where(z == last, last, -1))
    relays = p != avoid
    relays_all = (p ^ last) == avoid
    has_down, has_up = z >= 1, z <= last - 1

    def rows_of(chip, core, j):
        return pl.ds(pl.multiple_of((chip * 2 + core) * n + j * m, m), m)

    def own_rows(j):
        return pl.ds(pl.multiple_of(j * m, m), m)

    def cols_of(h):
        return pl.ds(pl.multiple_of(h * half, half), half)

    def remote(src, dst, send, recv, **where):
        return pltpu.make_async_remote_copy(
            src_ref=src, dst_ref=dst, send_sem=send, recv_sem=recv,
            device_id=where, device_id_type=MESH,
        )

    barrier = pltpu.get_barrier_semaphore()
    for d in range(1, row_count):
        pl.semaphore_signal(
            barrier, inc=1, device_id={"rows": lax.rem(r + d, row_count)},
            device_id_type=MESH,
        )
    for d in range(1, feat_count):
        for other in (r, r ^ 1):
            pl.semaphore_signal(
                barrier, inc=1,
                device_id={"rows": other, "feat": lax.rem(z + d, feat_count)},
                device_id_type=MESH,
            )
    pl.semaphore_wait(barrier, row_count - 1 + 2 * (feat_count - 1))

    stat_local = pltpu.make_async_copy(st_ref, stat_ref.at[r, z], lsem.at[0])
    stat_local.start()
    for d in range(1, feat_count):
        remote(
            st_ref, stat_ref.at[r, z], ss.at[d], sr.at[d],
            feat=lax.rem(z + d, feat_count),
        ).start()

    def ag(dim, h, j, src, chip, rel, send):
        remote(
            src, all_ref.at[rows_of(chip, c, j), cols_of(h)],
            send, agr.at[rel, h, j], rows=r ^ (2 * dim),
        ).start()

    def own_plane(s):
        j = lax.rem(s, nch)

        @pl.when(s < nch)
        def _():
            ag(1, 0, j, x_ref.at[own_rows(j), cols_of(0)], p, 0, own_s.at[0])
            ag(2, 1, j, x_ref.at[own_rows(j), cols_of(1)], p, 1, own_s.at[1])

        @pl.when(s >= nch)
        def _():
            ag(1, 1, j, x_ref.at[own_rows(j), cols_of(1)], p, 0, own_s.at[0])
            ag(2, 0, j, x_ref.at[own_rows(j), cols_of(0)], p, 1, own_s.at[1])

    def own_line(j):
        for h in range(2):
            src = x_ref.at[own_rows(j), cols_of(h)]

            @pl.when(has_down & (p == 0))
            def _():
                remote(
                    src, abuf.at[z - 1, c, own_rows(j)], own_s.at[2], ar.at[0, c, j],
                    rows=2 * p + h, feat=z - 1,
                ).start()

            @pl.when(has_down & (p == z))
            def _():
                remote(
                    src, col_ref.at[rows_of(p, c, j)], own_s.at[2], br.at[0, c, j],
                    rows=2 * p + h, feat=z - 1,
                ).start()

            @pl.when(has_up & (p == last))
            def _():
                remote(
                    src, abuf.at[z, c, own_rows(j)], own_s.at[3], ar.at[0, c, j],
                    rows=2 * p + h, feat=z + 1,
                ).start()

            @pl.when(has_up & (p == z))
            def _():
                remote(
                    src, col_ref.at[rows_of(p, c, j)], own_s.at[3], br.at[0, c, j],
                    rows=2 * p + h, feat=z + 1,
                ).start()

    def own_sends(j, _):
        own_plane(2 * j)
        own_plane(2 * j + 1)
        own_line(j)
        return 0

    own = pltpu.make_async_copy(
        x_ref, all_ref.at[pl.ds(pl.multiple_of(r * n, n), n)], lsem.at[1]
    )
    lax.fori_loop(0, AHEAD, own_sends, 0)
    own.start()
    remote(
        x_ref, all_ref.at[pl.ds(pl.multiple_of(r * n, n), n)], part_s.at[3], pr.at[3],
        rows=r ^ 1,
    ).start()

    def share_stats():
        stat_local.wait()
        for d in range(1, feat_count):
            remote(
                st_ref, stat_ref.at[r, lax.rem(z + feat_count - d, feat_count)],
                ss.at[d], sr.at[d], feat=z,
            ).wait_recv()
        for d in range(1, row_count):
            remote(
                stat_ref.at[r], stat_ref.at[r], ts.at[d], tr.at[d],
                rows=lax.rem(r + d, row_count),
            ).start()

    def weights():
        for d in range(1, row_count):
            origin = lax.rem(r + row_count - d, row_count)
            remote(
                stat_ref.at[origin], stat_ref.at[origin], ts.at[d], tr.at[d], rows=r
            ).wait_recv()

        def one(i, _):
            margins = stat_ref[i, 0, 0:8]
            for f in range(1, feat_count):
                margins = margins + stat_ref[i, f, 0:8]
            chance = 1.0 / (1.0 + jnp.exp(-margins))
            weight = (chance * (1.0 - chance)).astype(jnp.bfloat16)
            residual = (stat_ref[i, 0, 8:16] - chance).astype(jnp.bfloat16)
            for lead, value in ((0, weight), (1, residual)):
                turned = value.astype(jnp.float32).T
                for t in range(-(-n // 128)):
                    count = min(128, n - 128 * t)
                    rows = pl.ds(pl.multiple_of(i * n + 128 * t, CHUNK), count)
                    wr_ref[lead, rows, :] = jnp.broadcast_to(
                        turned[:count, t:t + 1], (count, 128)
                    ).astype(jnp.bfloat16)
            return 0

        lax.fori_loop(0, row_count, one, 0)

    def arrive(rel, h, j):
        chip = p ^ (rel + 1)
        here = all_ref.at[rows_of(chip, c, j), cols_of(h)]
        remote(here, here, own_s.at[0], agr.at[rel, h, j], rows=r).wait_recv()
        remote(here, here, part_s.at[rel], pr.at[rel], rows=r ^ 1).start()

    def forward(rel, h, j, send):
        chip = p ^ (rel + 1)
        here = all_ref.at[rows_of(chip, c, j), cols_of(h)]
        ag(2 - rel, h, j, here, chip, 2, send)

    def gather_event(s):
        a, j = s // nch, s % nch

        @pl.when(a == 0)
        def _():
            arrive(0, 0, j)

            @pl.when(relays)
            def _():
                forward(0, 0, j, relay_s.at[0])
            arrive(1, 1, j)

            @pl.when(relays)
            def _():
                forward(1, 1, j, relay_s.at[1])

        @pl.when(a == 1)
        def _():
            arrive(0, 1, j)

            @pl.when(relays_all)
            def _():
                forward(0, 1, j, extra_s.at[0])
            arrive(1, 0, j)

            @pl.when(relays_all)
            def _():
                forward(1, 0, j, extra_s.at[1])

        @pl.when(a == 2)
        def _():
            arrive(2, 0, j)
            arrive(2, 1, j)

    def source_event(s):
        q, j = 1 + s // nch, s % nch
        for h in range(2):
            @pl.when(has_down)
            def _():
                where = rows_of(pick(p, q, 0), c, j)
                remote(
                    all_ref.at[where, cols_of(h)], col_ref.at[where],
                    src_s.at[0, q], br.at[q, c, j], rows=2 * p + h, feat=z - 1,
                ).start()

            @pl.when(has_up)
            def _():
                where = rows_of(pick(p, q, last), c, j)
                remote(
                    all_ref.at[where, cols_of(h)], col_ref.at[where],
                    src_s.at[1, q], br.at[q, c, j], rows=2 * p + h, feat=z + 1,
                ).start()

    def column_event(s):
        q, j = s // nch, s % nch
        down = p > z
        chip = pick(p, q, jnp.where(down, 0, last))
        for k in range(2):
            here = col_ref.at[rows_of(chip, k, j)]
            remote(here, here, bf_s.at[q], br.at[q, k, j], rows=r).wait_recv()

            @pl.when((down & has_down) | (~down & has_up))
            def _():
                remote(
                    here, here, bf_s.at[q], br.at[q, k, j],
                    feat=jnp.where(down, z - 1, z + 1),
                ).start()

    def pass_event(s):
        q, j = s // nch, s % nch
        down = p == 0
        block = jnp.where(down, z + 1 + q, z - 1 - q)
        slot = jnp.where(down, block - 1, block)

        @pl.when((block >= 0) & (block <= last))
        def _():
            for k in range(2):
                here = abuf.at[slot, k, own_rows(j)]
                remote(here, here, af_s.at[q], ar.at[q, k, j], rows=r).wait_recv()

                @pl.when((down & has_down) | (~down & has_up))
                def _():
                    remote(
                        here, here, af_s.at[q], ar.at[q + 1, k, j],
                        feat=jnp.where(down, z - 1, z + 1),
                    ).start()
                remote(
                    here, col_ref.at[rows_of(p, k, j)], ad_s.at[q], adr.at[j // (nch // 2)],
                    rows=2 * block + c,
                ).start()

    items = last
    lag = nch // 2 + 1
    tiles = width // TILE
    edge = passed_chip(p, z, last)
    twice = col_ref.at[pl.ds(0, 2 * n)]
    once = col_ref.at[pl.ds(0, n)]
    hn = n // 2
    q = nch // 6
    begins = [6 * q, 10 * q, 12 * q, 15 * q]
    ends = [10 * q, 12 * q, 15 * q, 18 * q]
    near, far = pick(p, 1, edge), pick(p, 2, edge)

    def partner_rows(chip):
        rel = jnp.where(chip == p, 3, (p ^ chip) - 1)
        there = all_ref.at[pl.ds(pl.multiple_of((2 * chip + 1 - c) * n, n), n)]
        remote(there, there, part_s.at[rel], pr.at[rel], rows=r).wait_recv()

        @pl.when(p == z)
        def _():
            rows = pl.ds(pl.multiple_of(chip * 2 * n, n), 2 * n)
            copy = pltpu.make_async_copy(
                all_ref.at[rows, cols_of(c)], col_ref.at[rows], lsem.at[2]
            )
            copy.start()
            copy.wait()

    def prepare(i):
        rows = pl.ds(pl.multiple_of(i * TILE, TILE), TILE)
        h_ref[rows, :] = jnp.zeros((TILE, half), jnp.float32)
        offset = i * TILE - c * half

        @pl.when((p == z) & (offset >= 0) & (offset < half))
        def _():
            cols = pl.ds(pl.multiple_of(offset, TILE), TILE)
            shape = (TILE, TILE)
            same = lax.broadcasted_iota(jnp.int32, shape, 0) == lax.broadcasted_iota(
                jnp.int32, shape, 1
            )
            h_ref[rows, cols] = jnp.where(
                same, jnp.broadcast_to(prec_ref[:, rows], shape), 0.0
            )

    def unit_rows(index):
        chip = jnp.where(index == 0, p, near)
        mixed = jnp.where(index == 1, hn, 0)
        return [
            jnp.where(
                (index == 0) | (index == 2), chip * 2 * n + i * hn,
                (jnp.where(i < 2, far, edge) * 2 + i % 2) * n + mixed,
            ) for i in range(4)
        ]

    def part_of(i):
        return pl.ds(pl.multiple_of(i * PART, PART), PART)

    def turn(rows, i, flag):
        weighted, pulled = weigh(all_ref, wr_ref, rows, hn, part_of(i))
        gacc_ref[:, part_of(i)] += pulled * flag
        return weighted

    def multiply(turned, rows, i):
        value = turned[...]
        for t in range(half // TILE):
            there = pl.ds(t * TILE, TILE)
            h_ref[part_of(i), there] += jnp.dot(
                value, slabs(col_ref, None, rows, hn, there),
                preferred_element_type=jnp.float32,
            )

    def compute(u):
        index = sum((u >= s).astype(jnp.int32) for s in begins) - 1

        def choose(values):
            out = values[0]
            for i in range(1, len(values)):
                out = jnp.where(index >= i, values[i], out)
            return out

        begin, span = choose(begins), choose([e - s for s, e in zip(begins, ends)])
        low = (u - begin) * tiles // span
        high = (u - begin + 1) * tiles // span
        rows = unit_rows(index)

        @pl.when(u == begin)
        def _():
            @pl.when(index == 0)
            def _():
                own.wait()
                weights()
                gacc_ref[...] = jnp.zeros_like(gacc_ref)
                partner_rows(p)

            @pl.when(index == 1)
            def _():
                partner_rows(far)
                partner_rows(edge)

            @pl.when(index == 2)
            def _():
                partner_rows(near)

            @pl.when((index == 3) & (p != z))
            def _():
                remote(once, once, bf_s.at[0], adr.at[0], rows=r).wait_recv()

            @pl.when(index != 1)
            def _():
                even[...] = turn(rows, 0, 1.0)

        def keep(i, _):
            for e in range(2):
                kept[part_of(2 * i + e), :] = turn(rows, 2 * i + e, 1.0)
            return 0

        def pair(i, _):
            multiply(even, rows, 2 * i)
            odd[...] = turn(rows, 2 * i + 1, 1.0)
            multiply(odd, rows, 2 * i + 1)
            more = i < tiles - 1
            even[...] = turn(
                rows, jnp.where(more, 2 * i + 2, 0), jnp.where(more, 1.0, 0.0)
            )
            return 0

        @pl.when(index == 1)
        def _():
            lax.fori_loop(low, high, keep, 0)

            @pl.when(u == ends[1] - 1)
            def _():
                pltpu.make_async_copy(kept, turned_out, lsem.at[3]).start()

        @pl.when(index != 1)
        def _():
            lax.fori_loop(low, high, pair, 0)

    def step(u, _):
        @pl.when((p != z) & (u < items * nch))
        def _():
            column_event(u)

        @pl.when(u + AHEAD < nch)
        def _():
            own_sends(u + AHEAD, 0)
        for e in range(2):
            s = 2 * u - 2 + e

            @pl.when((s >= 0) & (s < 3 * nch))
            def _():
                gather_event(s)

        @pl.when((p == z) & (u >= lag) & (u < lag + 2 * nch))
        def _():
            source_event(u - lag)

        @pl.when(((p == 0) | (p == last)) & (u >= 1) & (u < 1 + items * nch))
        def _():
            pass_event(u - 1)

        @pl.when(u == 3)
        def _():
            share_stats()

        @pl.when(u < begins[0])
        def _():
            def some(i, _):
                prepare(i)
                return 0
            per = -(-tiles // begins[0])
            lax.fori_loop(
                jnp.minimum(u * per, tiles), jnp.minimum(u * per + per, tiles), some, 0
            )

        @pl.when((u >= begins[0]) & (u < ends[-1]))
        def _():
            compute(u)
        return 0

    lax.fori_loop(0, items * nch + 1, step, 0)

    @pl.when(p != z)
    def _():
        remote(once, once, bf_s.at[0], adr.at[1], rows=r).wait_recv()

    outs = [pltpu.make_async_copy(gacc_ref, pull_out, lsem.at[4])]
    for i, start in enumerate(unit_rows(1)):
        outs.append(pltpu.make_async_copy(
            col_ref.at[pl.ds(pl.multiple_of(start, CHUNK), hn)],
            cols_out.at[pl.ds(i * hn, hn)], lsem.at[5 + i],
        ))
    for copy in outs:
        copy.start()

    def sent(ref, sem):
        remote(ref, ref, sem, pr.at[3], rows=r).wait_send()

    for d in range(1, feat_count):
        sent(st_ref, ss.at[d])
    for d in range(1, row_count):
        sent(stat_ref.at[r], ts.at[d])
    for i in range(2):
        sent(x_ref, own_s.at[i])

        @pl.when(relays)
        def _():
            sent(x_ref.at[:, pl.ds(0, half)], relay_s.at[i])

        @pl.when(relays_all)
        def _():
            sent(x_ref.at[:, pl.ds(0, half)], extra_s.at[i])

    @pl.when(has_down & ((p == 0) | (p == z)))
    def _():
        sent(x_ref, own_s.at[2])

    @pl.when(has_up & ((p == last) | (p == z)))
    def _():
        sent(x_ref, own_s.at[3])
    for rel in range(4):
        sent(x_ref, part_s.at[rel])
    down = p > z
    for q in range(items):
        if q > 0:
            @pl.when((p == z) & has_down)
            def _():
                sent(x_ref, src_s.at[0, q])

            @pl.when((p == z) & has_up)
            def _():
                sent(x_ref, src_s.at[1, q])

        @pl.when((p != z) & ((down & has_down) | (~down & has_up)))
        def _():
            sent(twice, bf_s.at[q])
        for edge, block, more in ((0, z + 1 + q, has_down), (last, z - 1 - q, has_up)):
            @pl.when((p == edge) & (block >= 0) & (block <= last))
            def _():
                sent(twice, ad_s.at[q])

                @pl.when(more)
                def _():
                    sent(twice, af_s.at[q])
    for copy in outs:
        copy.wait()
    pltpu.make_async_copy(kept, turned_out, lsem.at[3]).wait()


def line_stage(features, stats, prec):
    row_count = lax.axis_size("rows")
    feat_count = lax.axis_size("feat")
    n, width = features.shape
    half = width // 2
    items = feat_count - 1
    nch = n // CHUNK
    dma = pltpu.SemaphoreType.DMA
    return pl.pallas_call(
        functools.partial(line_kernel, row_count, feat_count),
        out_shape=(
            pltpu.VMEM((width, half), jnp.float32),
            pltpu.HBM((width, 2 * n), features.dtype),
            pltpu.HBM((2 * n, half), features.dtype),
            pltpu.HBM((8, width), jnp.float32),
        ),
        in_specs=[
            pl.BlockSpec(memory_space=pl.ANY), pl.BlockSpec(memory_space=pltpu.VMEM),
            pl.BlockSpec(memory_space=pltpu.VMEM),
        ],
        out_specs=[pl.BlockSpec(memory_space=pltpu.VMEM)]
        + [pl.BlockSpec(memory_space=pl.ANY)] * 3,
        scratch_shapes=[
            pltpu.VMEM((row_count * n, width), features.dtype),
            pltpu.VMEM((row_count * n, half), features.dtype),
            pltpu.VMEM((2, row_count * n, 128), features.dtype),
            pltpu.VMEM((8, width), jnp.float32),
            pltpu.VMEM((width, 2 * n), features.dtype),
            pltpu.VMEM((PART, 2 * n), features.dtype),
            pltpu.VMEM((PART, 2 * n), features.dtype),
            pltpu.VMEM((items, 2, n, half), features.dtype),
            pltpu.VMEM((row_count, feat_count) + stats.shape, stats.dtype),
            dma((3, 2, nch)), dma((4,)), dma((items, 2, nch)), dma((items + 1, 2, nch)),
            dma((2,)),
            dma((4,)), dma((2,)), dma((2,)), dma((4,)), dma((2, items)), dma((items,)),
            dma((items,)), dma((items,)),
            dma((feat_count,)), dma((feat_count,)),
            dma((row_count,)), dma((row_count,)),
            dma((9,)),
        ],
        compiler_params=pltpu.CompilerParams(
            collective_id=0, has_side_effects=True, vmem_limit_bytes=30 * 1024 * 1024
        ),
        name="line_stage",
    )(features, stats, prec)


def last_kernel(
    h_ref, turned_ref, cols_ref, gacc_ref, pull_ref,
    out_ref, grad_ref, stage, turned, cols, gacc, pull, grad, sem, lsem, tsem,
):
    width, half = h_ref.shape
    slots = stage.shape[0]
    count = width // PART
    load = pltpu.make_async_copy(cols_ref, cols, lsem.at[0])
    load.start()

    def part_of(i):
        return pl.ds(pl.multiple_of(i * PART, PART), PART)

    def take(i):
        return pltpu.make_async_copy(
            turned_ref.at[part_of(i)], turned.at[part_of(i)], tsem.at[i]
        )

    def put(i):
        slot = lax.rem(i, slots)
        return pltpu.make_async_copy(stage.at[slot], out_ref.at[part_of(i)], sem.at[slot])

    for i in range(count):
        take(i).start()
    late = [
        pltpu.make_async_copy(gacc_ref, gacc, lsem.at[1]),
        pltpu.make_async_copy(pull_ref, pull, lsem.at[2]),
    ]
    for copy in late:
        copy.start()
    load.wait()

    def one(i, _):
        @pl.when(i >= slots)
        def _():
            put(i - slots).wait()
        take(i).wait()
        slot = lax.rem(i, slots)
        value = turned[part_of(i), :]
        for t in range(half // TILE):
            there = pl.ds(t * TILE, TILE)
            stage[slot, :, there] = h_ref[part_of(i), there] + jnp.dot(
                value, cols[:, there], preferred_element_type=jnp.float32
            )
        put(i).start()
        return 0

    lax.fori_loop(0, count, one, 0)
    for copy in late:
        copy.wait()
    grad[...] = jnp.sum(gacc[...], axis=0, keepdims=True) - pull[...]
    give = pltpu.make_async_copy(grad, grad_ref, lsem.at[3])
    give.start()
    for i in range(max(0, count - slots), count):
        put(i).wait()
    give.wait()


def last_stage(h, turned, cols, gacc, pull):
    width, half = h.shape
    dma = pltpu.SemaphoreType.DMA
    h = pltpu.with_memory_space_constraint(h, pltpu.VMEM)
    kept = [pltpu.with_memory_space_constraint(a, pltpu.HBM) for a in (turned, cols, gacc, pull)]
    return pl.pallas_call(
        last_kernel,
        out_shape=(
            pltpu.HBM((width, half), jnp.float32),
            pltpu.HBM((1, width), jnp.float32),
        ),
        in_specs=[pl.BlockSpec(memory_space=pltpu.VMEM)]
        + [pl.BlockSpec(memory_space=pl.ANY)] * 4,
        out_specs=[pl.BlockSpec(memory_space=pl.ANY)] * 2,
        scratch_shapes=[
            pltpu.VMEM((3, PART, half), jnp.float32),
            pltpu.VMEM(turned.shape, turned.dtype),
            pltpu.VMEM(cols.shape, cols.dtype),
            pltpu.VMEM(gacc.shape, gacc.dtype),
            pltpu.VMEM(pull.shape, pull.dtype),
            pltpu.VMEM(pull.shape, pull.dtype),
            dma((3,)), dma((4,)), dma((width // PART,)),
        ],
        compiler_params=pltpu.CompilerParams(vmem_limit_bytes=14 * 1024 * 1024),
        name="last_stage",
    )(h, *kept)


def paired(row_count, feat_count, n, width):
    half = width // 2
    rows = row_count * n
    held = 4 * width * half + 2 * rows * (width + half + 256) + 12 * n * half + 4 * n * width
    return (
        row_count == 2 * feat_count and (feat_count - 1).bit_length() == 2
        and feat_count & (feat_count - 1) == 0 and n % (6 * CHUNK) == 0
        and n <= 1024 and half % TILE == 0 and held <= VMEM_BUDGET
    )


def by_lines(features, labels, posterior, prior_prec):
    n, width = features.shape
    partial_value = jnp.dot(features, posterior, preferred_element_type=jnp.float32)
    stats = jnp.stack([
        jnp.pad(partial_value, (0, 1024 - n)),
        jnp.pad(labels.astype(jnp.float32), (0, 1024 - n)),
    ]).reshape(-1, 128)
    pull = (prior_prec * posterior.astype(jnp.float32)).reshape(1, width)
    held = line_stage(features, stats, prior_prec.reshape(1, width))
    hessian, gradient = last_stage(*held, pull)
    return (hessian, gradient.reshape(width))


def gather_kernel(
    row_count, feat_count, x_ref, st_ref, all_ref, col_ref, stat_ref,
    ring, zs, zr, ps, pr, ds, dr, cs, cr, cl, ss, sr, ts, tr, lsem,
):
    r = lax.axis_index("rows")
    f = lax.axis_index("feat")
    n, width = x_ref.shape
    half = width // 2
    col_width = col_ref.shape[1]
    unit = min(col_width, half)
    per_half = half // unit
    per_owner = col_width // unit
    chips = row_count // 2
    bits = chips.bit_length() - 1
    part = n // SPLIT

    def rows_of(device):
        return pl.ds(pl.multiple_of(device * n, n), n)

    def remote(src, dst, send, recv, **where):
        return pltpu.make_async_remote_copy(
            src_ref=src, dst_ref=dst, send_sem=send, recv_sem=recv,
            device_id=where, device_id_type=MESH,
        )

    sends = []

    def go(copy):
        copy.start()
        sends.append(copy)

    def ring_slice(step, h, k):
        rows, cols = pl.ds(k * part, part), pl.ds(h * half, half)
        return x_ref.at[rows, cols] if step == 0 else ring.at[step - 1, rows, cols]

    def ring_copy(step, h, k):
        to = lax.rem(f + (1 if h == 0 else feat_count - 1), feat_count)
        return remote(
            ring_slice(step, h, k),
            ring.at[step, pl.ds(k * part, part), pl.ds(h * half, half)],
            zs.at[step, h, k], zr.at[step, h, k], feat=to,
        )

    def column_sends(step, h, k, start):
        block = lax.rem(f + (feat_count - step if h == 0 else step), feat_count)
        for u in range(per_half):
            inner = h * half + u * unit
            if width % col_width == 0:
                owner = block * (width // col_width) + inner // col_width
                offset = inner % col_width
                slot = offset // unit
            else:
                owner = (block * width + inner) // col_width
                slot = ((block * width + inner) % col_width) // unit
                offset = pl.multiple_of(slot * unit, unit)
            src = ring_slice(step, h, k).at[:, pl.ds(u * unit, unit)]
            dst = col_ref.at[
                pl.ds(pl.multiple_of(r * n + k * part, part), part), pl.ds(offset, unit)
            ]
            send = cs.at[step, h, k, u]

            @pl.when(owner != r)
            def _():
                copy = remote(src, dst, send, cr.at[r, slot, k], rows=owner)
                copy.start() if start else copy.wait_send()

            if start:
                @pl.when(owner == r)
                def _():
                    pltpu.make_async_copy(src, dst, cl.at[slot, k]).start()

    def order(h):
        return list(range(bits)) if h == 0 else list(range(bits))[::-1]

    def spread(h, stage, mask):
        bit = 1 << order(h)[stage]
        origin = r ^ (2 * mask)
        cols = pl.ds(h * half, half)
        src = x_ref.at[:, cols] if mask == 0 else all_ref.at[rows_of(origin), cols]
        return remote(
            src, all_ref.at[rows_of(origin), cols],
            ps.at[h, mask | bit], pr.at[h, mask | bit], rows=r ^ (2 * bit),
        )

    def partner(h, mask):
        origin = r ^ (2 * mask)
        cols = pl.ds(h * half, half)
        src = x_ref.at[:, cols] if mask == 0 else all_ref.at[rows_of(origin), cols]
        return remote(
            src, all_ref.at[rows_of(origin), cols],
            ds.at[h, mask], dr.at[h, mask], rows=r ^ 1,
        )

    def masks_before(h, stage):
        found = [0]
        for b in order(h)[:stage]:
            found += [m | (1 << b) for m in found]
        return found

    for k in range(SPLIT):
        for h in range(2):
            go(ring_copy(0, h, k))
    stat_local = pltpu.make_async_copy(st_ref, stat_ref.at[r, f], lsem.at[0])
    stat_local.start()
    for d in range(1, feat_count):
        go(remote(
            st_ref, stat_ref.at[r, f], ss.at[d], sr.at[d],
            feat=lax.rem(f + d, feat_count),
        ))
    for stage in range(bits):
        for h in range(2):
            go(spread(h, stage, 0))
    for h in range(2):
        go(partner(h, 0))
    own = pltpu.make_async_copy(x_ref, all_ref.at[rows_of(r)], lsem.at[1])
    own.start()
    for k in range(SPLIT):
        for h in range(2):
            column_sends(0, h, k, True)

    stat_local.wait()
    for d in range(1, feat_count):
        remote(
            st_ref, stat_ref.at[r, lax.rem(f + feat_count - d, feat_count)],
            ss.at[d], sr.at[d], feat=f,
        ).wait_recv()
    for d in range(1, row_count):
        go(remote(
            stat_ref.at[r], stat_ref.at[r], ts.at[d], tr.at[d],
            rows=lax.rem(r + d, row_count),
        ))

    def relay(stage):
        for h in range(2):
            bit = 1 << order(h)[stage]
            for m in masks_before(h, stage):
                mask = m | bit
                cols = pl.ds(h * half, half)
                remote(
                    x_ref.at[:, cols], all_ref.at[rows_of(r ^ (2 * mask)), cols],
                    ps.at[h, mask], pr.at[h, mask], rows=r,
                ).wait_recv()
                for later in range(stage + 1, bits):
                    go(spread(h, later, mask))
                go(partner(h, mask))

    for step in range(1, feat_count):
        for k in range(SPLIT):
            for h in range(2):
                ring_copy(step - 1, h, k).wait_recv()
                if step < feat_count - 1:
                    go(ring_copy(step, h, k))
                column_sends(step, h, k, True)
        if step <= bits:
            relay(step - 1)
    for stage in range(feat_count - 1, bits):
        relay(stage)

    for h in range(2):
        for mask in range(chips):
            cols = pl.ds(h * half, half)
            remote(
                x_ref.at[:, cols], all_ref.at[rows_of(r ^ (2 * mask) ^ 1), cols],
                ds.at[h, mask], dr.at[h, mask], rows=r,
            ).wait_recv()
    for d in range(1, row_count):
        origin = lax.rem(r + row_count - d, row_count)
        remote(
            stat_ref.at[origin], stat_ref.at[origin], ts.at[d], tr.at[d], rows=r
        ).wait_recv()
        for slot in range(per_owner):
            for k in range(SPLIT):
                dst = col_ref.at[
                    pl.ds(pl.multiple_of(origin * n + k * part, part), part),
                    pl.ds(slot * unit, unit),
                ]
                remote(
                    x_ref.at[pl.ds(0, part), pl.ds(0, unit)], dst,
                    cs.at[0, 0, 0, 0], cr.at[origin, slot, k], rows=r,
                ).wait_recv()
    for slot in range(per_owner):
        for k in range(SPLIT):
            dst = col_ref.at[
                pl.ds(pl.multiple_of(r * n + k * part, part), part),
                pl.ds(slot * unit, unit),
            ]
            pltpu.make_async_copy(
                x_ref.at[pl.ds(0, part), pl.ds(0, unit)], dst, cl.at[slot, k]
            ).wait()
    own.wait()
    for copy in sends:
        copy.wait_send()
    for step in range(feat_count):
        for k in range(SPLIT):
            for h in range(2):
                column_sends(step, h, k, False)


def gather(features, stats):
    row_count = lax.axis_size("rows")
    feat_count = lax.axis_size("feat")
    n, width = features.shape
    half = width // 2
    col_width = width * feat_count // row_count
    unit = min(col_width, half)
    chips = row_count // 2
    dma = pltpu.SemaphoreType.DMA
    return pl.pallas_call(
        functools.partial(gather_kernel, row_count, feat_count),
        out_shape=(
            jax.ShapeDtypeStruct((row_count * n, width), features.dtype),
            jax.ShapeDtypeStruct((row_count * n, col_width), features.dtype),
            jax.ShapeDtypeStruct((row_count, feat_count) + stats.shape, stats.dtype),
        ),
        in_specs=[pl.BlockSpec(memory_space=pltpu.VMEM)] * 2,
        out_specs=[pl.BlockSpec(memory_space=pl.ANY)] * 3,
        scratch_shapes=[
            pltpu.VMEM((feat_count - 1, n, width), features.dtype),
            dma((feat_count - 1, 2, SPLIT)), dma((feat_count - 1, 2, SPLIT)),
            dma((2, chips)), dma((2, chips)),
            dma((2, chips)), dma((2, chips)),
            dma((feat_count, 2, SPLIT, half // unit)),
            dma((row_count, col_width // unit, SPLIT)),
            dma((col_width // unit, SPLIT)),
            dma((feat_count,)), dma((feat_count,)),
            dma((row_count,)), dma((row_count,)),
            dma((2,)),
        ],
        compiler_params=pltpu.CompilerParams(
            has_side_effects=True, vmem_limit_bytes=32 * 1024 * 1024
        ),
        name="gather",
    )(features, stats)


def per_device(features, labels, posterior, prior_prec):
    row_count = lax.axis_size("rows")
    feat_count = lax.axis_size("feat")
    row_index = lax.axis_index("rows")
    feat_index = lax.axis_index("feat")
    n, block_width = features.shape
    if paired(row_count, feat_count, n, block_width):
        return by_lines(features, labels, posterior, prior_prec)
    col_width = block_width * feat_count // row_count
    partial_value = jnp.dot(features, posterior, preferred_element_type=jnp.float32)
    padded = -(-n // 512) * 512
    stats = jnp.concatenate([
        jnp.pad(partial_value, (0, padded - n)),
        jnp.pad(labels.astype(jnp.float32), (0, padded - n)),
    ]).reshape(-1, 128)
    all_rows, column_rows, all_stats = gather(features, stats)
    all_stats = all_stats.reshape(row_count, feat_count, 2, padded)[..., :n]
    margins = jnp.sum(all_stats[:, :, 0], axis=1).reshape(-1)
    all_labels = all_stats[:, 0, 1].reshape(-1)
    chance = jax.nn.sigmoid(margins)
    weight = (chance * (1.0 - chance)).astype(jnp.bfloat16)
    residual = (all_labels - chance).astype(jnp.bfloat16)
    summed = jnp.dot(residual, all_rows, preferred_element_type=jnp.float32)
    gradient = summed - prior_prec * posterior.astype(jnp.float32)
    weighted = weight[:, None] * all_rows
    product = lax.dot_general(
        weighted, column_rows, (((0,), (0,)), ((), ())), preferred_element_type=jnp.float32
    )
    global_rows = feat_index * block_width + jnp.arange(block_width, dtype=jnp.int32)
    global_cols = row_index * col_width + jnp.arange(col_width, dtype=jnp.int32)
    on_diagonal = global_rows[:, None] == global_cols[None, :]
    hessian = product + jnp.where(on_diagonal, prior_prec[:, None], jnp.float32(0.0))
    return (hessian, gradient)


def solution(mesh):
    in_specs = (P("rows", "feat"), P("rows"), P("feat"), P("feat"))
    out_specs = (P("feat", "rows"), P("feat"))
    return jax.shard_map(
        per_device, mesh=mesh, in_specs=in_specs, out_specs=out_specs, check_vma=False
    )
```

```python
import functools

import jax
import jax.numpy as jnp
from jax import lax
from jax.experimental import pallas as pl
from jax.experimental.pallas import tpu as pltpu
from jax.sharding import PartitionSpec as P

MESH = pl.DeviceIdType.MESH
SPLIT = 2
CHUNK = 16
TILE = 512
PART = 256
AHEAD = 4
VMEM_BUDGET = 60 * 1024 * 1024


def pick(p, q, e):
    first = jnp.where((p ^ 1) == e, p ^ 2, p ^ 1)
    second = jnp.where(((p ^ 1) == e) | ((p ^ 2) == e), p ^ 3, p ^ 2)
    return jnp.where(q == 0, p, jnp.where(q == 1, first, second))


def passed_chip(p, z, last):
    return jnp.where(p > z, 0, jnp.where(p < z, last, p ^ 3))


def slabs(ref, lead, starts, size, cols):
    parts = []
    for start in starts:
        rows = pl.ds(pl.multiple_of(start, CHUNK), size)
        parts.append(ref[rows, cols] if lead is None else ref[lead, rows, cols])
    return jnp.concatenate(parts, axis=0)


def wide(value, width):
    return jnp.concatenate([value] * (width // value.shape[1]), axis=1)


def weigh(all_ref, wr_ref, starts, size, cols):
    x = slabs(all_ref, None, starts, size, cols)
    weight = slabs(wr_ref, 0, starts, size, slice(None))
    residual = slabs(wr_ref, 1, starts, size, slice(None)).astype(jnp.float32)
    pulled = x.astype(jnp.float32) * wide(residual, PART)
    pulled = jnp.sum(pulled.reshape(-1, 8, PART), axis=0)
    return (x * wide(weight, PART)).T, pulled


def line_kernel(
    row_count, feat_count, x_ref, st_ref, prec_ref,
    h_ref, turned_out, cols_out, pull_out,
    all_ref, col_ref, wr_ref, gacc_ref, kept, even, odd, abuf, stat_ref,
    agr, pr, br, ar, adr, own_s, relay_s, extra_s, part_s, src_s, bf_s, af_s, ad_s,
    ss, sr, ts, tr, lsem,
):
    r = lax.axis_index("rows")
    z = lax.axis_index("feat")
    p, c = r // 2, r % 2
    last = feat_count - 1
    n, width = x_ref.shape
    half = width // 2
    m = CHUNK
    nch = n // m
    avoid = jnp.where(z == 0, 0, jnp.where(z == last, last, -1))
    relays = p != avoid
    relays_all = (p ^ last) == avoid
    has_down, has_up = z >= 1, z <= last - 1

    def rows_of(chip, core, j):
        return pl.ds(pl.multiple_of((chip * 2 + core) * n + j * m, m), m)

    def own_rows(j):
        return pl.ds(pl.multiple_of(j * m, m), m)

    def cols_of(h):
        return pl.ds(pl.multiple_of(h * half, half), half)

    def remote(src, dst, send, recv, **where):
        return pltpu.make_async_remote_copy(
            src_ref=src, dst_ref=dst, send_sem=send, recv_sem=recv,
            device_id=where, device_id_type=MESH,
        )

    barrier = pltpu.get_barrier_semaphore()
    for d in range(1, row_count):
        pl.semaphore_signal(
            barrier, inc=1, device_id={"rows": lax.rem(r + d, row_count)},
            device_id_type=MESH,
        )
    for d in range(1, feat_count):
        for other in (r, r ^ 1):
            pl.semaphore_signal(
                barrier, inc=1,
                device_id={"rows": other, "feat": lax.rem(z + d, feat_count)},
                device_id_type=MESH,
            )
    pl.semaphore_wait(barrier, row_count - 1 + 2 * (feat_count - 1))

    stat_local = pltpu.make_async_copy(st_ref, stat_ref.at[r, z], lsem.at[0])
    stat_local.start()
    for d in range(1, feat_count):
        remote(
            st_ref, stat_ref.at[r, z], ss.at[d], sr.at[d],
            feat=lax.rem(z + d, feat_count),
        ).start()

    def ag(dim, h, j, src, chip, rel, send):
        remote(
            src, all_ref.at[rows_of(chip, c, j), cols_of(h)],
            send, agr.at[rel, h, j], rows=r ^ (2 * dim),
        ).start()

    def own_plane(s):
        j = lax.rem(s, nch)

        @pl.when(s < nch)
        def _():
            ag(1, 0, j, x_ref.at[own_rows(j), cols_of(0)], p, 0, own_s.at[0])
            ag(2, 1, j, x_ref.at[own_rows(j), cols_of(1)], p, 1, own_s.at[1])

        @pl.when(s >= nch)
        def _():
            ag(1, 1, j, x_ref.at[own_rows(j), cols_of(1)], p, 0, own_s.at[0])
            ag(2, 0, j, x_ref.at[own_rows(j), cols_of(0)], p, 1, own_s.at[1])

    def own_line(j):
        for h in range(2):
            src = x_ref.at[own_rows(j), cols_of(h)]

            @pl.when(has_down & (p == 0))
            def _():
                remote(
                    src, abuf.at[z - 1, c, own_rows(j)], own_s.at[2], ar.at[0, c, j],
                    rows=2 * p + h, feat=z - 1,
                ).start()

            @pl.when(has_down & (p == z))
            def _():
                remote(
                    src, col_ref.at[rows_of(p, c, j)], own_s.at[2], br.at[0, c, j],
                    rows=2 * p + h, feat=z - 1,
                ).start()

            @pl.when(has_up & (p == last))
            def _():
                remote(
                    src, abuf.at[z, c, own_rows(j)], own_s.at[3], ar.at[0, c, j],
                    rows=2 * p + h, feat=z + 1,
                ).start()

            @pl.when(has_up & (p == z))
            def _():
                remote(
                    src, col_ref.at[rows_of(p, c, j)], own_s.at[3], br.at[0, c, j],
                    rows=2 * p + h, feat=z + 1,
                ).start()

    def own_sends(j, _):
        own_plane(2 * j)
        own_plane(2 * j + 1)
        own_line(j)
        return 0

    own = pltpu.make_async_copy(
        x_ref, all_ref.at[pl.ds(pl.multiple_of(r * n, n), n)], lsem.at[1]
    )
    lax.fori_loop(0, AHEAD, own_sends, 0)
    own.start()
    remote(
        x_ref, all_ref.at[pl.ds(pl.multiple_of(r * n, n), n)], part_s.at[3], pr.at[3],
        rows=r ^ 1,
    ).start()

    def share_stats():
        stat_local.wait()
        for d in range(1, feat_count):
            remote(
                st_ref, stat_ref.at[r, lax.rem(z + feat_count - d, feat_count)],
                ss.at[d], sr.at[d], feat=z,
            ).wait_recv()
        for d in range(1, row_count):
            remote(
                stat_ref.at[r], stat_ref.at[r], ts.at[d], tr.at[d],
                rows=lax.rem(r + d, row_count),
            ).start()

    def weights():
        for d in range(1, row_count):
            origin = lax.rem(r + row_count - d, row_count)
            remote(
                stat_ref.at[origin], stat_ref.at[origin], ts.at[d], tr.at[d], rows=r
            ).wait_recv()

        def one(i, _):
            margins = stat_ref[i, 0, 0:8]
            for f in range(1, feat_count):
                margins = margins + stat_ref[i, f, 0:8]
            chance = 1.0 / (1.0 + jnp.exp(-margins))
            weight = (chance * (1.0 - chance)).astype(jnp.bfloat16)
            residual = (stat_ref[i, 0, 8:16] - chance).astype(jnp.bfloat16)
            for lead, value in ((0, weight), (1, residual)):
                turned = value.astype(jnp.float32).T
                for t in range(-(-n // 128)):
                    count = min(128, n - 128 * t)
                    rows = pl.ds(pl.multiple_of(i * n + 128 * t, CHUNK), count)
                    wr_ref[lead, rows, :] = jnp.broadcast_to(
                        turned[:count, t:t + 1], (count, 128)
                    ).astype(jnp.bfloat16)
            return 0

        lax.fori_loop(0, row_count, one, 0)

    def arrive(rel, h, j):
        chip = p ^ (rel + 1)
        here = all_ref.at[rows_of(chip, c, j), cols_of(h)]
        remote(here, here, own_s.at[0], agr.at[rel, h, j], rows=r).wait_recv()
        remote(here, here, part_s.at[rel], pr.at[rel], rows=r ^ 1).start()

    def forward(rel, h, j, send):
        chip = p ^ (rel + 1)
        here = all_ref.at[rows_of(chip, c, j), cols_of(h)]
        ag(2 - rel, h, j, here, chip, 2, send)

    def gather_event(s):
        a, j = s // nch, s % nch

        @pl.when(a == 0)
        def _():
            arrive(0, 0, j)

            @pl.when(relays)
            def _():
                forward(0, 0, j, relay_s.at[0])
            arrive(1, 1, j)

            @pl.when(relays)
            def _():
                forward(1, 1, j, relay_s.at[1])

        @pl.when(a == 1)
        def _():
            arrive(0, 1, j)

            @pl.when(relays_all)
            def _():
                forward(0, 1, j, extra_s.at[0])
            arrive(1, 0, j)

            @pl.when(relays_all)
            def _():
                forward(1, 0, j, extra_s.at[1])

    def corner_event(j):
        arrive(2, 0, j)
        arrive(2, 1, j)

    def source_event(s):
        q, j = 1 + s // nch, s % nch
        for h in range(2):
            @pl.when(has_down)
            def _():
                where = rows_of(pick(p, q, 0), c, j)
                remote(
                    all_ref.at[where, cols_of(h)], col_ref.at[where],
                    src_s.at[0, q], br.at[q, c, j], rows=2 * p + h, feat=z - 1,
                ).start()

            @pl.when(has_up)
            def _():
                where = rows_of(pick(p, q, last), c, j)
                remote(
                    all_ref.at[where, cols_of(h)], col_ref.at[where],
                    src_s.at[1, q], br.at[q, c, j], rows=2 * p + h, feat=z + 1,
                ).start()

    def column_event(s):
        q, j = s // nch, s % nch
        down = p > z
        chip = pick(p, q, jnp.where(down, 0, last))
        for k in range(2):
            here = col_ref.at[rows_of(chip, k, j)]
            remote(here, here, bf_s.at[q], br.at[q, k, j], rows=r).wait_recv()

            @pl.when((down & has_down) | (~down & has_up))
            def _():
                remote(
                    here, here, bf_s.at[q], br.at[q, k, j],
                    feat=jnp.where(down, z - 1, z + 1),
                ).start()

    def pass_event(s):
        q, j = s // nch, s % nch
        down = p == 0
        block = jnp.where(down, z + 1 + q, z - 1 - q)
        slot = jnp.where(down, block - 1, block)

        @pl.when((block >= 0) & (block <= last))
        def _():
            for k in range(2):
                here = abuf.at[slot, k, own_rows(j)]
                remote(here, here, af_s.at[q], ar.at[q, k, j], rows=r).wait_recv()

                @pl.when((down & has_down) | (~down & has_up))
                def _():
                    remote(
                        here, here, af_s.at[q], ar.at[q + 1, k, j],
                        feat=jnp.where(down, z - 1, z + 1),
                    ).start()

    def deliver_event(s):
        q, j = s // nch, s % nch
        down = p == 0
        block = jnp.where(down, z + 1 + q, z - 1 - q)
        slot = jnp.where(down, block - 1, block)

        @pl.when((block >= 0) & (block <= last))
        def _():
            for k in range(2):
                remote(
                    abuf.at[slot, k, own_rows(j)], col_ref.at[rows_of(p, k, j)],
                    ad_s.at[q], adr.at[j // (nch // 2)], rows=2 * block + c,
                ).start()

    items = last
    lag = nch // 2 + 3
    tiles = width // TILE
    edge = passed_chip(p, z, last)
    twice = col_ref.at[pl.ds(0, 2 * n)]
    once = col_ref.at[pl.ds(0, n)]
    hn = n // 2
    q = nch // 6
    begins = [6 * q, 11 * q, 12 * q, 15 * q]
    ends = [10 * q, 12 * q, 15 * q, 18 * q]
    near, far = pick(p, 1, edge), pick(p, 2, edge)

    def partner_rows(chip):
        rel = jnp.where(chip == p, 3, (p ^ chip) - 1)
        there = all_ref.at[pl.ds(pl.multiple_of((2 * chip + 1 - c) * n, n), n)]
        remote(there, there, part_s.at[rel], pr.at[rel], rows=r).wait_recv()

        @pl.when(p == z)
        def _():
            rows = pl.ds(pl.multiple_of(chip * 2 * n, n), 2 * n)
            copy = pltpu.make_async_copy(
                all_ref.at[rows, cols_of(c)], col_ref.at[rows], lsem.at[2]
            )
            copy.start()
            copy.wait()

    def prepare(i):
        rows = pl.ds(pl.multiple_of(i * TILE, TILE), TILE)
        h_ref[rows, :] = jnp.zeros((TILE, half), jnp.float32)
        offset = i * TILE - c * half

        @pl.when((p == z) & (offset >= 0) & (offset < half))
        def _():
            cols = pl.ds(pl.multiple_of(offset, TILE), TILE)
            shape = (TILE, TILE)
            same = lax.broadcasted_iota(jnp.int32, shape, 0) == lax.broadcasted_iota(
                jnp.int32, shape, 1
            )
            h_ref[rows, cols] = jnp.where(
                same, jnp.broadcast_to(prec_ref[:, rows], shape), 0.0
            )

    def unit_rows(index):
        chip = jnp.where(index == 0, p, near)
        mixed = jnp.where(index == 1, hn, 0)
        return [
            jnp.where(
                (index == 0) | (index == 2), chip * 2 * n + i * hn,
                (jnp.where(i < 2, far, edge) * 2 + i % 2) * n + mixed,
            ) for i in range(4)
        ]

    def part_of(i):
        return pl.ds(pl.multiple_of(i * PART, PART), PART)

    def turn(rows, i, flag):
        weighted, pulled = weigh(all_ref, wr_ref, rows, hn, part_of(i))
        gacc_ref[:, part_of(i)] += pulled * flag
        return weighted

    def multiply(turned, rows, i):
        value = turned[...]
        for t in range(half // TILE):
            there = pl.ds(t * TILE, TILE)
            h_ref[part_of(i), there] += jnp.dot(
                value, slabs(col_ref, None, rows, hn, there),
                preferred_element_type=jnp.float32,
            )

    def compute(u):
        index = sum((u >= s).astype(jnp.int32) for s in begins) - 1

        def choose(values):
            out = values[0]
            for i in range(1, len(values)):
                out = jnp.where(index >= i, values[i], out)
            return out

        begin, span = choose(begins), choose([e - s for s, e in zip(begins, ends)])
        low = jnp.minimum((u - begin) * tiles // span, tiles)
        high = jnp.minimum((u - begin + 1) * tiles // span, tiles)
        rows = unit_rows(index)

        @pl.when(u == begin)
        def _():
            @pl.when(index == 0)
            def _():
                own.wait()
                weights()
                gacc_ref[...] = jnp.zeros_like(gacc_ref)
                partner_rows(p)

            @pl.when(index == 1)
            def _():
                partner_rows(far)
                partner_rows(edge)

            @pl.when(index == 2)
            def _():
                partner_rows(near)

            @pl.when((index == 3) & (p != z))
            def _():
                remote(once, once, bf_s.at[0], adr.at[0], rows=r).wait_recv()

            @pl.when(index != 1)
            def _():
                even[...] = turn(rows, 0, 1.0)

        def keep(i, _):
            for e in range(2):
                kept[part_of(2 * i + e), :] = turn(rows, 2 * i + e, 1.0)
            return 0

        def pair(i, _):
            multiply(even, rows, 2 * i)
            odd[...] = turn(rows, 2 * i + 1, 1.0)
            multiply(odd, rows, 2 * i + 1)
            more = i < tiles - 1
            even[...] = turn(
                rows, jnp.where(more, 2 * i + 2, 0), jnp.where(more, 1.0, 0.0)
            )
            return 0

        @pl.when(index == 1)
        def _():
            lax.fori_loop(low, high, keep, 0)

            @pl.when(u == ends[1] - 1)
            def _():
                pltpu.make_async_copy(kept, turned_out, lsem.at[3]).start()

        @pl.when(index != 1)
        def _():
            lax.fori_loop(low, high, pair, 0)

    def some(event, low, high):
        def one(i, _):
            event(i)
            return 0
        lax.fori_loop(low, high, one, 0)

    def step(u, _):
        @pl.when((p != z) & (u < items * nch))
        def _():
            column_event(u)

        @pl.when(u == 1)
        def _():
            share_stats()

        @pl.when((u >= 1) & (4 * (u - 1) + AHEAD < nch))
        def _():
            low = 4 * (u - 1) + AHEAD
            some(lambda j: own_sends(j, 0), low, jnp.minimum(low + 4, nch))

        @pl.when((u >= 3) & (u < 3 + nch))
        def _():
            some(gather_event, 2 * u - 6, 2 * u - 4)

        @pl.when((u >= 9 * q) & (u < 11 * q))
        def _():
            some(corner_event, 3 * (u - 9 * q), 3 * (u - 9 * q) + 3)

        @pl.when((p == z) & (u >= lag) & (u < lag + 2 * nch))
        def _():
            source_event(u - lag)

        @pl.when(((p == 0) | (p == last)) & (u >= 1) & (u < 1 + items * nch))
        def _():
            pass_event(u - 1)

        @pl.when(((p == 0) | (p == last)) & (u >= nch))
        def _():
            low = jnp.minimum(2 * (u - nch), u - 1)
            some(deliver_event, low, jnp.minimum(2 * (u + 1 - nch), u))

        @pl.when(u < begins[0])
        def _():
            per = -(-tiles // begins[0])
            some(prepare, jnp.minimum(u * per, tiles), jnp.minimum(u * per + per, tiles))

        @pl.when((u >= begins[0]) & (u < ends[-1]))
        def _():
            compute(u)
        return 0

    lax.fori_loop(0, items * nch + 1, step, 0)

    @pl.when(p != z)
    def _():
        remote(once, once, bf_s.at[0], adr.at[1], rows=r).wait_recv()

    outs = [pltpu.make_async_copy(gacc_ref, pull_out, lsem.at[4])]
    for i, start in enumerate(unit_rows(1)):
        outs.append(pltpu.make_async_copy(
            col_ref.at[pl.ds(pl.multiple_of(start, CHUNK), hn)],
            cols_out.at[pl.ds(i * hn, hn)], lsem.at[5 + i],
        ))
    for copy in outs:
        copy.start()

    def sent(ref, sem):
        remote(ref, ref, sem, pr.at[3], rows=r).wait_send()

    for d in range(1, feat_count):
        sent(st_ref, ss.at[d])
    for d in range(1, row_count):
        sent(stat_ref.at[r], ts.at[d])
    for i in range(2):
        sent(x_ref, own_s.at[i])

        @pl.when(relays)
        def _():
            sent(x_ref.at[:, pl.ds(0, half)], relay_s.at[i])

        @pl.when(relays_all)
        def _():
            sent(x_ref.at[:, pl.ds(0, half)], extra_s.at[i])

    @pl.when(has_down & ((p == 0) | (p == z)))
    def _():
        sent(x_ref, own_s.at[2])

    @pl.when(has_up & ((p == last) | (p == z)))
    def _():
        sent(x_ref, own_s.at[3])
    for rel in range(4):
        sent(x_ref, part_s.at[rel])
    down = p > z
    for q in range(items):
        if q > 0:
            @pl.when((p == z) & has_down)
            def _():
                sent(x_ref, src_s.at[0, q])

            @pl.when((p == z) & has_up)
            def _():
                sent(x_ref, src_s.at[1, q])

        @pl.when((p != z) & ((down & has_down) | (~down & has_up)))
        def _():
            sent(twice, bf_s.at[q])
        for edge, block, more in ((0, z + 1 + q, has_down), (last, z - 1 - q, has_up)):
            @pl.when((p == edge) & (block >= 0) & (block <= last))
            def _():
                sent(twice, ad_s.at[q])

                @pl.when(more)
                def _():
                    sent(twice, af_s.at[q])
    for copy in outs:
        copy.wait()
    pltpu.make_async_copy(kept, turned_out, lsem.at[3]).wait()


def line_stage(features, stats, prec):
    row_count = lax.axis_size("rows")
    feat_count = lax.axis_size("feat")
    n, width = features.shape
    half = width // 2
    items = feat_count - 1
    nch = n // CHUNK
    dma = pltpu.SemaphoreType.DMA
    return pl.pallas_call(
        functools.partial(line_kernel, row_count, feat_count),
        out_shape=(
            pltpu.VMEM((width, half), jnp.float32),
            pltpu.HBM((width, 2 * n), features.dtype),
            pltpu.HBM((2 * n, half), features.dtype),
            pltpu.HBM((8, width), jnp.float32),
        ),
        in_specs=[
            pl.BlockSpec(memory_space=pl.ANY), pl.BlockSpec(memory_space=pltpu.VMEM),
            pl.BlockSpec(memory_space=pltpu.VMEM),
        ],
        out_specs=[pl.BlockSpec(memory_space=pltpu.VMEM)]
        + [pl.BlockSpec(memory_space=pl.ANY)] * 3,
        scratch_shapes=[
            pltpu.VMEM((row_count * n, width), features.dtype),
            pltpu.VMEM((row_count * n, half), features.dtype),
            pltpu.VMEM((2, row_count * n, 128), features.dtype),
            pltpu.VMEM((8, width), jnp.float32),
            pltpu.VMEM((width, 2 * n), features.dtype),
            pltpu.VMEM((PART, 2 * n), features.dtype),
            pltpu.VMEM((PART, 2 * n), features.dtype),
            pltpu.VMEM((items, 2, n, half), features.dtype),
            pltpu.VMEM((row_count, feat_count) + stats.shape, stats.dtype),
            dma((3, 2, nch)), dma((4,)), dma((items, 2, nch)), dma((items + 1, 2, nch)),
            dma((2,)),
            dma((4,)), dma((2,)), dma((2,)), dma((4,)), dma((2, items)), dma((items,)),
            dma((items,)), dma((items,)),
            dma((feat_count,)), dma((feat_count,)),
            dma((row_count,)), dma((row_count,)),
            dma((9,)),
        ],
        compiler_params=pltpu.CompilerParams(
            collective_id=0, has_side_effects=True, vmem_limit_bytes=30 * 1024 * 1024
        ),
        name="line_stage",
    )(features, stats, prec)


def last_kernel(
    h_ref, turned_ref, cols_ref, gacc_ref, pull_ref,
    out_ref, grad_ref, stage, turned, cols, gacc, pull, grad, sem, lsem, tsem,
):
    width, half = h_ref.shape
    slots = stage.shape[0]
    count = width // PART
    load = pltpu.make_async_copy(cols_ref, cols, lsem.at[0])
    load.start()

    def part_of(i):
        return pl.ds(pl.multiple_of(i * PART, PART), PART)

    def take(i):
        return pltpu.make_async_copy(
            turned_ref.at[part_of(i)], turned.at[part_of(i)], tsem.at[i]
        )

    def put(i):
        slot = lax.rem(i, slots)
        return pltpu.make_async_copy(stage.at[slot], out_ref.at[part_of(i)], sem.at[slot])

    for i in range(count):
        take(i).start()
    late = [
        pltpu.make_async_copy(gacc_ref, gacc, lsem.at[1]),
        pltpu.make_async_copy(pull_ref, pull, lsem.at[2]),
    ]
    for copy in late:
        copy.start()
    load.wait()

    def one(i, _):
        @pl.when(i >= slots)
        def _():
            put(i - slots).wait()
        take(i).wait()
        slot = lax.rem(i, slots)
        value = turned[part_of(i), :]
        for t in range(half // TILE):
            there = pl.ds(t * TILE, TILE)
            stage[slot, :, there] = h_ref[part_of(i), there] + jnp.dot(
                value, cols[:, there], preferred_element_type=jnp.float32
            )
        put(i).start()
        return 0

    lax.fori_loop(0, count, one, 0)
    for copy in late:
        copy.wait()
    grad[...] = jnp.sum(gacc[...], axis=0, keepdims=True) - pull[...]
    give = pltpu.make_async_copy(grad, grad_ref, lsem.at[3])
    give.start()
    for i in range(max(0, count - slots), count):
        put(i).wait()
    give.wait()


def last_stage(h, turned, cols, gacc, pull):
    width, half = h.shape
    dma = pltpu.SemaphoreType.DMA
    h = pltpu.with_memory_space_constraint(h, pltpu.VMEM)
    kept = [pltpu.with_memory_space_constraint(a, pltpu.HBM) for a in (turned, cols, gacc, pull)]
    return pl.pallas_call(
        last_kernel,
        out_shape=(
            pltpu.HBM((width, half), jnp.float32),
            pltpu.HBM((1, width), jnp.float32),
        ),
        in_specs=[pl.BlockSpec(memory_space=pltpu.VMEM)]
        + [pl.BlockSpec(memory_space=pl.ANY)] * 4,
        out_specs=[pl.BlockSpec(memory_space=pl.ANY)] * 2,
        scratch_shapes=[
            pltpu.VMEM((3, PART, half), jnp.float32),
            pltpu.VMEM(turned.shape, turned.dtype),
            pltpu.VMEM(cols.shape, cols.dtype),
            pltpu.VMEM(gacc.shape, gacc.dtype),
            pltpu.VMEM(pull.shape, pull.dtype),
            pltpu.VMEM(pull.shape, pull.dtype),
            dma((3,)), dma((4,)), dma((width // PART,)),
        ],
        compiler_params=pltpu.CompilerParams(vmem_limit_bytes=14 * 1024 * 1024),
        name="last_stage",
    )(h, *kept)


def paired(row_count, feat_count, n, width):
    half = width // 2
    rows = row_count * n
    held = 4 * width * half + 2 * rows * (width + half + 256) + 12 * n * half + 4 * n * width
    return (
        row_count == 2 * feat_count and (feat_count - 1).bit_length() == 2
        and feat_count & (feat_count - 1) == 0 and n % (6 * CHUNK) == 0
        and n <= 1024 and half % TILE == 0 and held <= VMEM_BUDGET
    )


def by_lines(features, labels, posterior, prior_prec):
    n, width = features.shape
    partial_value = jnp.dot(features, posterior, preferred_element_type=jnp.float32)
    stats = jnp.stack([
        jnp.pad(partial_value, (0, 1024 - n)),
        jnp.pad(labels.astype(jnp.float32), (0, 1024 - n)),
    ]).reshape(-1, 128)
    pull = (prior_prec * posterior.astype(jnp.float32)).reshape(1, width)
    held = line_stage(features, stats, prior_prec.reshape(1, width))
    hessian, gradient = last_stage(*held, pull)
    return (hessian, gradient.reshape(width))


def gather_kernel(
    row_count, feat_count, x_ref, st_ref, all_ref, col_ref, stat_ref,
    ring, zs, zr, ps, pr, ds, dr, cs, cr, cl, ss, sr, ts, tr, lsem,
):
    r = lax.axis_index("rows")
    f = lax.axis_index("feat")
    n, width = x_ref.shape
    half = width // 2
    col_width = col_ref.shape[1]
    unit = min(col_width, half)
    per_half = half // unit
    per_owner = col_width // unit
    chips = row_count // 2
    bits = chips.bit_length() - 1
    part = n // SPLIT

    def rows_of(device):
        return pl.ds(pl.multiple_of(device * n, n), n)

    def remote(src, dst, send, recv, **where):
        return pltpu.make_async_remote_copy(
            src_ref=src, dst_ref=dst, send_sem=send, recv_sem=recv,
            device_id=where, device_id_type=MESH,
        )

    sends = []

    def go(copy):
        copy.start()
        sends.append(copy)

    def ring_slice(step, h, k):
        rows, cols = pl.ds(k * part, part), pl.ds(h * half, half)
        return x_ref.at[rows, cols] if step == 0 else ring.at[step - 1, rows, cols]

    def ring_copy(step, h, k):
        to = lax.rem(f + (1 if h == 0 else feat_count - 1), feat_count)
        return remote(
            ring_slice(step, h, k),
            ring.at[step, pl.ds(k * part, part), pl.ds(h * half, half)],
            zs.at[step, h, k], zr.at[step, h, k], feat=to,
        )

    def column_sends(step, h, k, start):
        block = lax.rem(f + (feat_count - step if h == 0 else step), feat_count)
        for u in range(per_half):
            inner = h * half + u * unit
            if width % col_width == 0:
                owner = block * (width // col_width) + inner // col_width
                offset = inner % col_width
                slot = offset // unit
            else:
                owner = (block * width + inner) // col_width
                slot = ((block * width + inner) % col_width) // unit
                offset = pl.multiple_of(slot * unit, unit)
            src = ring_slice(step, h, k).at[:, pl.ds(u * unit, unit)]
            dst = col_ref.at[
                pl.ds(pl.multiple_of(r * n + k * part, part), part), pl.ds(offset, unit)
            ]
            send = cs.at[step, h, k, u]

            @pl.when(owner != r)
            def _():
                copy = remote(src, dst, send, cr.at[r, slot, k], rows=owner)
                copy.start() if start else copy.wait_send()

            if start:
                @pl.when(owner == r)
                def _():
                    pltpu.make_async_copy(src, dst, cl.at[slot, k]).start()

    def order(h):
        return list(range(bits)) if h == 0 else list(range(bits))[::-1]

    def spread(h, stage, mask):
        bit = 1 << order(h)[stage]
        origin = r ^ (2 * mask)
        cols = pl.ds(h * half, half)
        src = x_ref.at[:, cols] if mask == 0 else all_ref.at[rows_of(origin), cols]
        return remote(
            src, all_ref.at[rows_of(origin), cols],
            ps.at[h, mask | bit], pr.at[h, mask | bit], rows=r ^ (2 * bit),
        )

    def partner(h, mask):
        origin = r ^ (2 * mask)
        cols = pl.ds(h * half, half)
        src = x_ref.at[:, cols] if mask == 0 else all_ref.at[rows_of(origin), cols]
        return remote(
            src, all_ref.at[rows_of(origin), cols],
            ds.at[h, mask], dr.at[h, mask], rows=r ^ 1,
        )

    def masks_before(h, stage):
        found = [0]
        for b in order(h)[:stage]:
            found += [m | (1 << b) for m in found]
        return found

    for k in range(SPLIT):
        for h in range(2):
            go(ring_copy(0, h, k))
    stat_local = pltpu.make_async_copy(st_ref, stat_ref.at[r, f], lsem.at[0])
    stat_local.start()
    for d in range(1, feat_count):
        go(remote(
            st_ref, stat_ref.at[r, f], ss.at[d], sr.at[d],
            feat=lax.rem(f + d, feat_count),
        ))
    for stage in range(bits):
        for h in range(2):
            go(spread(h, stage, 0))
    for h in range(2):
        go(partner(h, 0))
    own = pltpu.make_async_copy(x_ref, all_ref.at[rows_of(r)], lsem.at[1])
    own.start()
    for k in range(SPLIT):
        for h in range(2):
            column_sends(0, h, k, True)

    stat_local.wait()
    for d in range(1, feat_count):
        remote(
            st_ref, stat_ref.at[r, lax.rem(f + feat_count - d, feat_count)],
            ss.at[d], sr.at[d], feat=f,
        ).wait_recv()
    for d in range(1, row_count):
        go(remote(
            stat_ref.at[r], stat_ref.at[r], ts.at[d], tr.at[d],
            rows=lax.rem(r + d, row_count),
        ))

    def relay(stage):
        for h in range(2):
            bit = 1 << order(h)[stage]
            for m in masks_before(h, stage):
                mask = m | bit
                cols = pl.ds(h * half, half)
                remote(
                    x_ref.at[:, cols], all_ref.at[rows_of(r ^ (2 * mask)), cols],
                    ps.at[h, mask], pr.at[h, mask], rows=r,
                ).wait_recv()
                for later in range(stage + 1, bits):
                    go(spread(h, later, mask))
                go(partner(h, mask))

    for step in range(1, feat_count):
        for k in range(SPLIT):
            for h in range(2):
                ring_copy(step - 1, h, k).wait_recv()
                if step < feat_count - 1:
                    go(ring_copy(step, h, k))
                column_sends(step, h, k, True)
        if step <= bits:
            relay(step - 1)
    for stage in range(feat_count - 1, bits):
        relay(stage)

    for h in range(2):
        for mask in range(chips):
            cols = pl.ds(h * half, half)
            remote(
                x_ref.at[:, cols], all_ref.at[rows_of(r ^ (2 * mask) ^ 1), cols],
                ds.at[h, mask], dr.at[h, mask], rows=r,
            ).wait_recv()
    for d in range(1, row_count):
        origin = lax.rem(r + row_count - d, row_count)
        remote(
            stat_ref.at[origin], stat_ref.at[origin], ts.at[d], tr.at[d], rows=r
        ).wait_recv()
        for slot in range(per_owner):
            for k in range(SPLIT):
                dst = col_ref.at[
                    pl.ds(pl.multiple_of(origin * n + k * part, part), part),
                    pl.ds(slot * unit, unit),
                ]
                remote(
                    x_ref.at[pl.ds(0, part), pl.ds(0, unit)], dst,
                    cs.at[0, 0, 0, 0], cr.at[origin, slot, k], rows=r,
                ).wait_recv()
    for slot in range(per_owner):
        for k in range(SPLIT):
            dst = col_ref.at[
                pl.ds(pl.multiple_of(r * n + k * part, part), part),
                pl.ds(slot * unit, unit),
            ]
            pltpu.make_async_copy(
                x_ref.at[pl.ds(0, part), pl.ds(0, unit)], dst, cl.at[slot, k]
            ).wait()
    own.wait()
    for copy in sends:
        copy.wait_send()
    for step in range(feat_count):
        for k in range(SPLIT):
            for h in range(2):
                column_sends(step, h, k, False)


def gather(features, stats):
    row_count = lax.axis_size("rows")
    feat_count = lax.axis_size("feat")
    n, width = features.shape
    half = width // 2
    col_width = width * feat_count // row_count
    unit = min(col_width, half)
    chips = row_count // 2
    dma = pltpu.SemaphoreType.DMA
    return pl.pallas_call(
        functools.partial(gather_kernel, row_count, feat_count),
        out_shape=(
            jax.ShapeDtypeStruct((row_count * n, width), features.dtype),
            jax.ShapeDtypeStruct((row_count * n, col_width), features.dtype),
            jax.ShapeDtypeStruct((row_count, feat_count) + stats.shape, stats.dtype),
        ),
        in_specs=[pl.BlockSpec(memory_space=pltpu.VMEM)] * 2,
        out_specs=[pl.BlockSpec(memory_space=pl.ANY)] * 3,
        scratch_shapes=[
            pltpu.VMEM((feat_count - 1, n, width), features.dtype),
            dma((feat_count - 1, 2, SPLIT)), dma((feat_count - 1, 2, SPLIT)),
            dma((2, chips)), dma((2, chips)),
            dma((2, chips)), dma((2, chips)),
            dma((feat_count, 2, SPLIT, half // unit)),
            dma((row_count, col_width // unit, SPLIT)),
            dma((col_width // unit, SPLIT)),
            dma((feat_count,)), dma((feat_count,)),
            dma((row_count,)), dma((row_count,)),
            dma((2,)),
        ],
        compiler_params=pltpu.CompilerParams(
            has_side_effects=True, vmem_limit_bytes=32 * 1024 * 1024
        ),
        name="gather",
    )(features, stats)


def per_device(features, labels, posterior, prior_prec):
    row_count = lax.axis_size("rows")
    feat_count = lax.axis_size("feat")
    row_index = lax.axis_index("rows")
    feat_index = lax.axis_index("feat")
    n, block_width = features.shape
    if paired(row_count, feat_count, n, block_width):
        return by_lines(features, labels, posterior, prior_prec)
    col_width = block_width * feat_count // row_count
    partial_value = jnp.dot(features, posterior, preferred_element_type=jnp.float32)
    padded = -(-n // 512) * 512
    stats = jnp.concatenate([
        jnp.pad(partial_value, (0, padded - n)),
        jnp.pad(labels.astype(jnp.float32), (0, padded - n)),
    ]).reshape(-1, 128)
    all_rows, column_rows, all_stats = gather(features, stats)
    all_stats = all_stats.reshape(row_count, feat_count, 2, padded)[..., :n]
    margins = jnp.sum(all_stats[:, :, 0], axis=1).reshape(-1)
    all_labels = all_stats[:, 0, 1].reshape(-1)
    chance = jax.nn.sigmoid(margins)
    weight = (chance * (1.0 - chance)).astype(jnp.bfloat16)
    residual = (all_labels - chance).astype(jnp.bfloat16)
    summed = jnp.dot(residual, all_rows, preferred_element_type=jnp.float32)
    gradient = summed - prior_prec * posterior.astype(jnp.float32)
    weighted = weight[:, None] * all_rows
    product = lax.dot_general(
        weighted, column_rows, (((0,), (0,)), ((), ())), preferred_element_type=jnp.float32
    )
    global_rows = feat_index * block_width + jnp.arange(block_width, dtype=jnp.int32)
    global_cols = row_index * col_width + jnp.arange(col_width, dtype=jnp.int32)
    on_diagonal = global_rows[:, None] == global_cols[None, :]
    hessian = product + jnp.where(on_diagonal, prior_prec[:, None], jnp.float32(0.0))
    return (hessian, gradient)


def solution(mesh):
    in_specs = (P("rows", "feat"), P("rows"), P("feat"), P("feat"))
    out_specs = (P("feat", "rows"), P("feat"))
    return jax.shard_map(
        per_device, mesh=mesh, in_specs=in_specs, out_specs=out_specs, check_vma=False
    )
```

```python
import functools

import jax
import jax.numpy as jnp
from jax import lax
from jax.experimental import pallas as pl
from jax.experimental.pallas import tpu as pltpu
from jax.sharding import PartitionSpec as P

MESH = pl.DeviceIdType.MESH
SPLIT = 2
CHUNK = 16
TILE = 512
PART = 256
AHEAD = 2
VMEM_BUDGET = 60 * 1024 * 1024


def pick(p, q, e):
    first = jnp.where((p ^ 1) == e, p ^ 2, p ^ 1)
    second = jnp.where(((p ^ 1) == e) | ((p ^ 2) == e), p ^ 3, p ^ 2)
    return jnp.where(q == 0, p, jnp.where(q == 1, first, second))


def passed_chip(p, z, last):
    return jnp.where(p > z, 0, jnp.where(p < z, last, p ^ 3))


def slabs(ref, lead, starts, size, cols):
    parts = []
    for start in starts:
        rows = pl.ds(pl.multiple_of(start, CHUNK), size)
        parts.append(ref[rows, cols] if lead is None else ref[lead, rows, cols])
    return jnp.concatenate(parts, axis=0)


def wide(value, width):
    return jnp.concatenate([value] * (width // value.shape[1]), axis=1)


def weigh(all_ref, wr_ref, starts, size, cols):
    x = slabs(all_ref, None, starts, size, cols)
    weight = slabs(wr_ref, 0, starts, size, slice(None))
    residual = slabs(wr_ref, 1, starts, size, slice(None)).astype(jnp.float32)
    pulled = x.astype(jnp.float32) * wide(residual, PART)
    pulled = jnp.sum(pulled.reshape(-1, 8, PART), axis=0)
    return (x * wide(weight, PART)).T, pulled


def line_kernel(
    row_count, feat_count, x_ref, label_ref, post_ref, prec_ref,
    h_ref, turned_out, cols_out, pull_out,
    all_ref, col_ref, wr_ref, gacc_ref, kept, even, odd, abuf, st_ref, stat_ref,
    agr, pr, br, ar, adr, own_s, relay_s, extra_s, part_s, src_s, bf_s, af_s, ad_s,
    ss, sr, ts, tr, lsem,
):
    r = lax.axis_index("rows")
    z = lax.axis_index("feat")
    p, c = r // 2, r % 2
    last = feat_count - 1
    n, width = x_ref.shape
    half = width // 2
    m = CHUNK
    nch = n // m
    avoid = jnp.where(z == 0, 0, jnp.where(z == last, last, -1))
    relays = p != avoid
    relays_all = (p ^ last) == avoid
    has_down, has_up = z >= 1, z <= last - 1

    def rows_of(chip, core, j):
        return pl.ds(pl.multiple_of((chip * 2 + core) * n + j * m, m), m)

    def own_rows(j):
        return pl.ds(pl.multiple_of(j * m, m), m)

    def cols_of(h):
        return pl.ds(pl.multiple_of(h * half, half), half)

    def remote(src, dst, send, recv, **where):
        return pltpu.make_async_remote_copy(
            src_ref=src, dst_ref=dst, send_sem=send, recv_sem=recv,
            device_id=where, device_id_type=MESH,
        )

    barrier = pltpu.get_barrier_semaphore()
    for d in range(1, row_count):
        pl.semaphore_signal(
            barrier, inc=1, device_id={"rows": lax.rem(r + d, row_count)},
            device_id_type=MESH,
        )
    for d in range(1, feat_count):
        for other in (r, r ^ 1):
            pl.semaphore_signal(
                barrier, inc=1,
                device_id={"rows": other, "feat": lax.rem(z + d, feat_count)},
                device_id_type=MESH,
            )
    pl.semaphore_wait(barrier, row_count - 1 + 2 * (feat_count - 1))

    def ag(dim, h, j, src, chip, rel, send):
        remote(
            src, all_ref.at[rows_of(chip, c, j), cols_of(h)],
            send, agr.at[rel, h, j], rows=r ^ (2 * dim),
        ).start()

    def own_plane(s):
        j = lax.rem(s, nch)

        @pl.when(s < nch)
        def _():
            ag(1, 0, j, x_ref.at[own_rows(j), cols_of(0)], p, 0, own_s.at[0])
            ag(2, 1, j, x_ref.at[own_rows(j), cols_of(1)], p, 1, own_s.at[1])

        @pl.when(s >= nch)
        def _():
            ag(1, 1, j, x_ref.at[own_rows(j), cols_of(1)], p, 0, own_s.at[0])
            ag(2, 0, j, x_ref.at[own_rows(j), cols_of(0)], p, 1, own_s.at[1])

    def own_line(j):
        for h in range(2):
            src = x_ref.at[own_rows(j), cols_of(h)]

            @pl.when(has_down & (p == 0))
            def _():
                remote(
                    src, abuf.at[z - 1, c, own_rows(j)], own_s.at[2], ar.at[0, c, j],
                    rows=2 * p + h, feat=z - 1,
                ).start()

            @pl.when(has_down & (p == z))
            def _():
                remote(
                    src, col_ref.at[rows_of(p, c, j)], own_s.at[2], br.at[0, c, j],
                    rows=2 * p + h, feat=z - 1,
                ).start()

            @pl.when(has_up & (p == last))
            def _():
                remote(
                    src, abuf.at[z, c, own_rows(j)], own_s.at[3], ar.at[0, c, j],
                    rows=2 * p + h, feat=z + 1,
                ).start()

            @pl.when(has_up & (p == z))
            def _():
                remote(
                    src, col_ref.at[rows_of(p, c, j)], own_s.at[3], br.at[0, c, j],
                    rows=2 * p + h, feat=z + 1,
                ).start()

    def own_sends(j, _):
        own_plane(2 * j)
        own_plane(2 * j + 1)
        own_line(j)
        return 0

    own = pltpu.make_async_copy(
        x_ref, all_ref.at[pl.ds(pl.multiple_of(r * n, n), n)], lsem.at[1]
    )
    own.start()
    lax.fori_loop(0, AHEAD, own_sends, 0)
    remote(
        x_ref, all_ref.at[pl.ds(pl.multiple_of(r * n, n), n)], part_s.at[3], pr.at[3],
        rows=r ^ 1,
    ).start()

    own.wait()
    st_ref[...] = jnp.zeros_like(st_ref)
    post = post_ref[...].astype(jnp.float32)
    for t in range(-(-n // 128)):
        count = min(128, n - 128 * t)
        here = pl.ds(128 * t, count)
        st_ref[8 + t:9 + t, 0:count] = label_ref[:, here].astype(jnp.float32)
        rows = pl.ds(pl.multiple_of(r * n + 128 * t, CHUNK), count)

        total = jnp.zeros((count, 128), jnp.float32)
        for i in range(width // 128):
            value = all_ref[rows, pl.ds(128 * i, 128)].astype(jnp.float32)
            total = total + value * post[i:i + 1, :]
        st_ref[t:t + 1, 0:count] = jnp.sum(total.T, axis=0, keepdims=True)
    gacc_ref[...] = jnp.zeros_like(gacc_ref)
    for t in range(width // 128):
        lanes = pl.ds(128 * t, 128)
        gacc_ref[0:1, lanes] = -prec_ref[:, lanes] * post[t:t + 1, :]
    lax.fori_loop(AHEAD, 2 * AHEAD, own_sends, 0)
    stat_local = pltpu.make_async_copy(st_ref, stat_ref.at[r, z], lsem.at[0])
    stat_local.start()
    for d in range(1, feat_count):
        remote(
            st_ref, stat_ref.at[r, z], ss.at[d], sr.at[d],
            feat=lax.rem(z + d, feat_count),
        ).start()

    def share_stats():
        stat_local.wait()
        for d in range(1, feat_count):
            remote(
                st_ref, stat_ref.at[r, lax.rem(z + feat_count - d, feat_count)],
                ss.at[d], sr.at[d], feat=z,
            ).wait_recv()
        for d in range(1, row_count):
            remote(
                stat_ref.at[r], stat_ref.at[r], ts.at[d], tr.at[d],
                rows=lax.rem(r + d, row_count),
            ).start()

    def weights():
        for d in range(1, row_count):
            origin = lax.rem(r + row_count - d, row_count)
            remote(
                stat_ref.at[origin], stat_ref.at[origin], ts.at[d], tr.at[d], rows=r
            ).wait_recv()

        def one(i, _):
            margins = stat_ref[i, 0, 0:8]
            for f in range(1, feat_count):
                margins = margins + stat_ref[i, f, 0:8]
            chance = 1.0 / (1.0 + jnp.exp(-margins))
            weight = (chance * (1.0 - chance)).astype(jnp.bfloat16)
            residual = (stat_ref[i, 0, 8:16] - chance).astype(jnp.bfloat16)
            for lead, value in ((0, weight), (1, residual)):
                turned = value.astype(jnp.float32).T
                for t in range(-(-n // 128)):
                    count = min(128, n - 128 * t)
                    rows = pl.ds(pl.multiple_of(i * n + 128 * t, CHUNK), count)
                    wr_ref[lead, rows, :] = jnp.broadcast_to(
                        turned[:count, t:t + 1], (count, 128)
                    ).astype(jnp.bfloat16)
            return 0

        lax.fori_loop(0, row_count, one, 0)

    def arrive(rel, h, j):
        chip = p ^ (rel + 1)
        here = all_ref.at[rows_of(chip, c, j), cols_of(h)]
        remote(here, here, own_s.at[0], agr.at[rel, h, j], rows=r).wait_recv()
        remote(here, here, part_s.at[rel], pr.at[rel], rows=r ^ 1).start()

    def forward(rel, h, j, send):
        chip = p ^ (rel + 1)
        here = all_ref.at[rows_of(chip, c, j), cols_of(h)]
        ag(2 - rel, h, j, here, chip, 2, send)

    def gather_event(s):
        a, j = s // nch, s % nch

        @pl.when(a == 0)
        def _():
            arrive(0, 0, j)

            @pl.when(relays)
            def _():
                forward(0, 0, j, relay_s.at[0])
            arrive(1, 1, j)

            @pl.when(relays)
            def _():
                forward(1, 1, j, relay_s.at[1])

        @pl.when(a == 1)
        def _():
            arrive(0, 1, j)

            @pl.when(relays_all)
            def _():
                forward(0, 1, j, extra_s.at[0])
            arrive(1, 0, j)

            @pl.when(relays_all)
            def _():
                forward(1, 0, j, extra_s.at[1])

    def corner_event(j):
        arrive(2, 0, j)
        arrive(2, 1, j)

    def source_event(s):
        q, j = 1 + s // nch, s % nch
        for h in range(2):
            @pl.when(has_down)
            def _():
                where = rows_of(pick(p, q, 0), c, j)
                remote(
                    all_ref.at[where, cols_of(h)], col_ref.at[where],
                    src_s.at[0, q], br.at[q, c, j], rows=2 * p + h, feat=z - 1,
                ).start()

            @pl.when(has_up)
            def _():
                where = rows_of(pick(p, q, last), c, j)
                remote(
                    all_ref.at[where, cols_of(h)], col_ref.at[where],
                    src_s.at[1, q], br.at[q, c, j], rows=2 * p + h, feat=z + 1,
                ).start()

    def column_event(s):
        q, j = s // nch, s % nch
        down = p > z
        chip = pick(p, q, jnp.where(down, 0, last))
        for k in range(2):
            here = col_ref.at[rows_of(chip, k, j)]
            remote(here, here, bf_s.at[q], br.at[q, k, j], rows=r).wait_recv()

            @pl.when((down & has_down) | (~down & has_up))
            def _():
                remote(
                    here, here, bf_s.at[q], br.at[q, k, j],
                    feat=jnp.where(down, z - 1, z + 1),
                ).start()

    def pass_event(s):
        q, j = s // nch, s % nch
        down = p == 0
        block = jnp.where(down, z + 1 + q, z - 1 - q)
        slot = jnp.where(down, block - 1, block)

        @pl.when((block >= 0) & (block <= last))
        def _():
            for k in range(2):
                here = abuf.at[slot, k, own_rows(j)]
                remote(here, here, af_s.at[q], ar.at[q, k, j], rows=r).wait_recv()

                @pl.when((down & has_down) | (~down & has_up))
                def _():
                    remote(
                        here, here, af_s.at[q], ar.at[q + 1, k, j],
                        feat=jnp.where(down, z - 1, z + 1),
                    ).start()

    def deliver_event(s):
        q, j = s // nch, s % nch
        down = p == 0
        block = jnp.where(down, z + 1 + q, z - 1 - q)
        slot = jnp.where(down, block - 1, block)

        @pl.when((block >= 0) & (block <= last))
        def _():
            for k in range(2):
                remote(
                    abuf.at[slot, k, own_rows(j)], col_ref.at[rows_of(p, k, j)],
                    ad_s.at[q], adr.at[j // (nch // 3)], rows=2 * block + c,
                ).start()

    items = last
    lag = nch // 2 + 3
    tiles = width // TILE
    edge = passed_chip(p, z, last)
    twice = col_ref.at[pl.ds(0, 2 * n)]
    third = n // 3
    once = col_ref.at[pl.ds(0, 2 * third)]
    q = nch // 3
    begins = [3 * q, 4 * q + 1, 5 * q + 1, 6 * q, 7 * q, 8 * q]
    ends = [4 * q, 5 * q + 1, 6 * q, 7 * q, 8 * q, 9 * q]
    near, far = pick(p, 1, edge), pick(p, 2, edge)

    def partner_rows(chip):
        rel = jnp.where(chip == p, 3, (p ^ chip) - 1)
        there = all_ref.at[pl.ds(pl.multiple_of((2 * chip + 1 - c) * n, n), n)]
        remote(there, there, part_s.at[rel], pr.at[rel], rows=r).wait_recv()

        @pl.when(p == z)
        def _():
            rows = pl.ds(pl.multiple_of(chip * 2 * n, n), 2 * n)
            copy = pltpu.make_async_copy(
                all_ref.at[rows, cols_of(c)], col_ref.at[rows], lsem.at[2]
            )
            copy.start()
            copy.wait()

    def prepare(i):
        rows = pl.ds(pl.multiple_of(i * TILE, TILE), TILE)
        h_ref[rows, :] = jnp.zeros((TILE, half), jnp.float32)
        offset = i * TILE - c * half

        @pl.when((p == z) & (offset >= 0) & (offset < half))
        def _():
            cols = pl.ds(pl.multiple_of(offset, TILE), TILE)
            shape = (TILE, TILE)
            same = lax.broadcasted_iota(jnp.int32, shape, 0) == lax.broadcasted_iota(
                jnp.int32, shape, 1
            )
            h_ref[rows, cols] = jnp.where(
                same, jnp.broadcast_to(prec_ref[:, rows], shape), 0.0
            )

    def unit_rows(index):
        def start(chip, core, piece):
            return (chip * 2 + core) * n + piece * third

        late = jnp.where(index == 2, 2, index - 4 + (index == 3))
        rows = []
        for i in range(4):
            core, upper = i % 2, i // 2
            pair = jnp.where(
                index == 0, start(p, core, upper),
                jnp.where(
                    index == 1, start(near if upper else p, core, 0 if upper else 2),
                    start(near, core, 1 + upper),
                ),
            )
            far_rows = start(edge if upper else far, core, late)
            rows.append(jnp.where((index == 0) | (index == 1) | (index == 3), pair, far_rows))
        return rows

    def part_of(i):
        return pl.ds(pl.multiple_of(i * PART, PART), PART)

    def turn(rows, i, flag):
        weighted, pulled = weigh(all_ref, wr_ref, rows, third, part_of(i))
        gacc_ref[:, part_of(i)] += pulled * flag
        return weighted

    def multiply(turned, rows, i):
        value = turned[...]
        for t in range(half // TILE):
            there = pl.ds(t * TILE, TILE)
            h_ref[part_of(i), there] += jnp.dot(
                value, slabs(col_ref, None, rows, third, there),
                preferred_element_type=jnp.float32,
            )

    def compute(u):
        index = sum((u >= s).astype(jnp.int32) for s in begins) - 1

        def choose(values):
            out = values[0]
            for i in range(1, len(values)):
                out = jnp.where(index >= i, values[i], out)
            return out

        begin, span = choose(begins), choose([e - s for s, e in zip(begins, ends)])
        low = jnp.minimum((u - begin) * tiles // span, tiles)
        high = jnp.minimum((u - begin + 1) * tiles // span, tiles)
        rows = unit_rows(index)

        @pl.when(u == begin)
        def _():
            @pl.when(index == 0)
            def _():
                weights()
                partner_rows(p)

            @pl.when(index == 1)
            def _():
                partner_rows(near)

            @pl.when(index == 2)
            def _():
                partner_rows(far)
                partner_rows(edge)

            @pl.when((index >= 4) & (p != z))
            def _():
                remote(once, once, bf_s.at[0], adr.at[index - 4], rows=r).wait_recv()

            @pl.when(index != 2)
            def _():
                even[...] = turn(rows, 0, 1.0)

        def keep(i, _):
            for e in range(2):
                kept[part_of(2 * i + e), :] = turn(rows, 2 * i + e, 1.0)
            return 0

        def pair(i, _):
            multiply(even, rows, 2 * i)
            odd[...] = turn(rows, 2 * i + 1, 1.0)
            multiply(odd, rows, 2 * i + 1)
            more = i < tiles - 1
            even[...] = turn(
                rows, jnp.where(more, 2 * i + 2, 0), jnp.where(more, 1.0, 0.0)
            )
            return 0

        @pl.when(index == 2)
        def _():
            lax.fori_loop(low, high, keep, 0)

            @pl.when(u == ends[2] - 1)
            def _():
                pltpu.make_async_copy(kept, turned_out, lsem.at[3]).start()

        @pl.when(index != 2)
        def _():
            lax.fori_loop(low, high, pair, 0)

    def some(event, low, high):
        def one(i, _):
            event(i)
            return 0
        lax.fori_loop(low, high, one, 0)

    def step(u, _):
        @pl.when((p != z) & (u < items * nch))
        def _():
            column_event(u)

        @pl.when(u == 3)
        def _():
            share_stats()

        @pl.when((u >= 1) & (u < 3))
        def _():
            own_sends(2 * AHEAD - 1 + u, 0)

        @pl.when(u >= 3)
        def _():
            low = 2 * AHEAD + 2 + 2 * (u - 3)
            some(lambda j: own_sends(j, 0), low, jnp.minimum(low + 2, nch))

        @pl.when((u >= 3) & (u < 3 + nch))
        def _():
            some(gather_event, 2 * u - 6, 2 * u - 4)

        corner = 9 * q // 2

        @pl.when((u >= corner) & (u < corner + q))
        def _():
            some(corner_event, 3 * (u - corner), 3 * (u - corner) + 3)

        @pl.when((p == z) & (u >= lag) & (u < lag + 2 * nch))
        def _():
            source_event(u - lag)

        @pl.when(((p == 0) | (p == last)) & (u >= 1) & (u < 1 + items * nch))
        def _():
            pass_event(u - 1)

        @pl.when(((p == 0) | (p == last)) & (u >= nch))
        def _():
            low = jnp.minimum(2 * (u - nch), u - 1)
            some(deliver_event, low, jnp.minimum(2 * (u + 1 - nch), u))

        @pl.when(u < begins[0])
        def _():
            per = -(-tiles // begins[0])
            some(prepare, jnp.minimum(u * per, tiles), jnp.minimum(u * per + per, tiles))

        @pl.when((u >= begins[0]) & (u < ends[-1]))
        def _():
            compute(u)
        return 0

    lax.fori_loop(0, items * nch + 1, step, 0)

    @pl.when(p != z)
    def _():
        remote(once, once, bf_s.at[0], adr.at[2], rows=r).wait_recv()

    outs = [pltpu.make_async_copy(gacc_ref, pull_out, lsem.at[4])]
    for i, start in enumerate(unit_rows(jnp.int32(2))):
        outs.append(pltpu.make_async_copy(
            col_ref.at[pl.ds(pl.multiple_of(start, CHUNK), third)],
            cols_out.at[pl.ds(i * third, third)], lsem.at[5 + i],
        ))
    for copy in outs:
        copy.start()

    def sent(ref, sem):
        remote(ref, ref, sem, pr.at[3], rows=r).wait_send()

    for d in range(1, feat_count):
        sent(st_ref, ss.at[d])
    for d in range(1, row_count):
        sent(stat_ref.at[r], ts.at[d])
    for i in range(2):
        sent(x_ref, own_s.at[i])

        @pl.when(relays)
        def _():
            sent(x_ref.at[:, pl.ds(0, half)], relay_s.at[i])

        @pl.when(relays_all)
        def _():
            sent(x_ref.at[:, pl.ds(0, half)], extra_s.at[i])

    @pl.when(has_down & ((p == 0) | (p == z)))
    def _():
        sent(x_ref, own_s.at[2])

    @pl.when(has_up & ((p == last) | (p == z)))
    def _():
        sent(x_ref, own_s.at[3])
    for rel in range(4):
        sent(x_ref, part_s.at[rel])
    down = p > z
    for q in range(items):
        if q > 0:
            @pl.when((p == z) & has_down)
            def _():
                sent(x_ref, src_s.at[0, q])

            @pl.when((p == z) & has_up)
            def _():
                sent(x_ref, src_s.at[1, q])

        @pl.when((p != z) & ((down & has_down) | (~down & has_up)))
        def _():
            sent(twice, bf_s.at[q])
        for edge, block, more in ((0, z + 1 + q, has_down), (last, z - 1 - q, has_up)):
            @pl.when((p == edge) & (block >= 0) & (block <= last))
            def _():
                sent(twice, ad_s.at[q])

                @pl.when(more)
                def _():
                    sent(twice, af_s.at[q])
    for copy in outs:
        copy.wait()
    pltpu.make_async_copy(kept, turned_out, lsem.at[3]).wait()


def line_stage(features, labels, post, prec):
    row_count = lax.axis_size("rows")
    feat_count = lax.axis_size("feat")
    n, width = features.shape
    half = width // 2
    items = feat_count - 1
    nch = n // CHUNK
    dma = pltpu.SemaphoreType.DMA
    return pl.pallas_call(
        functools.partial(line_kernel, row_count, feat_count),
        out_shape=(
            pltpu.VMEM((width, half), jnp.float32),
            pltpu.HBM((width, 4 * n // 3), features.dtype),
            pltpu.HBM((4 * n // 3, half), features.dtype),
            pltpu.HBM((8, width), jnp.float32),
        ),
        in_specs=[
            pl.BlockSpec(memory_space=pl.ANY), pl.BlockSpec(memory_space=pltpu.VMEM),
            pl.BlockSpec(memory_space=pltpu.VMEM), pl.BlockSpec(memory_space=pltpu.VMEM),
        ],
        out_specs=[pl.BlockSpec(memory_space=pltpu.VMEM)]
        + [pl.BlockSpec(memory_space=pl.ANY)] * 3,
        scratch_shapes=[
            pltpu.VMEM((row_count * n, width), features.dtype),
            pltpu.VMEM((row_count * n, half), features.dtype),
            pltpu.VMEM((2, row_count * n, 128), features.dtype),
            pltpu.VMEM((8, width), jnp.float32),
            pltpu.VMEM((width, 4 * n // 3), features.dtype),
            pltpu.VMEM((PART, 4 * n // 3), features.dtype),
            pltpu.VMEM((PART, 4 * n // 3), features.dtype),
            pltpu.VMEM((items, 2, n, half), features.dtype),
            pltpu.VMEM((16, 128), jnp.float32),
            pltpu.VMEM((row_count, feat_count, 16, 128), jnp.float32),
            dma((3, 2, nch)), dma((4,)), dma((items, 2, nch)), dma((items + 1, 2, nch)),
            dma((3,)),
            dma((4,)), dma((2,)), dma((2,)), dma((4,)), dma((2, items)), dma((items,)),
            dma((items,)), dma((items,)),
            dma((feat_count,)), dma((feat_count,)),
            dma((row_count,)), dma((row_count,)),
            dma((9,)),
        ],
        compiler_params=pltpu.CompilerParams(
            collective_id=0, has_side_effects=True, vmem_limit_bytes=30 * 1024 * 1024
        ),
        name="line_stage",
    )(features, labels, post, prec)


def last_kernel(
    h_ref, turned_ref, cols_ref, gacc_ref,
    out_ref, grad_ref, stage, turned, cols, gacc, grad, sem, lsem, tsem,
):
    width, half = h_ref.shape
    slots = stage.shape[0]
    count = width // PART
    load = pltpu.make_async_copy(cols_ref, cols, lsem.at[0])
    load.start()

    def part_of(i):
        return pl.ds(pl.multiple_of(i * PART, PART), PART)

    def take(i):
        return pltpu.make_async_copy(
            turned_ref.at[part_of(i)], turned.at[part_of(i)], tsem.at[i]
        )

    def put(i):
        slot = lax.rem(i, slots)
        return pltpu.make_async_copy(stage.at[slot], out_ref.at[part_of(i)], sem.at[slot])

    for i in range(count):
        take(i).start()
    late = pltpu.make_async_copy(gacc_ref, gacc, lsem.at[1])
    late.start()
    load.wait()

    def one(i, _):
        @pl.when(i >= slots)
        def _():
            put(i - slots).wait()
        take(i).wait()
        slot = lax.rem(i, slots)
        value = turned[part_of(i), :]
        for t in range(half // TILE):
            there = pl.ds(t * TILE, TILE)
            stage[slot, :, there] = h_ref[part_of(i), there] + jnp.dot(
                value, cols[:, there], preferred_element_type=jnp.float32
            )
        put(i).start()
        return 0

    lax.fori_loop(0, count, one, 0)
    late.wait()
    grad[...] = jnp.sum(gacc[...], axis=0, keepdims=True)
    give = pltpu.make_async_copy(grad, grad_ref, lsem.at[2])
    give.start()
    for i in range(max(0, count - slots), count):
        put(i).wait()
    give.wait()


def last_stage(h, turned, cols, gacc):
    width, half = h.shape
    dma = pltpu.SemaphoreType.DMA
    h = pltpu.with_memory_space_constraint(h, pltpu.VMEM)
    kept = [pltpu.with_memory_space_constraint(a, pltpu.HBM) for a in (turned, cols, gacc)]
    return pl.pallas_call(
        last_kernel,
        out_shape=(
            pltpu.HBM((width, half), jnp.float32),
            pltpu.HBM((1, width), jnp.float32),
        ),
        in_specs=[pl.BlockSpec(memory_space=pltpu.VMEM)]
        + [pl.BlockSpec(memory_space=pl.ANY)] * 3,
        out_specs=[pl.BlockSpec(memory_space=pl.ANY)] * 2,
        scratch_shapes=[
            pltpu.VMEM((3, PART, half), jnp.float32),
            pltpu.VMEM(turned.shape, turned.dtype),
            pltpu.VMEM(cols.shape, cols.dtype),
            pltpu.VMEM(gacc.shape, gacc.dtype),
            pltpu.VMEM((1, width), jnp.float32),
            dma((3,)), dma((3,)), dma((width // PART,)),
        ],
        compiler_params=pltpu.CompilerParams(vmem_limit_bytes=14 * 1024 * 1024),
        name="last_stage",
    )(h, *kept)


def paired(row_count, feat_count, n, width):
    half = width // 2
    rows = row_count * n
    held = 4 * width * half + 2 * rows * (width + half + 256) + 12 * n * half + 4 * n * width
    return (
        row_count == 2 * feat_count and (feat_count - 1).bit_length() == 2
        and feat_count & (feat_count - 1) == 0 and n % (3 * CHUNK) == 0 and n // CHUNK >= 3 * AHEAD + 3
        and n <= 1024 and half % TILE == 0 and held <= VMEM_BUDGET
    )


def by_lines(features, labels, posterior, prior_prec):
    n, width = features.shape
    held = line_stage(
        features, labels.reshape(1, n), posterior.reshape(width // 128, 128),
        prior_prec.reshape(1, width),
    )
    hessian, gradient = last_stage(*held)
    return (hessian, gradient.reshape(width))


def gather_kernel(
    row_count, feat_count, x_ref, st_ref, all_ref, col_ref, stat_ref,
    ring, zs, zr, ps, pr, ds, dr, cs, cr, cl, ss, sr, ts, tr, lsem,
):
    r = lax.axis_index("rows")
    f = lax.axis_index("feat")
    n, width = x_ref.shape
    half = width // 2
    col_width = col_ref.shape[1]
    unit = min(col_width, half)
    per_half = half // unit
    per_owner = col_width // unit
    chips = row_count // 2
    bits = chips.bit_length() - 1
    part = n // SPLIT

    def rows_of(device):
        return pl.ds(pl.multiple_of(device * n, n), n)

    def remote(src, dst, send, recv, **where):
        return pltpu.make_async_remote_copy(
            src_ref=src, dst_ref=dst, send_sem=send, recv_sem=recv,
            device_id=where, device_id_type=MESH,
        )

    sends = []

    def go(copy):
        copy.start()
        sends.append(copy)

    def ring_slice(step, h, k):
        rows, cols = pl.ds(k * part, part), pl.ds(h * half, half)
        return x_ref.at[rows, cols] if step == 0 else ring.at[step - 1, rows, cols]

    def ring_copy(step, h, k):
        to = lax.rem(f + (1 if h == 0 else feat_count - 1), feat_count)
        return remote(
            ring_slice(step, h, k),
            ring.at[step, pl.ds(k * part, part), pl.ds(h * half, half)],
            zs.at[step, h, k], zr.at[step, h, k], feat=to,
        )

    def column_sends(step, h, k, start):
        block = lax.rem(f + (feat_count - step if h == 0 else step), feat_count)
        for u in range(per_half):
            inner = h * half + u * unit
            if width % col_width == 0:
                owner = block * (width // col_width) + inner // col_width
                offset = inner % col_width
                slot = offset // unit
            else:
                owner = (block * width + inner) // col_width
                slot = ((block * width + inner) % col_width) // unit
                offset = pl.multiple_of(slot * unit, unit)
            src = ring_slice(step, h, k).at[:, pl.ds(u * unit, unit)]
            dst = col_ref.at[
                pl.ds(pl.multiple_of(r * n + k * part, part), part), pl.ds(offset, unit)
            ]
            send = cs.at[step, h, k, u]

            @pl.when(owner != r)
            def _():
                copy = remote(src, dst, send, cr.at[r, slot, k], rows=owner)
                copy.start() if start else copy.wait_send()

            if start:
                @pl.when(owner == r)
                def _():
                    pltpu.make_async_copy(src, dst, cl.at[slot, k]).start()

    def order(h):
        return list(range(bits)) if h == 0 else list(range(bits))[::-1]

    def spread(h, stage, mask):
        bit = 1 << order(h)[stage]
        origin = r ^ (2 * mask)
        cols = pl.ds(h * half, half)
        src = x_ref.at[:, cols] if mask == 0 else all_ref.at[rows_of(origin), cols]
        return remote(
            src, all_ref.at[rows_of(origin), cols],
            ps.at[h, mask | bit], pr.at[h, mask | bit], rows=r ^ (2 * bit),
        )

    def partner(h, mask):
        origin = r ^ (2 * mask)
        cols = pl.ds(h * half, half)
        src = x_ref.at[:, cols] if mask == 0 else all_ref.at[rows_of(origin), cols]
        return remote(
            src, all_ref.at[rows_of(origin), cols],
            ds.at[h, mask], dr.at[h, mask], rows=r ^ 1,
        )

    def masks_before(h, stage):
        found = [0]
        for b in order(h)[:stage]:
            found += [m | (1 << b) for m in found]
        return found

    for k in range(SPLIT):
        for h in range(2):
            go(ring_copy(0, h, k))
    stat_local = pltpu.make_async_copy(st_ref, stat_ref.at[r, f], lsem.at[0])
    stat_local.start()
    for d in range(1, feat_count):
        go(remote(
            st_ref, stat_ref.at[r, f], ss.at[d], sr.at[d],
            feat=lax.rem(f + d, feat_count),
        ))
    for stage in range(bits):
        for h in range(2):
            go(spread(h, stage, 0))
    for h in range(2):
        go(partner(h, 0))
    own = pltpu.make_async_copy(x_ref, all_ref.at[rows_of(r)], lsem.at[1])
    own.start()
    for k in range(SPLIT):
        for h in range(2):
            column_sends(0, h, k, True)

    stat_local.wait()
    for d in range(1, feat_count):
        remote(
            st_ref, stat_ref.at[r, lax.rem(f + feat_count - d, feat_count)],
            ss.at[d], sr.at[d], feat=f,
        ).wait_recv()
    for d in range(1, row_count):
        go(remote(
            stat_ref.at[r], stat_ref.at[r], ts.at[d], tr.at[d],
            rows=lax.rem(r + d, row_count),
        ))

    def relay(stage):
        for h in range(2):
            bit = 1 << order(h)[stage]
            for m in masks_before(h, stage):
                mask = m | bit
                cols = pl.ds(h * half, half)
                remote(
                    x_ref.at[:, cols], all_ref.at[rows_of(r ^ (2 * mask)), cols],
                    ps.at[h, mask], pr.at[h, mask], rows=r,
                ).wait_recv()
                for later in range(stage + 1, bits):
                    go(spread(h, later, mask))
                go(partner(h, mask))

    for step in range(1, feat_count):
        for k in range(SPLIT):
            for h in range(2):
                ring_copy(step - 1, h, k).wait_recv()
                if step < feat_count - 1:
                    go(ring_copy(step, h, k))
                column_sends(step, h, k, True)
        if step <= bits:
            relay(step - 1)
    for stage in range(feat_count - 1, bits):
        relay(stage)

    for h in range(2):
        for mask in range(chips):
            cols = pl.ds(h * half, half)
            remote(
                x_ref.at[:, cols], all_ref.at[rows_of(r ^ (2 * mask) ^ 1), cols],
                ds.at[h, mask], dr.at[h, mask], rows=r,
            ).wait_recv()
    for d in range(1, row_count):
        origin = lax.rem(r + row_count - d, row_count)
        remote(
            stat_ref.at[origin], stat_ref.at[origin], ts.at[d], tr.at[d], rows=r
        ).wait_recv()
        for slot in range(per_owner):
            for k in range(SPLIT):
                dst = col_ref.at[
                    pl.ds(pl.multiple_of(origin * n + k * part, part), part),
                    pl.ds(slot * unit, unit),
                ]
                remote(
                    x_ref.at[pl.ds(0, part), pl.ds(0, unit)], dst,
                    cs.at[0, 0, 0, 0], cr.at[origin, slot, k], rows=r,
                ).wait_recv()
    for slot in range(per_owner):
        for k in range(SPLIT):
            dst = col_ref.at[
                pl.ds(pl.multiple_of(r * n + k * part, part), part),
                pl.ds(slot * unit, unit),
            ]
            pltpu.make_async_copy(
                x_ref.at[pl.ds(0, part), pl.ds(0, unit)], dst, cl.at[slot, k]
            ).wait()
    own.wait()
    for copy in sends:
        copy.wait_send()
    for step in range(feat_count):
        for k in range(SPLIT):
            for h in range(2):
                column_sends(step, h, k, False)


def gather(features, stats):
    row_count = lax.axis_size("rows")
    feat_count = lax.axis_size("feat")
    n, width = features.shape
    half = width // 2
    col_width = width * feat_count // row_count
    unit = min(col_width, half)
    chips = row_count // 2
    dma = pltpu.SemaphoreType.DMA
    return pl.pallas_call(
        functools.partial(gather_kernel, row_count, feat_count),
        out_shape=(
            jax.ShapeDtypeStruct((row_count * n, width), features.dtype),
            jax.ShapeDtypeStruct((row_count * n, col_width), features.dtype),
            jax.ShapeDtypeStruct((row_count, feat_count) + stats.shape, stats.dtype),
        ),
        in_specs=[pl.BlockSpec(memory_space=pltpu.VMEM)] * 2,
        out_specs=[pl.BlockSpec(memory_space=pl.ANY)] * 3,
        scratch_shapes=[
            pltpu.VMEM((feat_count - 1, n, width), features.dtype),
            dma((feat_count - 1, 2, SPLIT)), dma((feat_count - 1, 2, SPLIT)),
            dma((2, chips)), dma((2, chips)),
            dma((2, chips)), dma((2, chips)),
            dma((feat_count, 2, SPLIT, half // unit)),
            dma((row_count, col_width // unit, SPLIT)),
            dma((col_width // unit, SPLIT)),
            dma((feat_count,)), dma((feat_count,)),
            dma((row_count,)), dma((row_count,)),
            dma((2,)),
        ],
        compiler_params=pltpu.CompilerParams(
            has_side_effects=True, vmem_limit_bytes=32 * 1024 * 1024
        ),
        name="gather",
    )(features, stats)


def per_device(features, labels, posterior, prior_prec):
    row_count = lax.axis_size("rows")
    feat_count = lax.axis_size("feat")
    row_index = lax.axis_index("rows")
    feat_index = lax.axis_index("feat")
    n, block_width = features.shape
    if paired(row_count, feat_count, n, block_width):
        return by_lines(features, labels, posterior, prior_prec)
    col_width = block_width * feat_count // row_count
    partial_value = jnp.dot(features, posterior, preferred_element_type=jnp.float32)
    padded = -(-n // 512) * 512
    stats = jnp.concatenate([
        jnp.pad(partial_value, (0, padded - n)),
        jnp.pad(labels.astype(jnp.float32), (0, padded - n)),
    ]).reshape(-1, 128)
    all_rows, column_rows, all_stats = gather(features, stats)
    all_stats = all_stats.reshape(row_count, feat_count, 2, padded)[..., :n]
    margins = jnp.sum(all_stats[:, :, 0], axis=1).reshape(-1)
    all_labels = all_stats[:, 0, 1].reshape(-1)
    chance = jax.nn.sigmoid(margins)
    weight = (chance * (1.0 - chance)).astype(jnp.bfloat16)
    residual = (all_labels - chance).astype(jnp.bfloat16)
    summed = jnp.dot(residual, all_rows, preferred_element_type=jnp.float32)
    gradient = summed - prior_prec * posterior.astype(jnp.float32)
    weighted = weight[:, None] * all_rows
    product = lax.dot_general(
        weighted, column_rows, (((0,), (0,)), ((), ())), preferred_element_type=jnp.float32
    )
    global_rows = feat_index * block_width + jnp.arange(block_width, dtype=jnp.int32)
    global_cols = row_index * col_width + jnp.arange(col_width, dtype=jnp.int32)
    on_diagonal = global_rows[:, None] == global_cols[None, :]
    hessian = product + jnp.where(on_diagonal, prior_prec[:, None], jnp.float32(0.0))
    return (hessian, gradient)


def solution(mesh):
    in_specs = (P("rows", "feat"), P("rows"), P("feat"), P("feat"))
    out_specs = (P("feat", "rows"), P("feat"))
    return jax.shard_map(
        per_device, mesh=mesh, in_specs=in_specs, out_specs=out_specs, check_vma=False
    )
```

```python
import functools

import jax
import jax.numpy as jnp
from jax import lax
from jax.experimental import pallas as pl
from jax.experimental.pallas import tpu as pltpu
from jax.sharding import PartitionSpec as P

MESH = pl.DeviceIdType.MESH
SPLIT = 2
CHUNK = 16
TILE = 512
PART = 256
AHEAD = 2
LATE = 4
VMEM_BUDGET = 60 * 1024 * 1024


def pick(p, q, e):
    first = jnp.where((p ^ 1) == e, p ^ 2, p ^ 1)
    second = jnp.where(((p ^ 1) == e) | ((p ^ 2) == e), p ^ 3, p ^ 2)
    return jnp.where(q == 0, p, jnp.where(q == 1, first, second))


def passed_chip(p, z, last):
    return jnp.where(p > z, 0, jnp.where(p < z, last, p ^ 3))


def slabs(ref, lead, starts, size, cols):
    parts = []
    for start in starts:
        rows = pl.ds(pl.multiple_of(start, CHUNK), size)
        parts.append(ref[rows, cols] if lead is None else ref[lead, rows, cols])
    return jnp.concatenate(parts, axis=0)


def wide(value, width):
    return jnp.concatenate([value] * (width // value.shape[1]), axis=1)


def weigh(all_ref, wr_ref, starts, size, cols):
    x = slabs(all_ref, None, starts, size, cols)
    weight = slabs(wr_ref, 0, starts, size, slice(None))
    residual = slabs(wr_ref, 1, starts, size, slice(None)).astype(jnp.float32)
    pulled = x.astype(jnp.float32) * wide(residual, PART)
    pulled = jnp.sum(pulled.reshape(-1, 8, PART), axis=0)
    return (x * wide(weight, PART)).T, pulled


def line_kernel(
    row_count, feat_count, x_ref, label_ref, post_ref, prec_ref,
    h_ref, turned_out, cols_out, pull_out,
    all_ref, col_ref, wr_ref, gacc_ref, kept, even, odd, abuf, st_ref, stat_ref,
    agr, pr, br, ar, adr, own_s, relay_s, extra_s, part_s, src_s, bf_s, af_s, ad_s,
    ss, sr, ts, tr, lsem,
):
    r = lax.axis_index("rows")
    z = lax.axis_index("feat")
    p, c = r // 2, r % 2
    last = feat_count - 1
    n, width = x_ref.shape
    half = width // 2
    m = CHUNK
    nch = n // m
    avoid = jnp.where(z == 0, 0, jnp.where(z == last, last, -1))
    relays = p != avoid
    relays_all = (p ^ last) == avoid
    has_down, has_up = z >= 1, z <= last - 1

    def rows_of(chip, core, j):
        return pl.ds(pl.multiple_of((chip * 2 + core) * n + j * m, m), m)

    def own_rows(j):
        return pl.ds(pl.multiple_of(j * m, m), m)

    def cols_of(h):
        return pl.ds(pl.multiple_of(h * half, half), half)

    def remote(src, dst, send, recv, **where):
        return pltpu.make_async_remote_copy(
            src_ref=src, dst_ref=dst, send_sem=send, recv_sem=recv,
            device_id=where, device_id_type=MESH,
        )

    barrier = pltpu.get_barrier_semaphore()
    for d in range(1, row_count):
        pl.semaphore_signal(
            barrier, inc=1, device_id={"rows": lax.rem(r + d, row_count)},
            device_id_type=MESH,
        )
    for d in range(1, feat_count):
        for other in (r, r ^ 1):
            pl.semaphore_signal(
                barrier, inc=1,
                device_id={"rows": other, "feat": lax.rem(z + d, feat_count)},
                device_id_type=MESH,
            )

    own = pltpu.make_async_copy(
        x_ref, all_ref.at[pl.ds(pl.multiple_of(r * n, n), n)], lsem.at[1]
    )
    own.start()
    own.wait()
    st_ref[...] = jnp.zeros_like(st_ref)
    post = post_ref[...].astype(jnp.float32)
    for t in range(-(-n // 128)):
        count = min(128, n - 128 * t)
        here = pl.ds(128 * t, count)
        st_ref[8 + t:9 + t, 0:count] = label_ref[:, here].astype(jnp.float32)
        rows = pl.ds(pl.multiple_of(r * n + 128 * t, CHUNK), count)

        total = jnp.zeros((count, 128), jnp.float32)
        for i in range(width // 128):
            value = all_ref[rows, pl.ds(128 * i, 128)].astype(jnp.float32)
            total = total + value * post[i:i + 1, :]
        st_ref[t:t + 1, 0:count] = jnp.sum(total.T, axis=0, keepdims=True)
    gacc_ref[...] = jnp.zeros_like(gacc_ref)
    for t in range(width // 128):
        lanes = pl.ds(128 * t, 128)
        gacc_ref[0:1, lanes] = -prec_ref[:, lanes] * post[t:t + 1, :]
    pl.semaphore_wait(barrier, row_count - 1 + 2 * (feat_count - 1))

    def ag(dim, h, j, src, chip, rel, send):
        remote(
            src, all_ref.at[rows_of(chip, c, j), cols_of(h)],
            send, agr.at[rel, h, j], rows=r ^ (2 * dim),
        ).start()

    def own_plane(s):
        j = lax.rem(s, nch)

        @pl.when(s < nch)
        def _():
            ag(1, 0, j, x_ref.at[own_rows(j), cols_of(0)], p, 0, own_s.at[0])
            ag(2, 1, j, x_ref.at[own_rows(j), cols_of(1)], p, 1, own_s.at[1])

        @pl.when(s >= nch)
        def _():
            ag(1, 1, j, x_ref.at[own_rows(j), cols_of(1)], p, 0, own_s.at[0])
            ag(2, 0, j, x_ref.at[own_rows(j), cols_of(0)], p, 1, own_s.at[1])

    def own_line(j):
        for h in range(2):
            src = x_ref.at[own_rows(j), cols_of(h)]

            @pl.when(has_down & (p == 0))
            def _():
                remote(
                    src, abuf.at[z - 1, c, own_rows(j)], own_s.at[2], ar.at[0, c, j],
                    rows=2 * p + h, feat=z - 1,
                ).start()

            @pl.when(has_down & (p == z))
            def _():
                remote(
                    src, col_ref.at[rows_of(p, c, j)], own_s.at[2], br.at[0, c, j],
                    rows=2 * p + h, feat=z - 1,
                ).start()

            @pl.when(has_up & (p == last))
            def _():
                remote(
                    src, abuf.at[z, c, own_rows(j)], own_s.at[3], ar.at[0, c, j],
                    rows=2 * p + h, feat=z + 1,
                ).start()

            @pl.when(has_up & (p == z))
            def _():
                remote(
                    src, col_ref.at[rows_of(p, c, j)], own_s.at[3], br.at[0, c, j],
                    rows=2 * p + h, feat=z + 1,
                ).start()

    def own_sends(j, _):
        own_plane(2 * j)
        own_plane(2 * j + 1)
        own_line(j)
        return 0

    own_sends(0, 0)
    remote(
        x_ref, all_ref.at[pl.ds(pl.multiple_of(r * n, n), n)], part_s.at[3], pr.at[3],
        rows=r ^ 1,
    ).start()

    stat_local = pltpu.make_async_copy(st_ref, stat_ref.at[r, z], lsem.at[0])
    stat_local.start()
    for d in range(1, feat_count):
        remote(
            st_ref, stat_ref.at[r, z], ss.at[d], sr.at[d],
            feat=lax.rem(z + d, feat_count),
        ).start()

    def share_stats():
        stat_local.wait()
        for d in range(1, feat_count):
            remote(
                st_ref, stat_ref.at[r, lax.rem(z + feat_count - d, feat_count)],
                ss.at[d], sr.at[d], feat=z,
            ).wait_recv()
        for d in range(1, row_count):
            remote(
                stat_ref.at[r], stat_ref.at[r], ts.at[d], tr.at[d],
                rows=lax.rem(r + d, row_count),
            ).start()

    def weights():
        for d in range(1, row_count):
            origin = lax.rem(r + row_count - d, row_count)
            remote(
                stat_ref.at[origin], stat_ref.at[origin], ts.at[d], tr.at[d], rows=r
            ).wait_recv()

        def one(i, _):
            margins = stat_ref[i, 0, 0:8]
            for f in range(1, feat_count):
                margins = margins + stat_ref[i, f, 0:8]
            chance = 1.0 / (1.0 + jnp.exp(-margins))
            weight = (chance * (1.0 - chance)).astype(jnp.bfloat16)
            residual = (stat_ref[i, 0, 8:16] - chance).astype(jnp.bfloat16)
            for lead, value in ((0, weight), (1, residual)):
                turned = value.astype(jnp.float32).T
                for t in range(-(-n // 128)):
                    count = min(128, n - 128 * t)
                    rows = pl.ds(pl.multiple_of(i * n + 128 * t, CHUNK), count)
                    wr_ref[lead, rows, :] = jnp.broadcast_to(
                        turned[:count, t:t + 1], (count, 128)
                    ).astype(jnp.bfloat16)
            return 0

        lax.fori_loop(0, row_count, one, 0)

    def arrive(rel, h, j):
        chip = p ^ (rel + 1)
        here = all_ref.at[rows_of(chip, c, j), cols_of(h)]
        remote(here, here, own_s.at[0], agr.at[rel, h, j], rows=r).wait_recv()
        remote(here, here, part_s.at[rel], pr.at[rel], rows=r ^ 1).start()

    def forward(rel, h, j, send):
        chip = p ^ (rel + 1)
        here = all_ref.at[rows_of(chip, c, j), cols_of(h)]
        ag(2 - rel, h, j, here, chip, 2, send)

    def gather_event(s):
        a, j = s // nch, s % nch

        @pl.when(a == 0)
        def _():
            arrive(0, 0, j)

            @pl.when(relays)
            def _():
                forward(0, 0, j, relay_s.at[0])
            arrive(1, 1, j)

            @pl.when(relays)
            def _():
                forward(1, 1, j, relay_s.at[1])

        @pl.when(a == 1)
        def _():
            arrive(0, 1, j)

            @pl.when(relays_all)
            def _():
                forward(0, 1, j, extra_s.at[0])
            arrive(1, 0, j)

            @pl.when(relays_all)
            def _():
                forward(1, 0, j, extra_s.at[1])

    def corner_event(j):
        arrive(2, 0, j)
        arrive(2, 1, j)

    def source_event(s):
        q, j = 1 + s // nch, s % nch
        for h in range(2):
            @pl.when(has_down)
            def _():
                where = rows_of(pick(p, q, 0), c, j)
                remote(
                    all_ref.at[where, cols_of(h)], col_ref.at[where],
                    src_s.at[0, q], br.at[q, c, j], rows=2 * p + h, feat=z - 1,
                ).start()

            @pl.when(has_up)
            def _():
                where = rows_of(pick(p, q, last), c, j)
                remote(
                    all_ref.at[where, cols_of(h)], col_ref.at[where],
                    src_s.at[1, q], br.at[q, c, j], rows=2 * p + h, feat=z + 1,
                ).start()

    def column_event(s):
        q, j = s // nch, s % nch
        down = p > z
        chip = pick(p, q, jnp.where(down, 0, last))
        for k in range(2):
            here = col_ref.at[rows_of(chip, k, j)]
            remote(here, here, bf_s.at[q], br.at[q, k, j], rows=r).wait_recv()

            @pl.when((down & has_down) | (~down & has_up))
            def _():
                remote(
                    here, here, bf_s.at[q], br.at[q, k, j],
                    feat=jnp.where(down, z - 1, z + 1),
                ).start()

    def pass_event(s):
        q, j = s // nch, s % nch
        down = p == 0
        block = jnp.where(down, z + 1 + q, z - 1 - q)
        slot = jnp.where(down, block - 1, block)

        @pl.when((block >= 0) & (block <= last))
        def _():
            for k in range(2):
                here = abuf.at[slot, k, own_rows(j)]
                remote(here, here, af_s.at[q], ar.at[q, k, j], rows=r).wait_recv()

                @pl.when((down & has_down) | (~down & has_up))
                def _():
                    remote(
                        here, here, af_s.at[q], ar.at[q + 1, k, j],
                        feat=jnp.where(down, z - 1, z + 1),
                    ).start()

    def deliver_event(s):
        q, j = s // nch, s % nch
        down = p == 0
        block = jnp.where(down, z + 1 + q, z - 1 - q)
        slot = jnp.where(down, block - 1, block)

        @pl.when((block >= 0) & (block <= last))
        def _():
            for k in range(2):
                remote(
                    abuf.at[slot, k, own_rows(j)], col_ref.at[rows_of(p, k, j)],
                    ad_s.at[q], adr.at[j // (nch // 3)], rows=2 * block + c,
                ).start()

    items = last
    lag = nch // 2 + 3
    tiles = width // TILE
    edge = passed_chip(p, z, last)
    twice = col_ref.at[pl.ds(0, 2 * n)]
    third = n // 3
    once = col_ref.at[pl.ds(0, 2 * third)]
    q = nch // 3
    begins = [3 * q, 4 * q + 1, 5 * q + 1, 6 * q, 7 * q, 8 * q]
    ends = [4 * q, 5 * q + 1, 6 * q, 7 * q, 8 * q, 9 * q]
    near, far = pick(p, 1, edge), pick(p, 2, edge)

    def partner_rows(chip):
        rel = jnp.where(chip == p, 3, (p ^ chip) - 1)
        there = all_ref.at[pl.ds(pl.multiple_of((2 * chip + 1 - c) * n, n), n)]
        remote(there, there, part_s.at[rel], pr.at[rel], rows=r).wait_recv()

        @pl.when(p == z)
        def _():
            rows = pl.ds(pl.multiple_of(chip * 2 * n, n), 2 * n)
            copy = pltpu.make_async_copy(
                all_ref.at[rows, cols_of(c)], col_ref.at[rows], lsem.at[2]
            )
            copy.start()
            copy.wait()

    def prepare(i):
        rows = pl.ds(pl.multiple_of(i * TILE, TILE), TILE)
        h_ref[rows, :] = jnp.zeros((TILE, half), jnp.float32)
        offset = i * TILE - c * half

        @pl.when((p == z) & (offset >= 0) & (offset < half))
        def _():
            cols = pl.ds(pl.multiple_of(offset, TILE), TILE)
            shape = (TILE, TILE)
            same = lax.broadcasted_iota(jnp.int32, shape, 0) == lax.broadcasted_iota(
                jnp.int32, shape, 1
            )
            h_ref[rows, cols] = jnp.where(
                same, jnp.broadcast_to(prec_ref[:, rows], shape), 0.0
            )

    def unit_rows(index):
        def start(chip, core, piece):
            return (chip * 2 + core) * n + piece * third

        late = jnp.where(index == 2, 2, index - 4 + (index == 3))
        rows = []
        for i in range(4):
            core, upper = i % 2, i // 2
            pair = jnp.where(
                index == 0, start(p, core, upper),
                jnp.where(
                    index == 1, start(near if upper else p, core, 0 if upper else 2),
                    start(near, core, 1 + upper),
                ),
            )
            far_rows = start(edge if upper else far, core, late)
            rows.append(jnp.where((index == 0) | (index == 1) | (index == 3), pair, far_rows))
        return rows

    def part_of(i):
        return pl.ds(pl.multiple_of(i * PART, PART), PART)

    def turn(rows, i, flag):
        weighted, pulled = weigh(all_ref, wr_ref, rows, third, part_of(i))
        gacc_ref[:, part_of(i)] += pulled * flag
        return weighted

    def multiply(turned, rows, i):
        value = turned[...]
        for t in range(half // TILE):
            there = pl.ds(t * TILE, TILE)
            h_ref[part_of(i), there] += jnp.dot(
                value, slabs(col_ref, None, rows, third, there),
                preferred_element_type=jnp.float32,
            )

    def compute(u):
        index = sum((u >= s).astype(jnp.int32) for s in begins) - 1

        def choose(values):
            out = values[0]
            for i in range(1, len(values)):
                out = jnp.where(index >= i, values[i], out)
            return out

        begin, span = choose(begins), choose([e - s for s, e in zip(begins, ends)])
        low = jnp.minimum((u - begin) * tiles // span, tiles)
        high = jnp.minimum((u - begin + 1) * tiles // span, tiles)
        rows = unit_rows(index)

        @pl.when(u == begin)
        def _():
            @pl.when(index == 0)
            def _():
                weights()
                partner_rows(p)

            @pl.when(index == 1)
            def _():
                partner_rows(near)

            @pl.when(index == 2)
            def _():
                partner_rows(far)
                partner_rows(edge)

            @pl.when((index >= 4) & (p != z))
            def _():
                remote(once, once, bf_s.at[0], adr.at[index - 4], rows=r).wait_recv()

            @pl.when(index != 2)
            def _():
                even[...] = turn(rows, 0, 1.0)

        def keep(i, _):
            for e in range(2):
                kept[part_of(2 * i + e), :] = turn(rows, 2 * i + e, 1.0)
            return 0

        def pair(i, _):
            multiply(even, rows, 2 * i)
            odd[...] = turn(rows, 2 * i + 1, 1.0)
            multiply(odd, rows, 2 * i + 1)
            more = i < tiles - 1
            even[...] = turn(
                rows, jnp.where(more, 2 * i + 2, 0), jnp.where(more, 1.0, 0.0)
            )
            return 0

        @pl.when(index == 2)
        def _():
            lax.fori_loop(low, high, keep, 0)

            @pl.when(u == ends[2] - 1)
            def _():
                pltpu.make_async_copy(kept, turned_out, lsem.at[3]).start()

        @pl.when(index != 2)
        def _():
            lax.fori_loop(low, high, pair, 0)

    def some(event, low, high):
        def one(i, _):
            event(i)
            return 0
        lax.fori_loop(low, high, one, 0)

    def step(u, _):
        @pl.when(u < begins[0])
        def _():
            per = -(-tiles // begins[0])
            some(prepare, jnp.minimum(u * per, tiles), jnp.minimum(u * per + per, tiles))

        @pl.when((u >= begins[0]) & (u < ends[-1]))
        def _():
            compute(u)

        @pl.when((p != z) & (u < items * nch))
        def _():
            column_event(u)

        @pl.when(u == 2)
        def _():
            share_stats()

        @pl.when(u < 2)
        def _():
            some(lambda j: own_sends(j, 0), 1 + AHEAD * u, 1 + AHEAD * (u + 1))

        @pl.when(u >= 2)
        def _():
            low = 1 + 2 * AHEAD + 3 * (u - 2)
            some(
                lambda j: own_sends(j, 0), jnp.minimum(low, nch), jnp.minimum(low + 3, nch)
            )

        @pl.when((u >= 3) & (u < 3 + nch))
        def _():
            some(gather_event, 2 * u - 6, 2 * u - 4)

        corner = 4 * q + 1

        @pl.when((u >= corner) & (u < corner + q))
        def _():
            some(corner_event, 3 * (u - corner), 3 * (u - corner) + 3)

        @pl.when((p == z) & (u >= lag) & (u < lag + 2 * nch))
        def _():
            source_event(u - lag)

        @pl.when(((p == 0) | (p == last)) & (u >= LATE) & (u < LATE + items * nch))
        def _():
            pass_event(u - LATE)

        @pl.when(((p == 0) | (p == last)) & (u >= nch))
        def _():
            low = jnp.minimum(2 * (u - nch), u - LATE)
            some(deliver_event, low, jnp.minimum(2 * (u + 1 - nch), u + 1 - LATE))

        return 0

    lax.fori_loop(0, items * nch + LATE, step, 0)

    @pl.when(p != z)
    def _():
        remote(once, once, bf_s.at[0], adr.at[2], rows=r).wait_recv()

    outs = [pltpu.make_async_copy(gacc_ref, pull_out, lsem.at[4])]
    for i, start in enumerate(unit_rows(jnp.int32(2))):
        outs.append(pltpu.make_async_copy(
            col_ref.at[pl.ds(pl.multiple_of(start, CHUNK), third)],
            cols_out.at[pl.ds(i * third, third)], lsem.at[5 + i],
        ))
    for copy in outs:
        copy.start()

    def sent(ref, sem):
        remote(ref, ref, sem, pr.at[3], rows=r).wait_send()

    for d in range(1, feat_count):
        sent(st_ref, ss.at[d])
    for d in range(1, row_count):
        sent(stat_ref.at[r], ts.at[d])
    for i in range(2):
        sent(x_ref, own_s.at[i])

        @pl.when(relays)
        def _():
            sent(x_ref.at[:, pl.ds(0, half)], relay_s.at[i])

        @pl.when(relays_all)
        def _():
            sent(x_ref.at[:, pl.ds(0, half)], extra_s.at[i])

    @pl.when(has_down & ((p == 0) | (p == z)))
    def _():
        sent(x_ref, own_s.at[2])

    @pl.when(has_up & ((p == last) | (p == z)))
    def _():
        sent(x_ref, own_s.at[3])
    for rel in range(4):
        sent(x_ref, part_s.at[rel])
    down = p > z
    for q in range(items):
        if q > 0:
            @pl.when((p == z) & has_down)
            def _():
                sent(x_ref, src_s.at[0, q])

            @pl.when((p == z) & has_up)
            def _():
                sent(x_ref, src_s.at[1, q])

        @pl.when((p != z) & ((down & has_down) | (~down & has_up)))
        def _():
            sent(twice, bf_s.at[q])
        for edge, block, more in ((0, z + 1 + q, has_down), (last, z - 1 - q, has_up)):
            @pl.when((p == edge) & (block >= 0) & (block <= last))
            def _():
                sent(twice, ad_s.at[q])

                @pl.when(more)
                def _():
                    sent(twice, af_s.at[q])
    for copy in outs:
        copy.wait()
    pltpu.make_async_copy(kept, turned_out, lsem.at[3]).wait()


def line_stage(features, labels, post, prec):
    row_count = lax.axis_size("rows")
    feat_count = lax.axis_size("feat")
    n, width = features.shape
    half = width // 2
    items = feat_count - 1
    nch = n // CHUNK
    dma = pltpu.SemaphoreType.DMA
    return pl.pallas_call(
        functools.partial(line_kernel, row_count, feat_count),
        out_shape=(
            pltpu.VMEM((width, half), jnp.float32),
            pltpu.HBM((width, 4 * n // 3), features.dtype),
            pltpu.HBM((4 * n // 3, half), features.dtype),
            pltpu.HBM((8, width), jnp.float32),
        ),
        in_specs=[
            pl.BlockSpec(memory_space=pl.ANY), pl.BlockSpec(memory_space=pltpu.VMEM),
            pl.BlockSpec(memory_space=pltpu.VMEM), pl.BlockSpec(memory_space=pltpu.VMEM),
        ],
        out_specs=[pl.BlockSpec(memory_space=pltpu.VMEM)]
        + [pl.BlockSpec(memory_space=pl.ANY)] * 3,
        scratch_shapes=[
            pltpu.VMEM((row_count * n, width), features.dtype),
            pltpu.VMEM((row_count * n, half), features.dtype),
            pltpu.VMEM((2, row_count * n, 128), features.dtype),
            pltpu.VMEM((8, width), jnp.float32),
            pltpu.VMEM((width, 4 * n // 3), features.dtype),
            pltpu.VMEM((PART, 4 * n // 3), features.dtype),
            pltpu.VMEM((PART, 4 * n // 3), features.dtype),
            pltpu.VMEM((items, 2, n, half), features.dtype),
            pltpu.VMEM((16, 128), jnp.float32),
            pltpu.VMEM((row_count, feat_count, 16, 128), jnp.float32),
            dma((3, 2, nch)), dma((4,)), dma((items, 2, nch)), dma((items + 1, 2, nch)),
            dma((3,)),
            dma((4,)), dma((2,)), dma((2,)), dma((4,)), dma((2, items)), dma((items,)),
            dma((items,)), dma((items,)),
            dma((feat_count,)), dma((feat_count,)),
            dma((row_count,)), dma((row_count,)),
            dma((9,)),
        ],
        compiler_params=pltpu.CompilerParams(
            collective_id=0, has_side_effects=True, vmem_limit_bytes=30 * 1024 * 1024
        ),
        name="line_stage",
    )(features, labels, post, prec)


def last_kernel(
    h_ref, turned_ref, cols_ref, gacc_ref,
    out_ref, grad_ref, stage, turned, cols, gacc, grad, sem, lsem, tsem,
):
    width, half = h_ref.shape
    slots = stage.shape[0]
    count = width // PART
    load = pltpu.make_async_copy(cols_ref, cols, lsem.at[0])
    load.start()

    def part_of(i):
        return pl.ds(pl.multiple_of(i * PART, PART), PART)

    def take(i):
        return pltpu.make_async_copy(
            turned_ref.at[part_of(i)], turned.at[part_of(i)], tsem.at[i]
        )

    def put(i):
        slot = lax.rem(i, slots)
        return pltpu.make_async_copy(stage.at[slot], out_ref.at[part_of(i)], sem.at[slot])

    for i in range(count):
        take(i).start()
    late = pltpu.make_async_copy(gacc_ref, gacc, lsem.at[1])
    late.start()
    load.wait()

    def one(i, _):
        @pl.when(i >= slots)
        def _():
            put(i - slots).wait()
        take(i).wait()
        slot = lax.rem(i, slots)
        value = turned[part_of(i), :]
        for t in range(half // TILE):
            there = pl.ds(t * TILE, TILE)
            stage[slot, :, there] = h_ref[part_of(i), there] + jnp.dot(
                value, cols[:, there], preferred_element_type=jnp.float32
            )
        put(i).start()
        return 0

    lax.fori_loop(0, count, one, 0)
    late.wait()
    grad[...] = jnp.sum(gacc[...], axis=0, keepdims=True)
    give = pltpu.make_async_copy(grad, grad_ref, lsem.at[2])
    give.start()
    for i in range(max(0, count - slots), count):
        put(i).wait()
    give.wait()


def last_stage(h, turned, cols, gacc):
    width, half = h.shape
    dma = pltpu.SemaphoreType.DMA
    h = pltpu.with_memory_space_constraint(h, pltpu.VMEM)
    kept = [pltpu.with_memory_space_constraint(a, pltpu.HBM) for a in (turned, cols, gacc)]
    return pl.pallas_call(
        last_kernel,
        out_shape=(
            pltpu.HBM((width, half), jnp.float32),
            pltpu.HBM((1, width), jnp.float32),
        ),
        in_specs=[pl.BlockSpec(memory_space=pltpu.VMEM)]
        + [pl.BlockSpec(memory_space=pl.ANY)] * 3,
        out_specs=[pl.BlockSpec(memory_space=pl.ANY)] * 2,
        scratch_shapes=[
            pltpu.VMEM((3, PART, half), jnp.float32),
            pltpu.VMEM(turned.shape, turned.dtype),
            pltpu.VMEM(cols.shape, cols.dtype),
            pltpu.VMEM(gacc.shape, gacc.dtype),
            pltpu.VMEM((1, width), jnp.float32),
            dma((3,)), dma((3,)), dma((width // PART,)),
        ],
        compiler_params=pltpu.CompilerParams(vmem_limit_bytes=14 * 1024 * 1024),
        name="last_stage",
    )(h, *kept)


def paired(row_count, feat_count, n, width):
    half = width // 2
    rows = row_count * n
    held = 4 * width * half + 2 * rows * (width + half + 256) + 12 * n * half + 4 * n * width
    return (
        row_count == 2 * feat_count and (feat_count - 1).bit_length() == 2
        and feat_count & (feat_count - 1) == 0 and n % (3 * CHUNK) == 0 and n // CHUNK >= 2 * AHEAD + 1
        and n <= 1024 and half % TILE == 0 and held <= VMEM_BUDGET
    )


def by_lines(features, labels, posterior, prior_prec):
    n, width = features.shape
    held = line_stage(
        features, labels.reshape(1, n), posterior.reshape(width // 128, 128),
        prior_prec.reshape(1, width),
    )
    hessian, gradient = last_stage(*held)
    return (hessian, gradient.reshape(width))


def gather_kernel(
    row_count, feat_count, x_ref, st_ref, all_ref, col_ref, stat_ref,
    ring, zs, zr, ps, pr, ds, dr, cs, cr, cl, ss, sr, ts, tr, lsem,
):
    r = lax.axis_index("rows")
    f = lax.axis_index("feat")
    n, width = x_ref.shape
    half = width // 2
    col_width = col_ref.shape[1]
    unit = min(col_width, half)
    per_half = half // unit
    per_owner = col_width // unit
    chips = row_count // 2
    bits = chips.bit_length() - 1
    part = n // SPLIT

    def rows_of(device):
        return pl.ds(pl.multiple_of(device * n, n), n)

    def remote(src, dst, send, recv, **where):
        return pltpu.make_async_remote_copy(
            src_ref=src, dst_ref=dst, send_sem=send, recv_sem=recv,
            device_id=where, device_id_type=MESH,
        )

    sends = []

    def go(copy):
        copy.start()
        sends.append(copy)

    def ring_slice(step, h, k):
        rows, cols = pl.ds(k * part, part), pl.ds(h * half, half)
        return x_ref.at[rows, cols] if step == 0 else ring.at[step - 1, rows, cols]

    def ring_copy(step, h, k):
        to = lax.rem(f + (1 if h == 0 else feat_count - 1), feat_count)
        return remote(
            ring_slice(step, h, k),
            ring.at[step, pl.ds(k * part, part), pl.ds(h * half, half)],
            zs.at[step, h, k], zr.at[step, h, k], feat=to,
        )

    def column_sends(step, h, k, start):
        block = lax.rem(f + (feat_count - step if h == 0 else step), feat_count)
        for u in range(per_half):
            inner = h * half + u * unit
            if width % col_width == 0:
                owner = block * (width // col_width) + inner // col_width
                offset = inner % col_width
                slot = offset // unit
            else:
                owner = (block * width + inner) // col_width
                slot = ((block * width + inner) % col_width) // unit
                offset = pl.multiple_of(slot * unit, unit)
            src = ring_slice(step, h, k).at[:, pl.ds(u * unit, unit)]
            dst = col_ref.at[
                pl.ds(pl.multiple_of(r * n + k * part, part), part), pl.ds(offset, unit)
            ]
            send = cs.at[step, h, k, u]

            @pl.when(owner != r)
            def _():
                copy = remote(src, dst, send, cr.at[r, slot, k], rows=owner)
                copy.start() if start else copy.wait_send()

            if start:
                @pl.when(owner == r)
                def _():
                    pltpu.make_async_copy(src, dst, cl.at[slot, k]).start()

    def order(h):
        return list(range(bits)) if h == 0 else list(range(bits))[::-1]

    def spread(h, stage, mask):
        bit = 1 << order(h)[stage]
        origin = r ^ (2 * mask)
        cols = pl.ds(h * half, half)
        src = x_ref.at[:, cols] if mask == 0 else all_ref.at[rows_of(origin), cols]
        return remote(
            src, all_ref.at[rows_of(origin), cols],
            ps.at[h, mask | bit], pr.at[h, mask | bit], rows=r ^ (2 * bit),
        )

    def partner(h, mask):
        origin = r ^ (2 * mask)
        cols = pl.ds(h * half, half)
        src = x_ref.at[:, cols] if mask == 0 else all_ref.at[rows_of(origin), cols]
        return remote(
            src, all_ref.at[rows_of(origin), cols],
            ds.at[h, mask], dr.at[h, mask], rows=r ^ 1,
        )

    def masks_before(h, stage):
        found = [0]
        for b in order(h)[:stage]:
            found += [m | (1 << b) for m in found]
        return found

    for k in range(SPLIT):
        for h in range(2):
            go(ring_copy(0, h, k))
    stat_local = pltpu.make_async_copy(st_ref, stat_ref.at[r, f], lsem.at[0])
    stat_local.start()
    for d in range(1, feat_count):
        go(remote(
            st_ref, stat_ref.at[r, f], ss.at[d], sr.at[d],
            feat=lax.rem(f + d, feat_count),
        ))
    for stage in range(bits):
        for h in range(2):
            go(spread(h, stage, 0))
    for h in range(2):
        go(partner(h, 0))
    own = pltpu.make_async_copy(x_ref, all_ref.at[rows_of(r)], lsem.at[1])
    own.start()
    for k in range(SPLIT):
        for h in range(2):
            column_sends(0, h, k, True)

    stat_local.wait()
    for d in range(1, feat_count):
        remote(
            st_ref, stat_ref.at[r, lax.rem(f + feat_count - d, feat_count)],
            ss.at[d], sr.at[d], feat=f,
        ).wait_recv()
    for d in range(1, row_count):
        go(remote(
            stat_ref.at[r], stat_ref.at[r], ts.at[d], tr.at[d],
            rows=lax.rem(r + d, row_count),
        ))

    def relay(stage):
        for h in range(2):
            bit = 1 << order(h)[stage]
            for m in masks_before(h, stage):
                mask = m | bit
                cols = pl.ds(h * half, half)
                remote(
                    x_ref.at[:, cols], all_ref.at[rows_of(r ^ (2 * mask)), cols],
                    ps.at[h, mask], pr.at[h, mask], rows=r,
                ).wait_recv()
                for later in range(stage + 1, bits):
                    go(spread(h, later, mask))
                go(partner(h, mask))

    for step in range(1, feat_count):
        for k in range(SPLIT):
            for h in range(2):
                ring_copy(step - 1, h, k).wait_recv()
                if step < feat_count - 1:
                    go(ring_copy(step, h, k))
                column_sends(step, h, k, True)
        if step <= bits:
            relay(step - 1)
    for stage in range(feat_count - 1, bits):
        relay(stage)

    for h in range(2):
        for mask in range(chips):
            cols = pl.ds(h * half, half)
            remote(
                x_ref.at[:, cols], all_ref.at[rows_of(r ^ (2 * mask) ^ 1), cols],
                ds.at[h, mask], dr.at[h, mask], rows=r,
            ).wait_recv()
    for d in range(1, row_count):
        origin = lax.rem(r + row_count - d, row_count)
        remote(
            stat_ref.at[origin], stat_ref.at[origin], ts.at[d], tr.at[d], rows=r
        ).wait_recv()
        for slot in range(per_owner):
            for k in range(SPLIT):
                dst = col_ref.at[
                    pl.ds(pl.multiple_of(origin * n + k * part, part), part),
                    pl.ds(slot * unit, unit),
                ]
                remote(
                    x_ref.at[pl.ds(0, part), pl.ds(0, unit)], dst,
                    cs.at[0, 0, 0, 0], cr.at[origin, slot, k], rows=r,
                ).wait_recv()
    for slot in range(per_owner):
        for k in range(SPLIT):
            dst = col_ref.at[
                pl.ds(pl.multiple_of(r * n + k * part, part), part),
                pl.ds(slot * unit, unit),
            ]
            pltpu.make_async_copy(
                x_ref.at[pl.ds(0, part), pl.ds(0, unit)], dst, cl.at[slot, k]
            ).wait()
    own.wait()
    for copy in sends:
        copy.wait_send()
    for step in range(feat_count):
        for k in range(SPLIT):
            for h in range(2):
                column_sends(step, h, k, False)


def gather(features, stats):
    row_count = lax.axis_size("rows")
    feat_count = lax.axis_size("feat")
    n, width = features.shape
    half = width // 2
    col_width = width * feat_count // row_count
    unit = min(col_width, half)
    chips = row_count // 2
    dma = pltpu.SemaphoreType.DMA
    return pl.pallas_call(
        functools.partial(gather_kernel, row_count, feat_count),
        out_shape=(
            jax.ShapeDtypeStruct((row_count * n, width), features.dtype),
            jax.ShapeDtypeStruct((row_count * n, col_width), features.dtype),
            jax.ShapeDtypeStruct((row_count, feat_count) + stats.shape, stats.dtype),
        ),
        in_specs=[pl.BlockSpec(memory_space=pltpu.VMEM)] * 2,
        out_specs=[pl.BlockSpec(memory_space=pl.ANY)] * 3,
        scratch_shapes=[
            pltpu.VMEM((feat_count - 1, n, width), features.dtype),
            dma((feat_count - 1, 2, SPLIT)), dma((feat_count - 1, 2, SPLIT)),
            dma((2, chips)), dma((2, chips)),
            dma((2, chips)), dma((2, chips)),
            dma((feat_count, 2, SPLIT, half // unit)),
            dma((row_count, col_width // unit, SPLIT)),
            dma((col_width // unit, SPLIT)),
            dma((feat_count,)), dma((feat_count,)),
            dma((row_count,)), dma((row_count,)),
            dma((2,)),
        ],
        compiler_params=pltpu.CompilerParams(
            has_side_effects=True, vmem_limit_bytes=32 * 1024 * 1024
        ),
        name="gather",
    )(features, stats)


def per_device(features, labels, posterior, prior_prec):
    row_count = lax.axis_size("rows")
    feat_count = lax.axis_size("feat")
    row_index = lax.axis_index("rows")
    feat_index = lax.axis_index("feat")
    n, block_width = features.shape
    if paired(row_count, feat_count, n, block_width):
        return by_lines(features, labels, posterior, prior_prec)
    col_width = block_width * feat_count // row_count
    partial_value = jnp.dot(features, posterior, preferred_element_type=jnp.float32)
    padded = -(-n // 512) * 512
    stats = jnp.concatenate([
        jnp.pad(partial_value, (0, padded - n)),
        jnp.pad(labels.astype(jnp.float32), (0, padded - n)),
    ]).reshape(-1, 128)
    all_rows, column_rows, all_stats = gather(features, stats)
    all_stats = all_stats.reshape(row_count, feat_count, 2, padded)[..., :n]
    margins = jnp.sum(all_stats[:, :, 0], axis=1).reshape(-1)
    all_labels = all_stats[:, 0, 1].reshape(-1)
    chance = jax.nn.sigmoid(margins)
    weight = (chance * (1.0 - chance)).astype(jnp.bfloat16)
    residual = (all_labels - chance).astype(jnp.bfloat16)
    summed = jnp.dot(residual, all_rows, preferred_element_type=jnp.float32)
    gradient = summed - prior_prec * posterior.astype(jnp.float32)
    weighted = weight[:, None] * all_rows
    product = lax.dot_general(
        weighted, column_rows, (((0,), (0,)), ((), ())), preferred_element_type=jnp.float32
    )
    global_rows = feat_index * block_width + jnp.arange(block_width, dtype=jnp.int32)
    global_cols = row_index * col_width + jnp.arange(col_width, dtype=jnp.int32)
    on_diagonal = global_rows[:, None] == global_cols[None, :]
    hessian = product + jnp.where(on_diagonal, prior_prec[:, None], jnp.float32(0.0))
    return (hessian, gradient)


def solution(mesh):
    in_specs = (P("rows", "feat"), P("rows"), P("feat"), P("feat"))
    out_specs = (P("feat", "rows"), P("feat"))
    return jax.shard_map(
        per_device, mesh=mesh, in_specs=in_specs, out_specs=out_specs, check_vma=False
    )
```

```python
import functools

import jax
import jax.numpy as jnp
from jax import lax
from jax.experimental import pallas as pl
from jax.experimental.pallas import tpu as pltpu
from jax.sharding import PartitionSpec as P

MESH = pl.DeviceIdType.MESH
SPLIT = 2
CHUNK = 16
TILE = 512
PART = 256
AHEAD = 2
LATE = 4
VMEM_BUDGET = 60 * 1024 * 1024


def pick(p, q, e):
    first = jnp.where((p ^ 1) == e, p ^ 2, p ^ 1)
    second = jnp.where(((p ^ 1) == e) | ((p ^ 2) == e), p ^ 3, p ^ 2)
    return jnp.where(q == 0, p, jnp.where(q == 1, first, second))


def passed_chip(p, z, last):
    return jnp.where(p > z, 0, jnp.where(p < z, last, p ^ 3))


def slabs(ref, lead, starts, size, cols):
    parts = []
    for start in starts:
        rows = pl.ds(pl.multiple_of(start, CHUNK), size)
        parts.append(ref[rows, cols] if lead is None else ref[lead, rows, cols])
    return jnp.concatenate(parts, axis=0)


def wide(value, width):
    return jnp.concatenate([value] * (width // value.shape[1]), axis=1)


def weigh(all_ref, wr_ref, starts, size, cols):
    x = slabs(all_ref, None, starts, size, cols)
    weight = slabs(wr_ref, 0, starts, size, slice(None))
    residual = slabs(wr_ref, 1, starts, size, slice(None)).astype(jnp.float32)
    pulled = x.astype(jnp.float32) * wide(residual, PART)
    pulled = jnp.sum(pulled.reshape(-1, 8, PART), axis=0)
    return (x * wide(weight, PART)).T, pulled


def line_kernel(
    row_count, feat_count, x_ref, label_ref, post_ref, prec_ref,
    h_ref, turned_out, pull_out,
    all_ref, col_ref, wr_ref, gacc_ref, kept, even, odd, abuf, st_ref, stat_ref,
    agr, pr, br, ar, adr, own_s, relay_s, extra_s, part_s, src_s, bf_s, af_s, ad_s,
    ss, sr, ts, tr, lsem,
):
    r = lax.axis_index("rows")
    z = lax.axis_index("feat")
    p, c = r // 2, r % 2
    last = feat_count - 1
    n, width = x_ref.shape
    half = width // 2
    m = CHUNK
    nch = n // m
    avoid = jnp.where(z == 0, 0, jnp.where(z == last, last, -8))
    relays = p != avoid
    relays_all = (p ^ last) == avoid
    has_down, has_up = z >= 1, z <= last - 1

    def rows_of(chip, core, j):
        return pl.ds(pl.multiple_of((chip * 2 + core) * n + j * m, m), m)

    def own_rows(j):
        return pl.ds(pl.multiple_of(j * m, m), m)

    def cols_of(h):
        return pl.ds(pl.multiple_of(h * half, half), half)

    def remote(src, dst, send, recv, **where):
        return pltpu.make_async_remote_copy(
            src_ref=src, dst_ref=dst, send_sem=send, recv_sem=recv,
            device_id=where, device_id_type=MESH,
        )

    barrier = pltpu.get_barrier_semaphore()
    for d in range(1, row_count):
        pl.semaphore_signal(
            barrier, inc=1, device_id={"rows": lax.rem(r + d, row_count)},
            device_id_type=MESH,
        )
    for d in range(1, feat_count):
        for other in (r, r ^ 1):
            pl.semaphore_signal(
                barrier, inc=1,
                device_id={"rows": other, "feat": lax.rem(z + d, feat_count)},
                device_id_type=MESH,
            )

    own = pltpu.make_async_copy(
        x_ref, all_ref.at[pl.ds(pl.multiple_of(r * n, n), n)], lsem.at[1]
    )
    own.start()
    own.wait()
    st_ref[...] = jnp.zeros_like(st_ref)
    post = post_ref[...].astype(jnp.float32)
    for t in range(-(-n // 128)):
        count = min(128, n - 128 * t)
        here = pl.ds(128 * t, count)
        st_ref[8 + t:9 + t, 0:count] = label_ref[:, here].astype(jnp.float32)
        rows = pl.ds(pl.multiple_of(r * n + 128 * t, CHUNK), count)

        total = jnp.zeros((count, 128), jnp.float32)
        for i in range(width // 128):
            value = all_ref[rows, pl.ds(128 * i, 128)].astype(jnp.float32)
            total = total + value * post[i:i + 1, :]
        st_ref[t:t + 1, 0:count] = jnp.sum(total.T, axis=0, keepdims=True)
    gacc_ref[...] = jnp.zeros_like(gacc_ref)
    for t in range(width // 128):
        lanes = pl.ds(128 * t, 128)
        gacc_ref[0:1, lanes] = -prec_ref[:, lanes] * post[t:t + 1, :]
    pl.semaphore_wait(barrier, row_count - 1 + 2 * (feat_count - 1))

    def ag(dim, h, j, src, chip, rel, send):
        remote(
            src, all_ref.at[rows_of(chip, c, j), cols_of(h)],
            send, agr.at[rel, h, j], rows=r ^ (2 * dim),
        ).start()

    def own_plane(s):
        j = lax.rem(s, nch)

        @pl.when(s < nch)
        def _():
            ag(1, 0, j, x_ref.at[own_rows(j), cols_of(0)], p, 0, own_s.at[0])
            ag(2, 1, j, x_ref.at[own_rows(j), cols_of(1)], p, 1, own_s.at[1])

        @pl.when(s >= nch)
        def _():
            ag(1, 1, j, x_ref.at[own_rows(j), cols_of(1)], p, 0, own_s.at[0])
            ag(2, 0, j, x_ref.at[own_rows(j), cols_of(0)], p, 1, own_s.at[1])

    def own_line(j):
        for h in range(2):
            src = x_ref.at[own_rows(j), cols_of(h)]

            @pl.when(has_down & (p == 0))
            def _():
                remote(
                    src, abuf.at[z - 1, c, own_rows(j)], own_s.at[2], ar.at[0, c, j],
                    rows=2 * p + h, feat=z - 1,
                ).start()

            @pl.when(has_down & (p == z))
            def _():
                remote(
                    src, col_ref.at[rows_of(p, c, j)], own_s.at[2], br.at[0, c, j],
                    rows=2 * p + h, feat=z - 1,
                ).start()

            @pl.when(has_up & (p == last))
            def _():
                remote(
                    src, abuf.at[z, c, own_rows(j)], own_s.at[3], ar.at[0, c, j],
                    rows=2 * p + h, feat=z + 1,
                ).start()

            @pl.when(has_up & (p == z))
            def _():
                remote(
                    src, col_ref.at[rows_of(p, c, j)], own_s.at[3], br.at[0, c, j],
                    rows=2 * p + h, feat=z + 1,
                ).start()

    def own_sends(j, _):
        own_line(j)
        own_plane(2 * j)
        own_plane(2 * j + 1)
        return 0

    own_sends(0, 0)
    remote(
        x_ref, all_ref.at[pl.ds(pl.multiple_of(r * n, n), n)], part_s.at[3], pr.at[3],
        rows=r ^ 1,
    ).start()

    stat_local = pltpu.make_async_copy(st_ref, stat_ref.at[r, z], lsem.at[0])
    stat_local.start()
    for d in range(1, feat_count):
        remote(
            st_ref, stat_ref.at[r, z], ss.at[d], sr.at[d],
            feat=lax.rem(z + d, feat_count),
        ).start()

    def share_stats():
        stat_local.wait()
        for d in range(1, feat_count):
            remote(
                st_ref, stat_ref.at[r, lax.rem(z + feat_count - d, feat_count)],
                ss.at[d], sr.at[d], feat=z,
            ).wait_recv()
        for d in range(1, row_count):
            remote(
                stat_ref.at[r], stat_ref.at[r], ts.at[d], tr.at[d],
                rows=lax.rem(r + d, row_count),
            ).start()

    def weights():
        for d in range(1, row_count):
            origin = lax.rem(r + row_count - d, row_count)
            remote(
                stat_ref.at[origin], stat_ref.at[origin], ts.at[d], tr.at[d], rows=r
            ).wait_recv()

        def one(i, _):
            margins = stat_ref[i, 0, 0:8]
            for f in range(1, feat_count):
                margins = margins + stat_ref[i, f, 0:8]
            chance = 1.0 / (1.0 + jnp.exp(-margins))
            weight = (chance * (1.0 - chance)).astype(jnp.bfloat16)
            residual = (stat_ref[i, 0, 8:16] - chance).astype(jnp.bfloat16)
            for lead, value in ((0, weight), (1, residual)):
                turned = value.astype(jnp.float32).T
                for t in range(-(-n // 128)):
                    count = min(128, n - 128 * t)
                    rows = pl.ds(pl.multiple_of(i * n + 128 * t, CHUNK), count)
                    wr_ref[lead, rows, :] = jnp.broadcast_to(
                        turned[:count, t:t + 1], (count, 128)
                    ).astype(jnp.bfloat16)
            return 0

        lax.fori_loop(0, row_count, one, 0)

    def arrive(rel, h, j):
        chip = p ^ (rel + 1)
        here = all_ref.at[rows_of(chip, c, j), cols_of(h)]
        remote(here, here, own_s.at[0], agr.at[rel, h, j], rows=r).wait_recv()
        remote(here, here, part_s.at[rel], pr.at[rel], rows=r ^ 1).start()

    def forward(rel, h, j, send):
        chip = p ^ (rel + 1)
        here = all_ref.at[rows_of(chip, c, j), cols_of(h)]
        ag(2 - rel, h, j, here, chip, 2, send)

    def gather_event(s):
        a, j = s // nch, s % nch

        @pl.when(a == 0)
        def _():
            arrive(0, 0, j)

            @pl.when(relays)
            def _():
                forward(0, 0, j, relay_s.at[0])
            arrive(1, 1, j)

            @pl.when(relays)
            def _():
                forward(1, 1, j, relay_s.at[1])

        @pl.when(a == 1)
        def _():
            arrive(0, 1, j)

            @pl.when(relays_all)
            def _():
                forward(0, 1, j, extra_s.at[0])
            arrive(1, 0, j)

            @pl.when(relays_all)
            def _():
                forward(1, 0, j, extra_s.at[1])

    def corner_event(j):
        arrive(2, 0, j)
        arrive(2, 1, j)

    def source_event(s):
        q, j = 1 + s // nch, s % nch
        for h in range(2):
            @pl.when(has_down)
            def _():
                where = rows_of(pick(p, q, 0), c, j)
                remote(
                    all_ref.at[where, cols_of(h)], col_ref.at[where],
                    src_s.at[0, q], br.at[q, c, j], rows=2 * p + h, feat=z - 1,
                ).start()

            @pl.when(has_up)
            def _():
                where = rows_of(pick(p, q, last), c, j)
                remote(
                    all_ref.at[where, cols_of(h)], col_ref.at[where],
                    src_s.at[1, q], br.at[q, c, j], rows=2 * p + h, feat=z + 1,
                ).start()

    def column_event(s):
        q, j = s // nch, s % nch
        down = p > z
        chip = pick(p, q, jnp.where(down, 0, last))
        for k in range(2):
            here = col_ref.at[rows_of(chip, k, j)]
            remote(here, here, bf_s.at[q], br.at[q, k, j], rows=r).wait_recv()

            @pl.when((down & has_down) | (~down & has_up))
            def _():
                remote(
                    here, here, bf_s.at[q], br.at[q, k, j],
                    feat=jnp.where(down, z - 1, z + 1),
                ).start()

    def pass_event(s):
        q, j = s // nch, s % nch
        down = p == 0
        block = jnp.where(down, z + 1 + q, z - 1 - q)
        slot = jnp.where(down, block - 1, block)

        @pl.when((block >= 0) & (block <= last))
        def _():
            for k in range(2):
                here = abuf.at[slot, k, own_rows(j)]
                remote(here, here, af_s.at[q], ar.at[q, k, j], rows=r).wait_recv()

                @pl.when((down & has_down) | (~down & has_up))
                def _():
                    remote(
                        here, here, af_s.at[q], ar.at[q + 1, k, j],
                        feat=jnp.where(down, z - 1, z + 1),
                    ).start()

    def deliver_event(s):
        q, j = s // nch, s % nch
        down = p == 0
        block = jnp.where(down, z + 1 + q, z - 1 - q)
        slot = jnp.where(down, block - 1, block)

        @pl.when((block >= 0) & (block <= last))
        def _():
            for k in range(2):
                remote(
                    abuf.at[slot, k, own_rows(j)], col_ref.at[rows_of(p, k, j)],
                    ad_s.at[q], adr.at[j // (nch // 3)], rows=2 * block + c,
                ).start()

    items = last
    lag = nch // 2 + 3
    tiles = width // TILE
    edge = passed_chip(p, z, last)
    twice = col_ref.at[pl.ds(0, 2 * n)]
    third = n // 3
    once = col_ref.at[pl.ds(0, 2 * third)]
    q = nch // 3
    begins = [2 * q + 1, 4 * q + 1, 5 * q + 1, 6 * q, 7 * q, 8 * q]
    ends = [4 * q - 1, 5 * q + 1, 6 * q, 7 * q, 8 * q, 9 * q]
    near, far = pick(p, 1, edge), pick(p, 2, edge)

    def partner_rows(chip):
        rel = jnp.where(chip == p, 3, (p ^ chip) - 1)
        there = all_ref.at[pl.ds(pl.multiple_of((2 * chip + 1 - c) * n, n), n)]
        remote(there, there, part_s.at[rel], pr.at[rel], rows=r).wait_recv()

        @pl.when(p == z)
        def _():
            rows = pl.ds(pl.multiple_of(chip * 2 * n, n), 2 * n)
            copy = pltpu.make_async_copy(
                all_ref.at[rows, cols_of(c)], col_ref.at[rows], lsem.at[2]
            )
            copy.start()
            copy.wait()

    def prepare(i):
        rows = pl.ds(pl.multiple_of(i * TILE, TILE), TILE)
        h_ref[rows, :] = jnp.zeros((TILE, half), jnp.float32)
        offset = i * TILE - c * half

        @pl.when((p == z) & (offset >= 0) & (offset < half))
        def _():
            cols = pl.ds(pl.multiple_of(offset, TILE), TILE)
            shape = (TILE, TILE)
            same = lax.broadcasted_iota(jnp.int32, shape, 0) == lax.broadcasted_iota(
                jnp.int32, shape, 1
            )
            h_ref[rows, cols] = jnp.where(
                same, jnp.broadcast_to(prec_ref[:, rows], shape), 0.0
            )

    def unit_rows(index):
        def start(chip, core, piece):
            return (chip * 2 + core) * n + piece * third

        late = jnp.where(index == 2, 2, index - 4 + (index == 3))
        rows = []
        for i in range(4):
            core, upper = i % 2, i // 2
            pair = jnp.where(
                index == 0, start(p, core, upper),
                jnp.where(
                    index == 1, start(near if upper else p, core, 0 if upper else 2),
                    start(near, core, 1 + upper),
                ),
            )
            far_rows = start(edge if upper else far, core, late)
            rows.append(jnp.where((index == 0) | (index == 1) | (index == 3), pair, far_rows))
        return rows

    def part_of(i):
        return pl.ds(pl.multiple_of(i * PART, PART), PART)

    def turn(rows, i, flag):
        weighted, pulled = weigh(all_ref, wr_ref, rows, third, part_of(i))
        gacc_ref[:, part_of(i)] += pulled * flag
        return weighted

    def multiply(turned, rows, i):
        value = turned[...]
        for t in range(half // TILE):
            there = pl.ds(t * TILE, TILE)
            h_ref[part_of(i), there] += jnp.dot(
                value, slabs(col_ref, None, rows, third, there),
                preferred_element_type=jnp.float32,
            )

    def compute(u):
        index = sum((u >= s).astype(jnp.int32) for s in begins) - 1

        def choose(values):
            out = values[0]
            for i in range(1, len(values)):
                out = jnp.where(index >= i, values[i], out)
            return out

        begin, span = choose(begins), choose([e - s for s, e in zip(begins, ends)])
        low = jnp.minimum((u - begin) * tiles // span, tiles)
        high = jnp.minimum((u - begin + 1) * tiles // span, tiles)
        rows = unit_rows(index)

        @pl.when(u == begin)
        def _():
            @pl.when(index == 0)
            def _():
                weights()
                partner_rows(p)

            @pl.when(index == 1)
            def _():
                partner_rows(near)

            @pl.when(index == 2)
            def _():
                partner_rows(far)
                partner_rows(edge)

            @pl.when((index >= 4) & (p != z))
            def _():
                remote(once, once, bf_s.at[0], adr.at[index - 4], rows=r).wait_recv()

            @pl.when(index != 2)
            def _():
                even[...] = turn(rows, 0, 1.0)

        def keep(i, _):
            for e in range(2):
                kept[part_of(2 * i + e), :] = turn(rows, 2 * i + e, 1.0)
            return 0

        def pair(i, _):
            multiply(even, rows, 2 * i)
            odd[...] = turn(rows, 2 * i + 1, 1.0)
            multiply(odd, rows, 2 * i + 1)
            more = i < tiles - 1
            even[...] = turn(
                rows, jnp.where(more, 2 * i + 2, 0), jnp.where(more, 1.0, 0.0)
            )
            return 0

        @pl.when(index == 2)
        def _():
            lax.fori_loop(low, high, keep, 0)

            @pl.when(u == ends[2] - 1)
            def _():
                pltpu.make_async_copy(kept, turned_out, lsem.at[3]).start()

        @pl.when(index != 2)
        def _():
            lax.fori_loop(low, high, pair, 0)

    def some(event, low, high):
        def one(i, _):
            event(i)
            return 0
        lax.fori_loop(low, high, one, 0)

    def step(u, _):
        @pl.when(u < begins[0])
        def _():
            per = -(-tiles // begins[0])
            some(prepare, jnp.minimum(u * per, tiles), jnp.minimum(u * per + per, tiles))

        @pl.when((u >= begins[0]) & (u < ends[-1]))
        def _():
            compute(u)

        @pl.when((p != z) & (u < items * nch))
        def _():
            column_event(u)

        @pl.when(u == 2)
        def _():
            share_stats()

        @pl.when(u < 2)
        def _():
            some(lambda j: own_sends(j, 0), 1 + AHEAD * u, 1 + AHEAD * (u + 1))

        @pl.when(u >= 2)
        def _():
            low = 1 + 2 * AHEAD + 3 * (u - 2)
            some(
                lambda j: own_sends(j, 0), jnp.minimum(low, nch), jnp.minimum(low + 3, nch)
            )

        @pl.when((u >= 3) & (u < 3 + nch))
        def _():
            some(gather_event, 2 * u - 6, 2 * u - 4)

        corner = 4 * q + 1

        @pl.when((u >= corner) & (u < corner + q))
        def _():
            some(corner_event, 3 * (u - corner), 3 * (u - corner) + 3)

        @pl.when((p == z) & (u >= lag) & (u < lag + 2 * nch))
        def _():
            source_event(u - lag)

        @pl.when(((p == 0) | (p == last)) & (u >= LATE) & (u < LATE + items * nch))
        def _():
            pass_event(u - LATE)

        @pl.when(((p == 0) | (p == last)) & (u >= nch))
        def _():
            low = jnp.minimum(2 * (u - nch), u - LATE)
            some(deliver_event, low, jnp.minimum(2 * (u + 1 - nch), u + 1 - LATE))
        return 0

    lax.fori_loop(0, items * nch + LATE, step, 0)

    @pl.when(p != z)
    def _():
        remote(once, once, bf_s.at[0], adr.at[2], rows=r).wait_recv()

    outs = [pltpu.make_async_copy(gacc_ref, pull_out, lsem.at[4])]
    for copy in outs:
        copy.start()
    for i, start in enumerate(unit_rows(jnp.int32(2))):
        held = col_ref[pl.ds(pl.multiple_of(start, CHUNK), third), :]
        h_ref[pl.ds(width + i * third, third), :] = held.astype(jnp.float32)

    def sent(ref, sem):
        remote(ref, ref, sem, pr.at[3], rows=r).wait_send()

    for d in range(1, feat_count):
        sent(st_ref, ss.at[d])
    for d in range(1, row_count):
        sent(stat_ref.at[r], ts.at[d])
    for i in range(2):
        sent(x_ref, own_s.at[i])

        @pl.when(relays)
        def _():
            sent(x_ref.at[:, pl.ds(0, half)], relay_s.at[i])

        @pl.when(relays_all)
        def _():
            sent(x_ref.at[:, pl.ds(0, half)], extra_s.at[i])

    @pl.when(has_down & ((p == 0) | (p == z)))
    def _():
        sent(x_ref, own_s.at[2])

    @pl.when(has_up & ((p == last) | (p == z)))
    def _():
        sent(x_ref, own_s.at[3])
    for rel in range(4):
        sent(x_ref, part_s.at[rel])
    down = p > z
    for q in range(items):
        if q > 0:
            @pl.when((p == z) & has_down)
            def _():
                sent(x_ref, src_s.at[0, q])

            @pl.when((p == z) & has_up)
            def _():
                sent(x_ref, src_s.at[1, q])

        @pl.when((p != z) & ((down & has_down) | (~down & has_up)))
        def _():
            sent(twice, bf_s.at[q])
        for edge, block, more in ((0, z + 1 + q, has_down), (last, z - 1 - q, has_up)):
            @pl.when((p == edge) & (block >= 0) & (block <= last))
            def _():
                sent(twice, ad_s.at[q])

                @pl.when(more)
                def _():
                    sent(twice, af_s.at[q])
    for copy in outs:
        copy.wait()
    pltpu.make_async_copy(kept, turned_out, lsem.at[3]).wait()


def line_stage(features, labels, post, prec):
    row_count = lax.axis_size("rows")
    feat_count = lax.axis_size("feat")
    n, width = features.shape
    half = width // 2
    items = feat_count - 1
    nch = n // CHUNK
    dma = pltpu.SemaphoreType.DMA
    return pl.pallas_call(
        functools.partial(line_kernel, row_count, feat_count),
        out_shape=(
            pltpu.VMEM((width + 4 * n // 3, half), jnp.float32),
            pltpu.HBM((width, 4 * n // 3), features.dtype),
            pltpu.HBM((8, width), jnp.float32),
        ),
        in_specs=[
            pl.BlockSpec(memory_space=pl.ANY), pl.BlockSpec(memory_space=pltpu.VMEM),
            pl.BlockSpec(memory_space=pltpu.VMEM), pl.BlockSpec(memory_space=pltpu.VMEM),
        ],
        out_specs=[pl.BlockSpec(memory_space=pltpu.VMEM)]
        + [pl.BlockSpec(memory_space=pl.ANY)] * 2,
        scratch_shapes=[
            pltpu.VMEM((row_count * n, width), features.dtype),
            pltpu.VMEM((row_count * n, half), features.dtype),
            pltpu.VMEM((2, row_count * n, 128), features.dtype),
            pltpu.VMEM((8, width), jnp.float32),
            pltpu.VMEM((width, 4 * n // 3), features.dtype),
            pltpu.VMEM((PART, 4 * n // 3), features.dtype),
            pltpu.VMEM((PART, 4 * n // 3), features.dtype),
            pltpu.VMEM((items, 2, n, half), features.dtype),
            pltpu.VMEM((16, 128), jnp.float32),
            pltpu.VMEM((row_count, feat_count, 16, 128), jnp.float32),
            dma((3, 2, nch)), dma((4,)), dma((items, 2, nch)), dma((items + 1, 2, nch)),
            dma((3,)),
            dma((4,)), dma((2,)), dma((2,)), dma((4,)), dma((2, items)), dma((items,)),
            dma((items,)), dma((items,)),
            dma((feat_count,)), dma((feat_count,)),
            dma((row_count,)), dma((row_count,)),
            dma((9,)),
        ],
        compiler_params=pltpu.CompilerParams(
            collective_id=0, has_side_effects=True, vmem_limit_bytes=28 * 1024 * 1024
        ),
        name="line_stage",
    )(features, labels, post, prec)


def last_kernel(
    h_ref, turned_ref, gacc_ref,
    out_ref, grad_ref, stage, turned, cols, gacc, grad, sem, lsem, tsem,
):
    width, half = out_ref.shape
    slots = stage.shape[0]
    count = width // PART

    def part_of(i):
        return pl.ds(pl.multiple_of(i * PART, PART), PART)

    def take(i):
        return pltpu.make_async_copy(
            turned_ref.at[part_of(i)], turned.at[part_of(i)], tsem.at[i]
        )

    def put(i):
        slot = lax.rem(i, slots)
        return pltpu.make_async_copy(stage.at[slot], out_ref.at[part_of(i)], sem.at[slot])

    for i in range(count):
        take(i).start()
    late = pltpu.make_async_copy(gacc_ref, gacc, lsem.at[1])
    late.start()
    cols[...] = h_ref[pl.ds(width, cols.shape[0]), :].astype(cols.dtype)

    def one(i, _):
        @pl.when(i >= slots)
        def _():
            put(i - slots).wait()
        take(i).wait()
        slot = lax.rem(i, slots)
        value = turned[part_of(i), :]
        for t in range(half // TILE):
            there = pl.ds(t * TILE, TILE)
            stage[slot, :, there] = h_ref[part_of(i), there] + jnp.dot(
                value, cols[:, there], preferred_element_type=jnp.float32
            )
        put(i).start()
        return 0

    lax.fori_loop(0, count, one, 0)
    late.wait()
    grad[...] = jnp.sum(gacc[...], axis=0, keepdims=True)
    give = pltpu.make_async_copy(grad, grad_ref, lsem.at[2])
    give.start()
    for i in range(max(0, count - slots), count):
        put(i).wait()
    give.wait()


def last_stage(h, turned, gacc):
    width, half = turned.shape[0], h.shape[1]
    dma = pltpu.SemaphoreType.DMA
    h = pltpu.with_memory_space_constraint(h, pltpu.VMEM)
    kept = [pltpu.with_memory_space_constraint(a, pltpu.HBM) for a in (turned, gacc)]
    return pl.pallas_call(
        last_kernel,
        out_shape=(
            pltpu.HBM((width, half), jnp.float32),
            pltpu.HBM((1, width), jnp.float32),
        ),
        in_specs=[pl.BlockSpec(memory_space=pltpu.VMEM)]
        + [pl.BlockSpec(memory_space=pl.ANY)] * 2,
        out_specs=[pl.BlockSpec(memory_space=pl.ANY)] * 2,
        scratch_shapes=[
            pltpu.VMEM((3, PART, half), jnp.float32),
            pltpu.VMEM(turned.shape, turned.dtype),
            pltpu.VMEM((h.shape[0] - width, half), turned.dtype),
            pltpu.VMEM(gacc.shape, gacc.dtype),
            pltpu.VMEM((1, width), jnp.float32),
            dma((3,)), dma((3,)), dma((width // PART,)),
        ],
        compiler_params=pltpu.CompilerParams(vmem_limit_bytes=14 * 1024 * 1024),
        name="last_stage",
    )(h, *kept)


def paired(row_count, feat_count, n, width):
    half = width // 2
    rows = row_count * n
    held = 4 * width * half + 2 * rows * (width + half + 256) + 12 * n * half + 4 * n * width
    return (
        row_count == 2 * feat_count and (feat_count - 1).bit_length() == 2
        and feat_count & (feat_count - 1) == 0 and n % (6 * CHUNK) == 0 and n // CHUNK >= 2 * AHEAD + 1
        and n <= 1024 and half % TILE == 0 and held <= VMEM_BUDGET
    )


def by_lines(features, labels, posterior, prior_prec):
    n, width = features.shape
    held = line_stage(
        features, labels.reshape(1, n), posterior.reshape(width // 128, 128),
        prior_prec.reshape(1, width),
    )
    hessian, gradient = last_stage(*held)
    return (hessian, gradient.reshape(width))


def gather_kernel(
    row_count, feat_count, x_ref, st_ref, all_ref, col_ref, stat_ref,
    ring, zs, zr, ps, pr, ds, dr, cs, cr, cl, ss, sr, ts, tr, lsem,
):
    r = lax.axis_index("rows")
    f = lax.axis_index("feat")
    n, width = x_ref.shape
    half = width // 2
    col_width = col_ref.shape[1]
    unit = min(col_width, half)
    per_half = half // unit
    per_owner = col_width // unit
    chips = row_count // 2
    bits = chips.bit_length() - 1
    part = n // SPLIT

    def rows_of(device):
        return pl.ds(pl.multiple_of(device * n, n), n)

    def remote(src, dst, send, recv, **where):
        return pltpu.make_async_remote_copy(
            src_ref=src, dst_ref=dst, send_sem=send, recv_sem=recv,
            device_id=where, device_id_type=MESH,
        )

    sends = []

    def go(copy):
        copy.start()
        sends.append(copy)

    def ring_slice(step, h, k):
        rows, cols = pl.ds(k * part, part), pl.ds(h * half, half)
        return x_ref.at[rows, cols] if step == 0 else ring.at[step - 1, rows, cols]

    def ring_copy(step, h, k):
        to = lax.rem(f + (1 if h == 0 else feat_count - 1), feat_count)
        return remote(
            ring_slice(step, h, k),
            ring.at[step, pl.ds(k * part, part), pl.ds(h * half, half)],
            zs.at[step, h, k], zr.at[step, h, k], feat=to,
        )

    def column_sends(step, h, k, start):
        block = lax.rem(f + (feat_count - step if h == 0 else step), feat_count)
        for u in range(per_half):
            inner = h * half + u * unit
            if width % col_width == 0:
                owner = block * (width // col_width) + inner // col_width
                offset = inner % col_width
                slot = offset // unit
            else:
                owner = (block * width + inner) // col_width
                slot = ((block * width + inner) % col_width) // unit
                offset = pl.multiple_of(slot * unit, unit)
            src = ring_slice(step, h, k).at[:, pl.ds(u * unit, unit)]
            dst = col_ref.at[
                pl.ds(pl.multiple_of(r * n + k * part, part), part), pl.ds(offset, unit)
            ]
            send = cs.at[step, h, k, u]

            @pl.when(owner != r)
            def _():
                copy = remote(src, dst, send, cr.at[r, slot, k], rows=owner)
                copy.start() if start else copy.wait_send()

            if start:
                @pl.when(owner == r)
                def _():
                    pltpu.make_async_copy(src, dst, cl.at[slot, k]).start()

    def order(h):
        return list(range(bits)) if h == 0 else list(range(bits))[::-1]

    def spread(h, stage, mask):
        bit = 1 << order(h)[stage]
        origin = r ^ (2 * mask)
        cols = pl.ds(h * half, half)
        src = x_ref.at[:, cols] if mask == 0 else all_ref.at[rows_of(origin), cols]
        return remote(
            src, all_ref.at[rows_of(origin), cols],
            ps.at[h, mask | bit], pr.at[h, mask | bit], rows=r ^ (2 * bit),
        )

    def partner(h, mask):
        origin = r ^ (2 * mask)
        cols = pl.ds(h * half, half)
        src = x_ref.at[:, cols] if mask == 0 else all_ref.at[rows_of(origin), cols]
        return remote(
            src, all_ref.at[rows_of(origin), cols],
            ds.at[h, mask], dr.at[h, mask], rows=r ^ 1,
        )

    def masks_before(h, stage):
        found = [0]
        for b in order(h)[:stage]:
            found += [m | (1 << b) for m in found]
        return found

    for k in range(SPLIT):
        for h in range(2):
            go(ring_copy(0, h, k))
    stat_local = pltpu.make_async_copy(st_ref, stat_ref.at[r, f], lsem.at[0])
    stat_local.start()
    for d in range(1, feat_count):
        go(remote(
            st_ref, stat_ref.at[r, f], ss.at[d], sr.at[d],
            feat=lax.rem(f + d, feat_count),
        ))
    for stage in range(bits):
        for h in range(2):
            go(spread(h, stage, 0))
    for h in range(2):
        go(partner(h, 0))
    own = pltpu.make_async_copy(x_ref, all_ref.at[rows_of(r)], lsem.at[1])
    own.start()
    for k in range(SPLIT):
        for h in range(2):
            column_sends(0, h, k, True)

    stat_local.wait()
    for d in range(1, feat_count):
        remote(
            st_ref, stat_ref.at[r, lax.rem(f + feat_count - d, feat_count)],
            ss.at[d], sr.at[d], feat=f,
        ).wait_recv()
    for d in range(1, row_count):
        go(remote(
            stat_ref.at[r], stat_ref.at[r], ts.at[d], tr.at[d],
            rows=lax.rem(r + d, row_count),
        ))

    def relay(stage):
        for h in range(2):
            bit = 1 << order(h)[stage]
            for m in masks_before(h, stage):
                mask = m | bit
                cols = pl.ds(h * half, half)
                remote(
                    x_ref.at[:, cols], all_ref.at[rows_of(r ^ (2 * mask)), cols],
                    ps.at[h, mask], pr.at[h, mask], rows=r,
                ).wait_recv()
                for later in range(stage + 1, bits):
                    go(spread(h, later, mask))
                go(partner(h, mask))

    for step in range(1, feat_count):
        for k in range(SPLIT):
            for h in range(2):
                ring_copy(step - 1, h, k).wait_recv()
                if step < feat_count - 1:
                    go(ring_copy(step, h, k))
                column_sends(step, h, k, True)
        if step <= bits:
            relay(step - 1)
    for stage in range(feat_count - 1, bits):
        relay(stage)

    for h in range(2):
        for mask in range(chips):
            cols = pl.ds(h * half, half)
            remote(
                x_ref.at[:, cols], all_ref.at[rows_of(r ^ (2 * mask) ^ 1), cols],
                ds.at[h, mask], dr.at[h, mask], rows=r,
            ).wait_recv()
    for d in range(1, row_count):
        origin = lax.rem(r + row_count - d, row_count)
        remote(
            stat_ref.at[origin], stat_ref.at[origin], ts.at[d], tr.at[d], rows=r
        ).wait_recv()
        for slot in range(per_owner):
            for k in range(SPLIT):
                dst = col_ref.at[
                    pl.ds(pl.multiple_of(origin * n + k * part, part), part),
                    pl.ds(slot * unit, unit),
                ]
                remote(
                    x_ref.at[pl.ds(0, part), pl.ds(0, unit)], dst,
                    cs.at[0, 0, 0, 0], cr.at[origin, slot, k], rows=r,
                ).wait_recv()
    for slot in range(per_owner):
        for k in range(SPLIT):
            dst = col_ref.at[
                pl.ds(pl.multiple_of(r * n + k * part, part), part),
                pl.ds(slot * unit, unit),
            ]
            pltpu.make_async_copy(
                x_ref.at[pl.ds(0, part), pl.ds(0, unit)], dst, cl.at[slot, k]
            ).wait()
    own.wait()
    for copy in sends:
        copy.wait_send()
    for step in range(feat_count):
        for k in range(SPLIT):
            for h in range(2):
                column_sends(step, h, k, False)


def gather(features, stats):
    row_count = lax.axis_size("rows")
    feat_count = lax.axis_size("feat")
    n, width = features.shape
    half = width // 2
    col_width = width * feat_count // row_count
    unit = min(col_width, half)
    chips = row_count // 2
    dma = pltpu.SemaphoreType.DMA
    return pl.pallas_call(
        functools.partial(gather_kernel, row_count, feat_count),
        out_shape=(
            jax.ShapeDtypeStruct((row_count * n, width), features.dtype),
            jax.ShapeDtypeStruct((row_count * n, col_width), features.dtype),
            jax.ShapeDtypeStruct((row_count, feat_count) + stats.shape, stats.dtype),
        ),
        in_specs=[pl.BlockSpec(memory_space=pltpu.VMEM)] * 2,
        out_specs=[pl.BlockSpec(memory_space=pl.ANY)] * 3,
        scratch_shapes=[
            pltpu.VMEM((feat_count - 1, n, width), features.dtype),
            dma((feat_count - 1, 2, SPLIT)), dma((feat_count - 1, 2, SPLIT)),
            dma((2, chips)), dma((2, chips)),
            dma((2, chips)), dma((2, chips)),
            dma((feat_count, 2, SPLIT, half // unit)),
            dma((row_count, col_width // unit, SPLIT)),
            dma((col_width // unit, SPLIT)),
            dma((feat_count,)), dma((feat_count,)),
            dma((row_count,)), dma((row_count,)),
            dma((2,)),
        ],
        compiler_params=pltpu.CompilerParams(
            has_side_effects=True, vmem_limit_bytes=32 * 1024 * 1024
        ),
        name="gather",
    )(features, stats)


def per_device(features, labels, posterior, prior_prec):
    row_count = lax.axis_size("rows")
    feat_count = lax.axis_size("feat")
    row_index = lax.axis_index("rows")
    feat_index = lax.axis_index("feat")
    n, block_width = features.shape
    if paired(row_count, feat_count, n, block_width):
        return by_lines(features, labels, posterior, prior_prec)
    col_width = block_width * feat_count // row_count
    partial_value = jnp.dot(features, posterior, preferred_element_type=jnp.float32)
    padded = -(-n // 512) * 512
    stats = jnp.concatenate([
        jnp.pad(partial_value, (0, padded - n)),
        jnp.pad(labels.astype(jnp.float32), (0, padded - n)),
    ]).reshape(-1, 128)
    all_rows, column_rows, all_stats = gather(features, stats)
    all_stats = all_stats.reshape(row_count, feat_count, 2, padded)[..., :n]
    margins = jnp.sum(all_stats[:, :, 0], axis=1).reshape(-1)
    all_labels = all_stats[:, 0, 1].reshape(-1)
    chance = jax.nn.sigmoid(margins)
    weight = (chance * (1.0 - chance)).astype(jnp.bfloat16)
    residual = (all_labels - chance).astype(jnp.bfloat16)
    summed = jnp.dot(residual, all_rows, preferred_element_type=jnp.float32)
    gradient = summed - prior_prec * posterior.astype(jnp.float32)
    weighted = weight[:, None] * all_rows
    product = lax.dot_general(
        weighted, column_rows, (((0,), (0,)), ((), ())), preferred_element_type=jnp.float32
    )
    global_rows = feat_index * block_width + jnp.arange(block_width, dtype=jnp.int32)
    global_cols = row_index * col_width + jnp.arange(col_width, dtype=jnp.int32)
    on_diagonal = global_rows[:, None] == global_cols[None, :]
    hessian = product + jnp.where(on_diagonal, prior_prec[:, None], jnp.float32(0.0))
    return (hessian, gradient)


def solution(mesh):
    in_specs = (P("rows", "feat"), P("rows"), P("feat"), P("feat"))
    out_specs = (P("feat", "rows"), P("feat"))
    return jax.shard_map(
        per_device, mesh=mesh, in_specs=in_specs, out_specs=out_specs, check_vma=False
    )
```

```python
import functools

import jax
import jax.numpy as jnp
from jax import lax
from jax.experimental import pallas as pl
from jax.experimental.pallas import tpu as pltpu
from jax.sharding import PartitionSpec as P

MESH = pl.DeviceIdType.MESH
SPLIT = 2
CHUNK = 16
PIECES = 4
TILE = 512
PART = 256
AHEAD = 2
LATE = 4
VMEM_BUDGET = 60 * 1024 * 1024


def pick(p, q, e):
    first = jnp.where((p ^ 1) == e, p ^ 2, p ^ 1)
    second = jnp.where(((p ^ 1) == e) | ((p ^ 2) == e), p ^ 3, p ^ 2)
    return jnp.where(q == 0, p, jnp.where(q == 1, first, second))


def passed_chip(p, z, last):
    return jnp.where(p > z, 0, jnp.where(p < z, last, p ^ 3))


def slabs(ref, lead, starts, size, cols):
    parts = []
    for start in starts:
        rows = pl.ds(pl.multiple_of(start, 16), size)
        parts.append(ref[rows, cols] if lead is None else ref[lead, rows, cols])
    return jnp.concatenate(parts, axis=0)


def wide(value, width):
    return jnp.concatenate([value] * (width // value.shape[1]), axis=1)


def weigh(all_ref, wr_ref, starts, size, cols):
    x = slabs(all_ref, None, starts, size, cols)
    weight = slabs(wr_ref, 0, starts, size, slice(None))
    residual = slabs(wr_ref, 1, starts, size, slice(None)).astype(jnp.float32)
    pulled = x.astype(jnp.float32) * wide(residual, PART)
    pulled = jnp.sum(pulled.reshape(-1, 8, PART), axis=0)
    return (x * wide(weight, PART)).T, pulled


def line_kernel(
    row_count, feat_count, x_ref, label_ref, post_ref, prec_ref,
    h_ref, turned_out, pull_out,
    all_ref, col_ref, wr_ref, gacc_ref, kept, even, odd, abuf, st_ref, stat_ref,
    agr, pr, br, ar, adr, own_s, relay_s, extra_s, part_s, src_s, bf_s, af_s, ad_s,
    side_r, side_s, ss, sr, ts, tr, lsem,
):
    r = lax.axis_index("rows")
    z = lax.axis_index("feat")
    p, c = r // 2, r % 2
    last = feat_count - 1
    n, width = x_ref.shape
    half = width // 2
    m = CHUNK
    nch = n // m
    items = last
    big = n // PIECES
    pace = nch // (3 * PIECES)
    avoid = jnp.where(z == 0, 0, jnp.where(z == last, last, -8))
    relays = p != avoid
    relays_all = (p ^ last) == avoid
    has_down, has_up = z >= 1, z <= last - 1

    def rows_of(chip, core, j):
        return pl.ds(pl.multiple_of((chip * 2 + core) * n + j * m, m), m)

    def own_rows(j):
        return pl.ds(pl.multiple_of(j * m, m), m)

    def big_rows(chip, core, j):
        return pl.ds(pl.multiple_of((chip * 2 + core) * n + j * big, 16), big)

    def cols_of(h):
        return pl.ds(pl.multiple_of(h * half, half), half)

    def remote(src, dst, send, recv, **where):
        return pltpu.make_async_remote_copy(
            src_ref=src, dst_ref=dst, send_sem=send, recv_sem=recv,
            device_id=where, device_id_type=MESH,
        )

    barrier = pltpu.get_barrier_semaphore()
    for d in range(1, row_count):
        pl.semaphore_signal(
            barrier, inc=1, device_id={"rows": lax.rem(r + d, row_count)},
            device_id_type=MESH,
        )
    for d in range(1, feat_count):
        for other in (r, r ^ 1):
            pl.semaphore_signal(
                barrier, inc=1,
                device_id={"rows": other, "feat": lax.rem(z + d, feat_count)},
                device_id_type=MESH,
            )

    own = pltpu.make_async_copy(
        x_ref, all_ref.at[pl.ds(pl.multiple_of(r * n, n), n)], lsem.at[1]
    )
    own.start()
    own.wait()
    st_ref[...] = jnp.zeros_like(st_ref)
    post = post_ref[...].astype(jnp.float32)
    for t in range(-(-n // 128)):
        count = min(128, n - 128 * t)
        here = pl.ds(128 * t, count)
        st_ref[8 + t:9 + t, 0:count] = label_ref[:, here].astype(jnp.float32)
        rows = pl.ds(pl.multiple_of(r * n + 128 * t, 16), count)

        total = jnp.zeros((count, 128), jnp.float32)
        for i in range(width // 128):
            value = all_ref[rows, pl.ds(128 * i, 128)].astype(jnp.float32)
            total = total + value * post[i:i + 1, :]
        st_ref[t:t + 1, 0:count] = jnp.sum(total.T, axis=0, keepdims=True)
    gacc_ref[...] = jnp.zeros_like(gacc_ref)
    for t in range(width // 128):
        lanes = pl.ds(128 * t, 128)
        gacc_ref[0:1, lanes] = -prec_ref[:, lanes] * post[t:t + 1, :]
    pl.semaphore_wait(barrier, row_count - 1 + 2 * (feat_count - 1))

    def ag(dim, h, j, src, chip, rel, send):
        remote(
            src, all_ref.at[big_rows(chip, c, j), cols_of(h)],
            send, agr.at[rel, h, j], rows=r ^ (2 * dim),
        ).start()

    def own_plane(s):
        j = lax.rem(s, PIECES)
        rows = pl.ds(pl.multiple_of(j * big, 16), big)

        @pl.when(s < PIECES)
        def _():
            ag(1, 0, j, x_ref.at[rows, cols_of(0)], p, 0, own_s.at[0])
            ag(2, 1, j, x_ref.at[rows, cols_of(1)], p, 1, own_s.at[1])

        @pl.when(s >= PIECES)
        def _():
            ag(1, 1, j, x_ref.at[rows, cols_of(1)], p, 0, own_s.at[0])
            ag(2, 0, j, x_ref.at[rows, cols_of(0)], p, 1, own_s.at[1])

    def own_line(j):
        for h in range(2):
            src = x_ref.at[own_rows(j), cols_of(h)]

            @pl.when(has_down & (p == 0))
            def _():
                remote(
                    src, abuf.at[z - 1, c, own_rows(j)], own_s.at[2], ar.at[0, c, j],
                    rows=2 * p + h, feat=z - 1,
                ).start()

            @pl.when(has_down & (p == z))
            def _():
                remote(
                    src, col_ref.at[rows_of(p, c, j)], own_s.at[2], br.at[0, c, j],
                    rows=2 * p + h, feat=z - 1,
                ).start()

            @pl.when(has_up & (p == last))
            def _():
                remote(
                    src, abuf.at[z, c, own_rows(j)], own_s.at[3], ar.at[0, c, j],
                    rows=2 * p + h, feat=z + 1,
                ).start()

            @pl.when(has_up & (p == z))
            def _():
                remote(
                    src, col_ref.at[rows_of(p, c, j)], own_s.at[3], br.at[0, c, j],
                    rows=2 * p + h, feat=z + 1,
                ).start()

    def own_sends(j, _):
        own_line(j)

        @pl.when(lax.rem(j, 3 * pace) == 0)
        def _():
            own_plane(2 * (j // (3 * pace)))
            own_plane(2 * (j // (3 * pace)) + 1)
        return 0

    own_sends(0, 0)
    remote(
        x_ref, all_ref.at[pl.ds(pl.multiple_of(r * n, n), n)], part_s.at[3], pr.at[3],
        rows=r ^ 1,
    ).start()

    stat_local = pltpu.make_async_copy(st_ref, stat_ref.at[r, z], lsem.at[0])
    stat_local.start()
    for d in range(1, feat_count):
        remote(
            st_ref, stat_ref.at[r, z], ss.at[d], sr.at[d],
            feat=lax.rem(z + d, feat_count),
        ).start()

    def share_stats():
        stat_local.wait()
        for d in range(1, feat_count):
            remote(
                st_ref, stat_ref.at[r, lax.rem(z + feat_count - d, feat_count)],
                ss.at[d], sr.at[d], feat=z,
            ).wait_recv()
        for d in range(1, row_count):
            remote(
                stat_ref.at[r], stat_ref.at[r], ts.at[d], tr.at[d],
                rows=lax.rem(r + d, row_count),
            ).start()

    def weights():
        for d in range(1, row_count):
            origin = lax.rem(r + row_count - d, row_count)
            remote(
                stat_ref.at[origin], stat_ref.at[origin], ts.at[d], tr.at[d], rows=r
            ).wait_recv()

        def one(i, _):
            margins = stat_ref[i, 0, 0:8]
            for f in range(1, feat_count):
                margins = margins + stat_ref[i, f, 0:8]
            chance = 1.0 / (1.0 + jnp.exp(-margins))
            weight = (chance * (1.0 - chance)).astype(jnp.bfloat16)
            residual = (stat_ref[i, 0, 8:16] - chance).astype(jnp.bfloat16)
            for lead, value in ((0, weight), (1, residual)):
                turned = value.astype(jnp.float32).T
                for t in range(-(-n // 128)):
                    count = min(128, n - 128 * t)
                    rows = pl.ds(pl.multiple_of(i * n + 128 * t, 16), count)
                    wr_ref[lead, rows, :] = jnp.broadcast_to(
                        turned[:count, t:t + 1], (count, 128)
                    ).astype(jnp.bfloat16)
            return 0

        lax.fori_loop(0, row_count, one, 0)

    def arrive(rel, h, j):
        chip = p ^ (rel + 1)
        here = all_ref.at[big_rows(chip, c, j), cols_of(h)]
        remote(here, here, own_s.at[0], agr.at[rel, h, j], rows=r).wait_recv()
        remote(here, here, part_s.at[rel], pr.at[rel], rows=r ^ 1).start()

    def forward(rel, h, j, send):
        chip = p ^ (rel + 1)
        here = all_ref.at[big_rows(chip, c, j), cols_of(h)]
        ag(2 - rel, h, j, here, chip, 2, send)

    def gather_event(s):
        a, j = s // PIECES, s % PIECES

        @pl.when(a == 0)
        def _():
            arrive(0, 0, j)

            @pl.when(relays)
            def _():
                forward(0, 0, j, relay_s.at[0])
            arrive(1, 1, j)

            @pl.when(relays)
            def _():
                forward(1, 1, j, relay_s.at[1])

        @pl.when(a == 1)
        def _():
            arrive(0, 1, j)

            @pl.when(relays_all)
            def _():
                forward(0, 1, j, extra_s.at[0])
            arrive(1, 0, j)

            @pl.when(relays_all)
            def _():
                forward(1, 0, j, extra_s.at[1])

    def corner_event(j):
        arrive(2, 0, j)
        arrive(2, 1, j)

    def source_event(s):
        q, j = 1 + s // nch, s % nch
        for h in range(2):
            @pl.when(has_down)
            def _():
                where = rows_of(pick(p, q, 0), c, j)
                remote(
                    all_ref.at[where, cols_of(h)], col_ref.at[where],
                    src_s.at[0, q], br.at[q, c, j], rows=2 * p + h, feat=z - 1,
                ).start()

            @pl.when(has_up)
            def _():
                where = rows_of(pick(p, q, last), c, j)
                remote(
                    all_ref.at[where, cols_of(h)], col_ref.at[where],
                    src_s.at[1, q], br.at[q, c, j], rows=2 * p + h, feat=z + 1,
                ).start()

    def column_event(s):
        q, j = s // nch, s % nch
        down = p > z
        chip = pick(p, q, jnp.where(down, 0, last))
        for k in range(2):
            here = col_ref.at[rows_of(chip, k, j)]
            remote(here, here, bf_s.at[q], br.at[q, k, j], rows=r).wait_recv()

            rest = (s < items * nch - 1) | ((p != 0) & (p != last))

            @pl.when(((down & has_down) | (~down & has_up)) & rest)
            def _():
                remote(
                    here, here, bf_s.at[q], br.at[q, k, j],
                    feat=jnp.where(down, z - 1, z + 1),
                ).start()

    side_down, side_up = (p ^ 2) == last, p == 2
    side_first = (side_down & (z == last)) | (side_up & (z == 0))
    side_later = (side_down & (z < last)) | (side_up & (z > 0))
    side_more = (side_down & has_down) | (side_up & has_up)
    side_give = (side_down & (z <= last - 2)) | (side_up & (z >= 2))
    side_next = jnp.where(side_down, z - 1, z + 1)
    side_rows = own_rows(nch - 1)

    def side_own():
        for h in range(2):
            remote(
                x_ref.at[side_rows, cols_of(h)], abuf.at[0, c, side_rows],
                side_s.at[0], side_r.at[c], rows=2 * p + h, feat=side_next,
            ).start()

    def side_event():
        for k in range(2):
            here = abuf.at[0, k, side_rows]
            remote(here, here, side_s.at[1], side_r.at[k], rows=r).wait_recv()

            @pl.when(side_more)
            def _():
                remote(here, here, side_s.at[1], side_r.at[k], feat=side_next).start()

            @pl.when(side_give)
            def _():
                remote(
                    here, col_ref.at[rows_of(p, k, nch - 1)], side_s.at[2],
                    br.at[items - 1, k, nch - 1], rows=2 * (p ^ 2) + c,
                ).start()

    def pass_event(s):
        q, j = s // nch, s % nch
        down = p == 0
        block = jnp.where(down, z + 1 + q, z - 1 - q)
        slot = jnp.where(down, block - 1, block)

        @pl.when((block >= 0) & (block <= last))
        def _():
            for k in range(2):
                here = abuf.at[slot, k, own_rows(j)]
                remote(here, here, af_s.at[q], ar.at[q, k, j], rows=r).wait_recv()

                @pl.when((down & has_down) | (~down & has_up))
                def _():
                    remote(
                        here, here, af_s.at[q], ar.at[q + 1, k, j],
                        feat=jnp.where(down, z - 1, z + 1),
                    ).start()

    def deliver_event(s):
        q, j = s // nch, s % nch
        down = p == 0
        block = jnp.where(down, z + 1 + q, z - 1 - q)
        slot = jnp.where(down, block - 1, block)

        @pl.when((block >= 0) & (block <= last))
        def _():
            for k in range(2):
                remote(
                    abuf.at[slot, k, own_rows(j)], col_ref.at[rows_of(p, k, j)],
                    ad_s.at[q], adr.at[j // (nch // 3)], rows=2 * block + c,
                ).start()

    lag = 10 * pace
    tiles = width // TILE
    edge = passed_chip(p, z, last)
    twice = col_ref.at[pl.ds(0, 2 * n)]
    third = n // 3
    once = col_ref.at[pl.ds(0, 2 * third)]
    q = nch // 3
    begins = [2 * q + 1, 4 * q + 1, 5 * q + 1, 6 * q, 7 * q, 8 * q]
    ends = [4 * q - 1, 5 * q + 1, 6 * q, 7 * q, 8 * q, 9 * q - pace]
    near, far = pick(p, 1, edge), pick(p, 2, edge)

    def partner_rows(chip):
        rel = jnp.where(chip == p, 3, (p ^ chip) - 1)
        there = all_ref.at[pl.ds(pl.multiple_of((2 * chip + 1 - c) * n, n), n)]
        remote(there, there, part_s.at[rel], pr.at[rel], rows=r).wait_recv()

        @pl.when(p == z)
        def _():
            rows = pl.ds(pl.multiple_of(chip * 2 * n, n), 2 * n)
            copy = pltpu.make_async_copy(
                all_ref.at[rows, cols_of(c)], col_ref.at[rows], lsem.at[2]
            )
            copy.start()
            copy.wait()

    def prepare(i):
        rows = pl.ds(pl.multiple_of(i * TILE, TILE), TILE)
        h_ref[rows, :] = jnp.zeros((TILE, half), jnp.float32)
        offset = i * TILE - c * half

        @pl.when((p == z) & (offset >= 0) & (offset < half))
        def _():
            cols = pl.ds(pl.multiple_of(offset, TILE), TILE)
            shape = (TILE, TILE)
            same = lax.broadcasted_iota(jnp.int32, shape, 0) == lax.broadcasted_iota(
                jnp.int32, shape, 1
            )
            h_ref[rows, cols] = jnp.where(
                same, jnp.broadcast_to(prec_ref[:, rows], shape), 0.0
            )

    def unit_rows(index):
        def start(chip, core, piece):
            return (chip * 2 + core) * n + piece * third

        late = jnp.where(index == 2, 2, index - 4 + (index == 3))
        rows = []
        for i in range(4):
            core, upper = i % 2, i // 2
            pair = jnp.where(
                index == 0, start(p, core, upper),
                jnp.where(
                    index == 1, start(near if upper else p, core, 0 if upper else 2),
                    start(near, core, 1 + upper),
                ),
            )
            far_rows = start(edge if upper else far, core, late)
            rows.append(jnp.where((index == 0) | (index == 1) | (index == 3), pair, far_rows))
        return rows

    def part_of(i):
        return pl.ds(pl.multiple_of(i * PART, PART), PART)

    def turn(rows, i, flag):
        weighted, pulled = weigh(all_ref, wr_ref, rows, third, part_of(i))
        gacc_ref[:, part_of(i)] += pulled * flag
        return weighted

    def multiply(turned, rows, i):
        value = turned[...]
        for t in range(half // TILE):
            there = pl.ds(t * TILE, TILE)
            h_ref[part_of(i), there] += jnp.dot(
                value, slabs(col_ref, None, rows, third, there),
                preferred_element_type=jnp.float32,
            )

    def compute(u):
        index = sum((u >= s).astype(jnp.int32) for s in begins) - 1

        def choose(values):
            out = values[0]
            for i in range(1, len(values)):
                out = jnp.where(index >= i, values[i], out)
            return out

        begin, span = choose(begins), choose([e - s for s, e in zip(begins, ends)])
        low = jnp.minimum((u - begin) * tiles // span, tiles)
        high = jnp.minimum((u - begin + 1) * tiles // span, tiles)
        rows = unit_rows(index)

        @pl.when(u == begin)
        def _():
            @pl.when(index == 0)
            def _():
                weights()
                partner_rows(p)

            @pl.when(index == 1)
            def _():
                partner_rows(near)

            @pl.when(index == 2)
            def _():
                partner_rows(far)
                partner_rows(edge)

            @pl.when((index >= 4) & (p != z))
            def _():
                remote(once, once, bf_s.at[0], adr.at[index - 4], rows=r).wait_recv()

            @pl.when(index != 2)
            def _():
                even[...] = turn(rows, 0, 1.0)

        def keep(i, _):
            for e in range(2):
                kept[part_of(2 * i + e), :] = turn(rows, 2 * i + e, 1.0)
            return 0

        def pair(i, _):
            multiply(even, rows, 2 * i)
            odd[...] = turn(rows, 2 * i + 1, 1.0)
            multiply(odd, rows, 2 * i + 1)
            more = i < tiles - 1
            even[...] = turn(
                rows, jnp.where(more, 2 * i + 2, 0), jnp.where(more, 1.0, 0.0)
            )
            return 0

        @pl.when(index == 2)
        def _():
            lax.fori_loop(low, high, keep, 0)

            @pl.when(u == ends[2] - 1)
            def _():
                pltpu.make_async_copy(kept, turned_out, lsem.at[3]).start()

        @pl.when(index != 2)
        def _():
            lax.fori_loop(low, high, pair, 0)

        @pl.when(u == ends[-1] - 1)
        def _():
            pltpu.make_async_copy(gacc_ref, pull_out, lsem.at[4]).start()

    def some(event, low, high):
        def one(i, _):
            event(i)
            return 0
        lax.fori_loop(low, high, one, 0)

    def step(u, _):
        @pl.when(u < begins[0])
        def _():
            per = -(-tiles // begins[0])
            some(prepare, jnp.minimum(u * per, tiles), jnp.minimum(u * per + per, tiles))

        @pl.when((u >= begins[0]) & (u < ends[-1]))
        def _():
            compute(u)

        @pl.when((p != z) & (u < items * nch))
        def _():
            column_event(u)

        @pl.when(u == 2)
        def _():
            share_stats()

        @pl.when(u < 2)
        def _():
            some(lambda j: own_sends(j, 0), 1 + AHEAD * u, 1 + AHEAD * (u + 1))

        @pl.when(u >= 2)
        def _():
            low = 1 + 2 * AHEAD + 3 * (u - 2)
            some(
                lambda j: own_sends(j, 0), jnp.minimum(low, nch), jnp.minimum(low + 3, nch)
            )

        @pl.when((u == 0) & side_first)
        def _():
            side_own()
        hops = jnp.where(side_down, last - z, z)

        @pl.when((u == 3 * hops + 4) & side_later)
        def _():
            side_event()
        for e in range(2):
            i = u - (4 + 2 * e) * pace

            @pl.when((i >= 0) & (i % (3 * pace) == 0) & (i < 3 * pace * PIECES))
            def _():
                gather_event(2 * (i // (3 * pace)) + e)

        corner = u - 4 * q - 1

        @pl.when((corner >= 0) & (corner < q) & (corner % pace == 0))
        def _():
            corner_event(corner // pace)

        @pl.when((p == z) & (u >= lag) & (u < lag + 2 * nch))
        def _():
            source_event(u - lag)

        @pl.when(((p == 0) | (p == last)) & (u >= LATE) & (u < LATE + items * nch))
        def _():
            pass_event(u - LATE)

        @pl.when(((p == 0) | (p == last)) & (u >= nch))
        def _():
            low = jnp.minimum(2 * (u - nch), u - LATE)
            some(deliver_event, low, jnp.minimum(2 * (u + 1 - nch), u + 1 - LATE))
        return 0

    lax.fori_loop(0, items * nch + LATE, step, 0)

    @pl.when(p != z)
    def _():
        remote(once, once, bf_s.at[0], adr.at[2], rows=r).wait_recv()

    for i, start in enumerate(unit_rows(jnp.int32(2))):
        held = col_ref[pl.ds(pl.multiple_of(start, 16), third), :]
        h_ref[pl.ds(width + i * third, third), :] = held.astype(jnp.float32)

    def sent(ref, sem):
        remote(ref, ref, sem, pr.at[3], rows=r).wait_send()

    for d in range(1, feat_count):
        sent(st_ref, ss.at[d])
    for d in range(1, row_count):
        sent(stat_ref.at[r], ts.at[d])
    for i in range(2):
        sent(x_ref, own_s.at[i])

        @pl.when(relays)
        def _():
            sent(x_ref.at[:, pl.ds(0, half)], relay_s.at[i])

        @pl.when(relays_all)
        def _():
            sent(x_ref.at[:, pl.ds(0, half)], extra_s.at[i])

    @pl.when(has_down & ((p == 0) | (p == z)))
    def _():
        sent(x_ref, own_s.at[2])

    @pl.when(has_up & ((p == last) | (p == z)))
    def _():
        sent(x_ref, own_s.at[3])
    for rel in range(4):
        sent(x_ref, part_s.at[rel])
    @pl.when(side_first)
    def _():
        sent(x_ref.at[pl.ds(0, m)], side_s.at[0])

    @pl.when(side_later & side_more)
    def _():
        sent(col_ref.at[pl.ds(0, 2 * m)], side_s.at[1])

    @pl.when(side_later & side_give)
    def _():
        sent(col_ref.at[pl.ds(0, 2 * m)], side_s.at[2])
    down = p > z
    for q in range(items):
        if q > 0:
            @pl.when((p == z) & has_down)
            def _():
                sent(x_ref, src_s.at[0, q])

            @pl.when((p == z) & has_up)
            def _():
                sent(x_ref, src_s.at[1, q])

        sends = (p != z) & ((down & has_down) | (~down & has_up))
        short = ((p == 0) | (p == last)) if q == items - 1 else p < 0

        @pl.when(sends & ~short)
        def _():
            sent(twice, bf_s.at[q])

        @pl.when(sends & short)
        def _():
            sent(col_ref.at[pl.ds(0, 2 * n - 2 * m)], bf_s.at[q])
        for edge, block, more in ((0, z + 1 + q, has_down), (last, z - 1 - q, has_up)):
            @pl.when((p == edge) & (block >= 0) & (block <= last))
            def _():
                sent(twice, ad_s.at[q])

                @pl.when(more)
                def _():
                    sent(twice, af_s.at[q])
    pltpu.make_async_copy(gacc_ref, pull_out, lsem.at[4]).wait()
    pltpu.make_async_copy(kept, turned_out, lsem.at[3]).wait()


def line_stage(features, labels, post, prec):
    row_count = lax.axis_size("rows")
    feat_count = lax.axis_size("feat")
    n, width = features.shape
    half = width // 2
    items = feat_count - 1
    nch = n // CHUNK
    dma = pltpu.SemaphoreType.DMA
    return pl.pallas_call(
        functools.partial(line_kernel, row_count, feat_count),
        out_shape=(
            pltpu.VMEM((width + 4 * n // 3, half), jnp.float32),
            pltpu.HBM((width, 4 * n // 3), features.dtype),
            pltpu.HBM((8, width), jnp.float32),
        ),
        in_specs=[
            pl.BlockSpec(memory_space=pl.ANY), pl.BlockSpec(memory_space=pltpu.VMEM),
            pl.BlockSpec(memory_space=pltpu.VMEM), pl.BlockSpec(memory_space=pltpu.VMEM),
        ],
        out_specs=[pl.BlockSpec(memory_space=pltpu.VMEM)]
        + [pl.BlockSpec(memory_space=pl.ANY)] * 2,
        scratch_shapes=[
            pltpu.VMEM((row_count * n, width), features.dtype),
            pltpu.VMEM((row_count * n, half), features.dtype),
            pltpu.VMEM((2, row_count * n, 128), features.dtype),
            pltpu.VMEM((8, width), jnp.float32),
            pltpu.VMEM((width, 4 * n // 3), features.dtype),
            pltpu.VMEM((PART, 4 * n // 3), features.dtype),
            pltpu.VMEM((PART, 4 * n // 3), features.dtype),
            pltpu.VMEM((items, 2, n, half), features.dtype),
            pltpu.VMEM((16, 128), jnp.float32),
            pltpu.VMEM((row_count, feat_count, 16, 128), jnp.float32),
            dma((3, 2, PIECES)), dma((4,)), dma((items, 2, nch)), dma((items + 1, 2, nch)),
            dma((3,)),
            dma((4,)), dma((2,)), dma((2,)), dma((4,)), dma((2, items)), dma((items,)),
            dma((items,)), dma((items,)), dma((2,)), dma((3,)),
            dma((feat_count,)), dma((feat_count,)),
            dma((row_count,)), dma((row_count,)),
            dma((9,)),
        ],
        compiler_params=pltpu.CompilerParams(
            collective_id=0, has_side_effects=True, vmem_limit_bytes=28 * 1024 * 1024
        ),
        name="line_stage",
    )(features, labels, post, prec)


def last_kernel(
    h_ref, turned_ref, gacc_ref,
    out_ref, grad_ref, stage, turned, cols, gacc, grad, sem, lsem, tsem,
):
    width, half = out_ref.shape
    slots = stage.shape[0]
    count = width // PART

    def part_of(i):
        return pl.ds(pl.multiple_of(i * PART, PART), PART)

    def take(i):
        return pltpu.make_async_copy(
            turned_ref.at[part_of(i)], turned.at[part_of(i)], tsem.at[i]
        )

    def put(i):
        slot = lax.rem(i, slots)
        return pltpu.make_async_copy(stage.at[slot], out_ref.at[part_of(i)], sem.at[slot])

    for i in range(count):
        take(i).start()
    late = pltpu.make_async_copy(gacc_ref, gacc, lsem.at[1])
    late.start()
    cols[...] = h_ref[pl.ds(width, cols.shape[0]), :].astype(cols.dtype)

    def one(i, _):
        @pl.when(i >= slots)
        def _():
            put(i - slots).wait()
        take(i).wait()
        slot = lax.rem(i, slots)
        value = turned[part_of(i), :]
        for t in range(half // TILE):
            there = pl.ds(t * TILE, TILE)
            stage[slot, :, there] = h_ref[part_of(i), there] + jnp.dot(
                value, cols[:, there], preferred_element_type=jnp.float32
            )
        put(i).start()
        return 0

    lax.fori_loop(0, count, one, 0)
    late.wait()
    grad[...] = jnp.sum(gacc[...], axis=0, keepdims=True)
    give = pltpu.make_async_copy(grad, grad_ref, lsem.at[2])
    give.start()
    for i in range(max(0, count - slots), count):
        put(i).wait()
    give.wait()


def last_stage(h, turned, gacc):
    width, half = turned.shape[0], h.shape[1]
    dma = pltpu.SemaphoreType.DMA
    h = pltpu.with_memory_space_constraint(h, pltpu.VMEM)
    kept = [pltpu.with_memory_space_constraint(a, pltpu.HBM) for a in (turned, gacc)]
    return pl.pallas_call(
        last_kernel,
        out_shape=(
            pltpu.HBM((width, half), jnp.float32),
            pltpu.HBM((1, width), jnp.float32),
        ),
        in_specs=[pl.BlockSpec(memory_space=pltpu.VMEM)]
        + [pl.BlockSpec(memory_space=pl.ANY)] * 2,
        out_specs=[pl.BlockSpec(memory_space=pl.ANY)] * 2,
        scratch_shapes=[
            pltpu.VMEM((3, PART, half), jnp.float32),
            pltpu.VMEM(turned.shape, turned.dtype),
            pltpu.VMEM((h.shape[0] - width, half), turned.dtype),
            pltpu.VMEM(gacc.shape, gacc.dtype),
            pltpu.VMEM((1, width), jnp.float32),
            dma((3,)), dma((3,)), dma((width // PART,)),
        ],
        compiler_params=pltpu.CompilerParams(vmem_limit_bytes=14 * 1024 * 1024),
        name="last_stage",
    )(h, *kept)


def paired(row_count, feat_count, n, width):
    half = width // 2
    rows = row_count * n
    held = 4 * width * half + 2 * rows * (width + half + 256) + 12 * n * half + 4 * n * width
    return (
        row_count == 2 * feat_count and (feat_count - 1).bit_length() == 2
        and feat_count & (feat_count - 1) == 0 and n % (3 * PIECES * CHUNK) == 0 and n // CHUNK >= 2 * AHEAD + 1
        and n <= 1024 and half % TILE == 0 and held <= VMEM_BUDGET
    )


def by_lines(features, labels, posterior, prior_prec):
    n, width = features.shape
    held = line_stage(
        features, labels.reshape(1, n), posterior.reshape(width // 128, 128),
        prior_prec.reshape(1, width),
    )
    hessian, gradient = last_stage(*held)
    return (hessian, gradient.reshape(width))


def gather_kernel(
    row_count, feat_count, x_ref, st_ref, all_ref, col_ref, stat_ref,
    ring, zs, zr, ps, pr, ds, dr, cs, cr, cl, ss, sr, ts, tr, lsem,
):
    r = lax.axis_index("rows")
    f = lax.axis_index("feat")
    n, width = x_ref.shape
    half = width // 2
    col_width = col_ref.shape[1]
    unit = min(col_width, half)
    per_half = half // unit
    per_owner = col_width // unit
    chips = row_count // 2
    bits = chips.bit_length() - 1
    part = n // SPLIT

    def rows_of(device):
        return pl.ds(pl.multiple_of(device * n, n), n)

    def remote(src, dst, send, recv, **where):
        return pltpu.make_async_remote_copy(
            src_ref=src, dst_ref=dst, send_sem=send, recv_sem=recv,
            device_id=where, device_id_type=MESH,
        )

    sends = []

    def go(copy):
        copy.start()
        sends.append(copy)

    def ring_slice(step, h, k):
        rows, cols = pl.ds(k * part, part), pl.ds(h * half, half)
        return x_ref.at[rows, cols] if step == 0 else ring.at[step - 1, rows, cols]

    def ring_copy(step, h, k):
        to = lax.rem(f + (1 if h == 0 else feat_count - 1), feat_count)
        return remote(
            ring_slice(step, h, k),
            ring.at[step, pl.ds(k * part, part), pl.ds(h * half, half)],
            zs.at[step, h, k], zr.at[step, h, k], feat=to,
        )

    def column_sends(step, h, k, start):
        block = lax.rem(f + (feat_count - step if h == 0 else step), feat_count)
        for u in range(per_half):
            inner = h * half + u * unit
            if width % col_width == 0:
                owner = block * (width // col_width) + inner // col_width
                offset = inner % col_width
                slot = offset // unit
            else:
                owner = (block * width + inner) // col_width
                slot = ((block * width + inner) % col_width) // unit
                offset = pl.multiple_of(slot * unit, unit)
            src = ring_slice(step, h, k).at[:, pl.ds(u * unit, unit)]
            dst = col_ref.at[
                pl.ds(pl.multiple_of(r * n + k * part, part), part), pl.ds(offset, unit)
            ]
            send = cs.at[step, h, k, u]

            @pl.when(owner != r)
            def _():
                copy = remote(src, dst, send, cr.at[r, slot, k], rows=owner)
                copy.start() if start else copy.wait_send()

            if start:
                @pl.when(owner == r)
                def _():
                    pltpu.make_async_copy(src, dst, cl.at[slot, k]).start()

    def order(h):
        return list(range(bits)) if h == 0 else list(range(bits))[::-1]

    def spread(h, stage, mask):
        bit = 1 << order(h)[stage]
        origin = r ^ (2 * mask)
        cols = pl.ds(h * half, half)
        src = x_ref.at[:, cols] if mask == 0 else all_ref.at[rows_of(origin), cols]
        return remote(
            src, all_ref.at[rows_of(origin), cols],
            ps.at[h, mask | bit], pr.at[h, mask | bit], rows=r ^ (2 * bit),
        )

    def partner(h, mask):
        origin = r ^ (2 * mask)
        cols = pl.ds(h * half, half)
        src = x_ref.at[:, cols] if mask == 0 else all_ref.at[rows_of(origin), cols]
        return remote(
            src, all_ref.at[rows_of(origin), cols],
            ds.at[h, mask], dr.at[h, mask], rows=r ^ 1,
        )

    def masks_before(h, stage):
        found = [0]
        for b in order(h)[:stage]:
            found += [m | (1 << b) for m in found]
        return found

    for k in range(SPLIT):
        for h in range(2):
            go(ring_copy(0, h, k))
    stat_local = pltpu.make_async_copy(st_ref, stat_ref.at[r, f], lsem.at[0])
    stat_local.start()
    for d in range(1, feat_count):
        go(remote(
            st_ref, stat_ref.at[r, f], ss.at[d], sr.at[d],
            feat=lax.rem(f + d, feat_count),
        ))
    for stage in range(bits):
        for h in range(2):
            go(spread(h, stage, 0))
    for h in range(2):
        go(partner(h, 0))
    own = pltpu.make_async_copy(x_ref, all_ref.at[rows_of(r)], lsem.at[1])
    own.start()
    for k in range(SPLIT):
        for h in range(2):
            column_sends(0, h, k, True)

    stat_local.wait()
    for d in range(1, feat_count):
        remote(
            st_ref, stat_ref.at[r, lax.rem(f + feat_count - d, feat_count)],
            ss.at[d], sr.at[d], feat=f,
        ).wait_recv()
    for d in range(1, row_count):
        go(remote(
            stat_ref.at[r], stat_ref.at[r], ts.at[d], tr.at[d],
            rows=lax.rem(r + d, row_count),
        ))

    def relay(stage):
        for h in range(2):
            bit = 1 << order(h)[stage]
            for m in masks_before(h, stage):
                mask = m | bit
                cols = pl.ds(h * half, half)
                remote(
                    x_ref.at[:, cols], all_ref.at[rows_of(r ^ (2 * mask)), cols],
                    ps.at[h, mask], pr.at[h, mask], rows=r,
                ).wait_recv()
                for later in range(stage + 1, bits):
                    go(spread(h, later, mask))
                go(partner(h, mask))

    for step in range(1, feat_count):
        for k in range(SPLIT):
            for h in range(2):
                ring_copy(step - 1, h, k).wait_recv()
                if step < feat_count - 1:
                    go(ring_copy(step, h, k))
                column_sends(step, h, k, True)
        if step <= bits:
            relay(step - 1)
    for stage in range(feat_count - 1, bits):
        relay(stage)

    for h in range(2):
        for mask in range(chips):
            cols = pl.ds(h * half, half)
            remote(
                x_ref.at[:, cols], all_ref.at[rows_of(r ^ (2 * mask) ^ 1), cols],
                ds.at[h, mask], dr.at[h, mask], rows=r,
            ).wait_recv()
    for d in range(1, row_count):
        origin = lax.rem(r + row_count - d, row_count)
        remote(
            stat_ref.at[origin], stat_ref.at[origin], ts.at[d], tr.at[d], rows=r
        ).wait_recv()
        for slot in range(per_owner):
            for k in range(SPLIT):
                dst = col_ref.at[
                    pl.ds(pl.multiple_of(origin * n + k * part, part), part),
                    pl.ds(slot * unit, unit),
                ]
                remote(
                    x_ref.at[pl.ds(0, part), pl.ds(0, unit)], dst,
                    cs.at[0, 0, 0, 0], cr.at[origin, slot, k], rows=r,
                ).wait_recv()
    for slot in range(per_owner):
        for k in range(SPLIT):
            dst = col_ref.at[
                pl.ds(pl.multiple_of(r * n + k * part, part), part),
                pl.ds(slot * unit, unit),
            ]
            pltpu.make_async_copy(
                x_ref.at[pl.ds(0, part), pl.ds(0, unit)], dst, cl.at[slot, k]
            ).wait()
    own.wait()
    for copy in sends:
        copy.wait_send()
    for step in range(feat_count):
        for k in range(SPLIT):
            for h in range(2):
                column_sends(step, h, k, False)


def gather(features, stats):
    row_count = lax.axis_size("rows")
    feat_count = lax.axis_size("feat")
    n, width = features.shape
    half = width // 2
    col_width = width * feat_count // row_count
    unit = min(col_width, half)
    chips = row_count // 2
    dma = pltpu.SemaphoreType.DMA
    return pl.pallas_call(
        functools.partial(gather_kernel, row_count, feat_count),
        out_shape=(
            jax.ShapeDtypeStruct((row_count * n, width), features.dtype),
            jax.ShapeDtypeStruct((row_count * n, col_width), features.dtype),
            jax.ShapeDtypeStruct((row_count, feat_count) + stats.shape, stats.dtype),
        ),
        in_specs=[pl.BlockSpec(memory_space=pltpu.VMEM)] * 2,
        out_specs=[pl.BlockSpec(memory_space=pl.ANY)] * 3,
        scratch_shapes=[
            pltpu.VMEM((feat_count - 1, n, width), features.dtype),
            dma((feat_count - 1, 2, SPLIT)), dma((feat_count - 1, 2, SPLIT)),
            dma((2, chips)), dma((2, chips)),
            dma((2, chips)), dma((2, chips)),
            dma((feat_count, 2, SPLIT, half // unit)),
            dma((row_count, col_width // unit, SPLIT)),
            dma((col_width // unit, SPLIT)),
            dma((feat_count,)), dma((feat_count,)),
            dma((row_count,)), dma((row_count,)),
            dma((2,)),
        ],
        compiler_params=pltpu.CompilerParams(
            has_side_effects=True, vmem_limit_bytes=32 * 1024 * 1024
        ),
        name="gather",
    )(features, stats)


def per_device(features, labels, posterior, prior_prec):
    row_count = lax.axis_size("rows")
    feat_count = lax.axis_size("feat")
    row_index = lax.axis_index("rows")
    feat_index = lax.axis_index("feat")
    n, block_width = features.shape
    if paired(row_count, feat_count, n, block_width):
        return by_lines(features, labels, posterior, prior_prec)
    col_width = block_width * feat_count // row_count
    partial_value = jnp.dot(features, posterior, preferred_element_type=jnp.float32)
    padded = -(-n // 512) * 512
    stats = jnp.concatenate([
        jnp.pad(partial_value, (0, padded - n)),
        jnp.pad(labels.astype(jnp.float32), (0, padded - n)),
    ]).reshape(-1, 128)
    all_rows, column_rows, all_stats = gather(features, stats)
    all_stats = all_stats.reshape(row_count, feat_count, 2, padded)[..., :n]
    margins = jnp.sum(all_stats[:, :, 0], axis=1).reshape(-1)
    all_labels = all_stats[:, 0, 1].reshape(-1)
    chance = jax.nn.sigmoid(margins)
    weight = (chance * (1.0 - chance)).astype(jnp.bfloat16)
    residual = (all_labels - chance).astype(jnp.bfloat16)
    summed = jnp.dot(residual, all_rows, preferred_element_type=jnp.float32)
    gradient = summed - prior_prec * posterior.astype(jnp.float32)
    weighted = weight[:, None] * all_rows
    product = lax.dot_general(
        weighted, column_rows, (((0,), (0,)), ((), ())), preferred_element_type=jnp.float32
    )
    global_rows = feat_index * block_width + jnp.arange(block_width, dtype=jnp.int32)
    global_cols = row_index * col_width + jnp.arange(col_width, dtype=jnp.int32)
    on_diagonal = global_rows[:, None] == global_cols[None, :]
    hessian = product + jnp.where(on_diagonal, prior_prec[:, None], jnp.float32(0.0))
    return (hessian, gradient)


def solution(mesh):
    in_specs = (P("rows", "feat"), P("rows"), P("feat"), P("feat"))
    out_specs = (P("feat", "rows"), P("feat"))
    return jax.shard_map(
        per_device, mesh=mesh, in_specs=in_specs, out_specs=out_specs, check_vma=False
    )
```

```python
import functools

import jax
import jax.numpy as jnp
from jax import lax
from jax.experimental import pallas as pl
from jax.experimental.pallas import tpu as pltpu
from jax.sharding import PartitionSpec as P

MESH = pl.DeviceIdType.MESH
SPLIT = 2
CHUNK = 16
PIECES = 4
TILE = 512
PART = 256
AHEAD = 2
LATE = 4
VMEM_BUDGET = 60 * 1024 * 1024


def pick(p, q, e):
    first = jnp.where((p ^ 1) == e, p ^ 2, p ^ 1)
    second = jnp.where(((p ^ 1) == e) | ((p ^ 2) == e), p ^ 3, p ^ 2)
    return jnp.where(q == 0, p, jnp.where(q == 1, first, second))


def passed_chip(p, z, last):
    return jnp.where(p > z, 0, jnp.where(p < z, last, p ^ 3))


def slabs(ref, lead, starts, size, cols):
    parts = []
    for start in starts:
        rows = pl.ds(pl.multiple_of(start, 16), size)
        parts.append(ref[rows, cols] if lead is None else ref[lead, rows, cols])
    return jnp.concatenate(parts, axis=0)


def wide(value, width):
    return jnp.concatenate([value] * (width // value.shape[1]), axis=1)


def weigh(all_ref, wr_ref, starts, size, cols):
    x = slabs(all_ref, None, starts, size, cols)
    weight = slabs(wr_ref, 0, starts, size, slice(None))
    residual = slabs(wr_ref, 1, starts, size, slice(None)).astype(jnp.float32)
    pulled = x.astype(jnp.float32) * wide(residual, PART)
    pulled = jnp.sum(pulled.reshape(-1, 8, PART), axis=0)
    return (x * wide(weight, PART)).T, pulled


def line_kernel(
    row_count, feat_count, x_ref, label_ref, post_ref, prec_ref,
    h_ref, turned_out, pull_out,
    all_ref, col_ref, wr_ref, gacc_ref, kept, even, odd, abuf, st_ref, stat_ref,
    agr, pr, br, ar, adr, own_s, relay_s, extra_s, part_s, src_s, bf_s, af_s, ad_s,
    side_r, side_s, ss, sr, ts, tr, lsem,
):
    r = lax.axis_index("rows")
    z = lax.axis_index("feat")
    p, c = r // 2, r % 2
    last = feat_count - 1
    n, width = x_ref.shape
    half = width // 2
    m = CHUNK
    nch = n // m
    items = last
    big = n // PIECES
    pace = nch // (3 * PIECES)
    avoid = jnp.where(z == 0, 0, jnp.where(z == last, last, -8))
    relays = p != avoid
    relays_all = (p ^ last) == avoid
    has_down, has_up = z >= 1, z <= last - 1

    def rows_of(chip, core, j):
        return pl.ds(pl.multiple_of((chip * 2 + core) * n + j * m, m), m)

    def own_rows(j):
        return pl.ds(pl.multiple_of(j * m, m), m)

    def big_rows(chip, core, j):
        return pl.ds(pl.multiple_of((chip * 2 + core) * n + j * big, 16), big)

    def cols_of(h):
        return pl.ds(pl.multiple_of(h * half, half), half)

    def remote(src, dst, send, recv, **where):
        return pltpu.make_async_remote_copy(
            src_ref=src, dst_ref=dst, send_sem=send, recv_sem=recv,
            device_id=where, device_id_type=MESH,
        )

    barrier = pltpu.get_barrier_semaphore()
    for d in range(1, row_count):
        pl.semaphore_signal(
            barrier, inc=1, device_id={"rows": lax.rem(r + d, row_count)},
            device_id_type=MESH,
        )
    for d in range(1, feat_count):
        for other in (r, r ^ 1):
            pl.semaphore_signal(
                barrier, inc=1,
                device_id={"rows": other, "feat": lax.rem(z + d, feat_count)},
                device_id_type=MESH,
            )

    own = pltpu.make_async_copy(
        x_ref, all_ref.at[pl.ds(pl.multiple_of(r * n, n), n)], lsem.at[1]
    )
    own.start()
    own.wait()
    st_ref[...] = jnp.zeros_like(st_ref)
    post = post_ref[...].astype(jnp.float32)
    for t in range(-(-n // 128)):
        count = min(128, n - 128 * t)
        here = pl.ds(128 * t, count)
        st_ref[8 + t:9 + t, 0:count] = label_ref[:, here].astype(jnp.float32)
        rows = pl.ds(pl.multiple_of(r * n + 128 * t, 16), count)

        total = jnp.zeros((count, 128), jnp.float32)
        for i in range(width // 128):
            value = all_ref[rows, pl.ds(128 * i, 128)].astype(jnp.float32)
            total = total + value * post[i:i + 1, :]
        st_ref[t:t + 1, 0:count] = jnp.sum(total.T, axis=0, keepdims=True)
    gacc_ref[...] = jnp.zeros_like(gacc_ref)
    for t in range(width // 128):
        lanes = pl.ds(128 * t, 128)
        gacc_ref[0:1, lanes] = -prec_ref[:, lanes] * post[t:t + 1, :]
    pl.semaphore_wait(barrier, row_count - 1 + 2 * (feat_count - 1))

    def ag(dim, h, j, src, chip, rel, send):
        remote(
            src, all_ref.at[big_rows(chip, c, j), cols_of(h)],
            send, agr.at[rel, h, j], rows=r ^ (2 * dim),
        ).start()

    def own_plane(s):
        j = lax.rem(s, PIECES)
        rows = pl.ds(pl.multiple_of(j * big, 16), big)

        @pl.when(s < PIECES)
        def _():
            ag(1, 0, j, x_ref.at[rows, cols_of(0)], p, 0, own_s.at[0])
            ag(2, 1, j, x_ref.at[rows, cols_of(1)], p, 1, own_s.at[1])

        @pl.when(s >= PIECES)
        def _():
            ag(1, 1, j, x_ref.at[rows, cols_of(1)], p, 0, own_s.at[0])
            ag(2, 0, j, x_ref.at[rows, cols_of(0)], p, 1, own_s.at[1])

    def own_line(j):
        for h in range(2):
            src = x_ref.at[own_rows(j), cols_of(h)]

            @pl.when(has_down & (p == 0))
            def _():
                remote(
                    src, abuf.at[z - 1, c, own_rows(j)], own_s.at[2], ar.at[0, c, j],
                    rows=2 * p + h, feat=z - 1,
                ).start()

            @pl.when(has_down & (p == z))
            def _():
                remote(
                    src, col_ref.at[rows_of(p, c, j)], own_s.at[2], br.at[0, c, j],
                    rows=2 * p + h, feat=z - 1,
                ).start()

            @pl.when(has_up & (p == last))
            def _():
                remote(
                    src, abuf.at[z, c, own_rows(j)], own_s.at[3], ar.at[0, c, j],
                    rows=2 * p + h, feat=z + 1,
                ).start()

            @pl.when(has_up & (p == z))
            def _():
                remote(
                    src, col_ref.at[rows_of(p, c, j)], own_s.at[3], br.at[0, c, j],
                    rows=2 * p + h, feat=z + 1,
                ).start()

    def own_sends(j, _):
        own_line(j)

        @pl.when(lax.rem(j, 3 * pace) == 0)
        def _():
            own_plane(2 * (j // (3 * pace)))
            own_plane(2 * (j // (3 * pace)) + 1)
        return 0

    own_sends(0, 0)
    remote(
        x_ref, all_ref.at[pl.ds(pl.multiple_of(r * n, n), n)], part_s.at[3], pr.at[3],
        rows=r ^ 1,
    ).start()

    stat_local = pltpu.make_async_copy(st_ref, stat_ref.at[r, z], lsem.at[0])
    stat_local.start()
    for d in range(1, feat_count):
        remote(
            st_ref, stat_ref.at[r, z], ss.at[d], sr.at[d],
            feat=lax.rem(z + d, feat_count),
        ).start()

    def share_stats():
        stat_local.wait()
        for d in range(1, feat_count):
            remote(
                st_ref, stat_ref.at[r, lax.rem(z + feat_count - d, feat_count)],
                ss.at[d], sr.at[d], feat=z,
            ).wait_recv()
        for d in range(1, row_count):
            remote(
                stat_ref.at[r], stat_ref.at[r], ts.at[d], tr.at[d],
                rows=lax.rem(r + d, row_count),
            ).start()

    def weights():
        for d in range(1, row_count):
            origin = lax.rem(r + row_count - d, row_count)
            remote(
                stat_ref.at[origin], stat_ref.at[origin], ts.at[d], tr.at[d], rows=r
            ).wait_recv()

        def one(i, _):
            margins = stat_ref[i, 0, 0:8]
            for f in range(1, feat_count):
                margins = margins + stat_ref[i, f, 0:8]
            chance = 1.0 / (1.0 + jnp.exp(-margins))
            weight = (chance * (1.0 - chance)).astype(jnp.bfloat16)
            residual = (stat_ref[i, 0, 8:16] - chance).astype(jnp.bfloat16)
            for lead, value in ((0, weight), (1, residual)):
                turned = value.astype(jnp.float32).T
                for t in range(-(-n // 128)):
                    count = min(128, n - 128 * t)
                    rows = pl.ds(pl.multiple_of(i * n + 128 * t, 16), count)
                    wr_ref[lead, rows, :] = jnp.broadcast_to(
                        turned[:count, t:t + 1], (count, 128)
                    ).astype(jnp.bfloat16)
            return 0

        lax.fori_loop(0, row_count, one, 0)

    def arrive(rel, h, j):
        chip = p ^ (rel + 1)
        here = all_ref.at[big_rows(chip, c, j), cols_of(h)]
        remote(here, here, own_s.at[0], agr.at[rel, h, j], rows=r).wait_recv()
        remote(here, here, part_s.at[rel], pr.at[rel], rows=r ^ 1).start()

    def forward(rel, h, j, send):
        chip = p ^ (rel + 1)
        here = all_ref.at[big_rows(chip, c, j), cols_of(h)]
        ag(2 - rel, h, j, here, chip, 2, send)

    def gather_event(s):
        a, j = s // PIECES, s % PIECES

        @pl.when(a == 0)
        def _():
            arrive(0, 0, j)

            @pl.when(relays)
            def _():
                forward(0, 0, j, relay_s.at[0])
            arrive(1, 1, j)

            @pl.when(relays)
            def _():
                forward(1, 1, j, relay_s.at[1])

        @pl.when(a == 1)
        def _():
            arrive(0, 1, j)

            @pl.when(relays_all)
            def _():
                forward(0, 1, j, extra_s.at[0])
            arrive(1, 0, j)

            @pl.when(relays_all)
            def _():
                forward(1, 0, j, extra_s.at[1])

    def corner_event(j):
        arrive(2, 0, j)
        arrive(2, 1, j)

    def source_event(s):
        q, j = 1 + s // nch, s % nch
        for h in range(2):
            @pl.when(has_down)
            def _():
                where = rows_of(pick(p, q, 0), c, j)
                remote(
                    all_ref.at[where, cols_of(h)], col_ref.at[where],
                    src_s.at[0, q], br.at[q, c, j], rows=2 * p + h, feat=z - 1,
                ).start()

            @pl.when(has_up)
            def _():
                where = rows_of(pick(p, q, last), c, j)
                remote(
                    all_ref.at[where, cols_of(h)], col_ref.at[where],
                    src_s.at[1, q], br.at[q, c, j], rows=2 * p + h, feat=z + 1,
                ).start()

    def column_event(s):
        q, j = s // nch, s % nch
        down = p > z
        chip = pick(p, q, jnp.where(down, 0, last))
        for k in range(2):
            here = col_ref.at[rows_of(chip, k, j)]
            remote(here, here, bf_s.at[q], br.at[q, k, j], rows=r).wait_recv()

            rest = (s < items * nch - 1) | ((p != 0) & (p != last))

            @pl.when(((down & has_down) | (~down & has_up)) & rest)
            def _():
                remote(
                    here, here, bf_s.at[q], br.at[q, k, j],
                    feat=jnp.where(down, z - 1, z + 1),
                ).start()

    side_down, side_up = (p ^ 2) == last, p == 2
    side_first = (side_down & (z == last)) | (side_up & (z == 0))
    side_later = (side_down & (z < last)) | (side_up & (z > 0))
    side_more = (side_down & has_down) | (side_up & has_up)
    side_give = (side_down & (z <= last - 2)) | (side_up & (z >= 2))
    side_next = jnp.where(side_down, z - 1, z + 1)
    side_rows = own_rows(nch - 1)

    def side_own():
        for h in range(2):
            remote(
                x_ref.at[side_rows, cols_of(h)], abuf.at[0, c, side_rows],
                side_s.at[0], side_r.at[c], rows=2 * p + h, feat=side_next,
            ).start()

    def side_event():
        for k in range(2):
            here = abuf.at[0, k, side_rows]
            remote(here, here, side_s.at[1], side_r.at[k], rows=r).wait_recv()

            @pl.when(side_more)
            def _():
                remote(here, here, side_s.at[1], side_r.at[k], feat=side_next).start()

            @pl.when(side_give)
            def _():
                remote(
                    here, col_ref.at[rows_of(p, k, nch - 1)], side_s.at[2],
                    br.at[items - 1, k, nch - 1], rows=2 * (p ^ 2) + c,
                ).start()

    def pass_event(s):
        q, j = s // nch, s % nch
        down = p == 0
        block = jnp.where(down, z + 1 + q, z - 1 - q)
        slot = jnp.where(down, block - 1, block)

        @pl.when((block >= 0) & (block <= last))
        def _():
            for k in range(2):
                here = abuf.at[slot, k, own_rows(j)]
                remote(here, here, af_s.at[q], ar.at[q, k, j], rows=r).wait_recv()

                @pl.when((down & has_down) | (~down & has_up))
                def _():
                    remote(
                        here, here, af_s.at[q], ar.at[q + 1, k, j],
                        feat=jnp.where(down, z - 1, z + 1),
                    ).start()

    def deliver_event(s):
        q, j = s // nch, s % nch
        down = p == 0
        block = jnp.where(down, z + 1 + q, z - 1 - q)
        slot = jnp.where(down, block - 1, block)

        @pl.when((block >= 0) & (block <= last))
        def _():
            for k in range(2):
                remote(
                    abuf.at[slot, k, own_rows(j)], col_ref.at[rows_of(p, k, j)],
                    ad_s.at[q], adr.at[j // (nch // 3)], rows=2 * block + c,
                ).start()

    lag = 10 * pace
    tiles = width // TILE
    edge = passed_chip(p, z, last)
    twice = col_ref.at[pl.ds(0, 2 * n)]
    third = n // 3
    once = col_ref.at[pl.ds(0, 2 * third)]
    q = nch // 3
    begins = [2 * q + 1, 4 * q + 1, 5 * q + 1, 6 * q, 7 * q, 8 * q]
    ends = [4 * q - 1, 5 * q + 1, 6 * q, 7 * q, 8 * q, 9 * q - pace]
    near, far = pick(p, 1, edge), pick(p, 2, edge)

    def partner_rows(chip):
        rel = jnp.where(chip == p, 3, (p ^ chip) - 1)
        there = all_ref.at[pl.ds(pl.multiple_of((2 * chip + 1 - c) * n, n), n)]
        remote(there, there, part_s.at[rel], pr.at[rel], rows=r).wait_recv()

        @pl.when(p == z)
        def _():
            rows = pl.ds(pl.multiple_of(chip * 2 * n, n), 2 * n)
            copy = pltpu.make_async_copy(
                all_ref.at[rows, cols_of(c)], col_ref.at[rows], lsem.at[2]
            )
            copy.start()
            copy.wait()

    def prepare(i):
        rows = pl.ds(pl.multiple_of(i * TILE, TILE), TILE)
        h_ref[rows, :] = jnp.zeros((TILE, half), jnp.float32)
        offset = i * TILE - c * half

        @pl.when((p == z) & (offset >= 0) & (offset < half))
        def _():
            cols = pl.ds(pl.multiple_of(offset, TILE), TILE)
            shape = (TILE, TILE)
            same = lax.broadcasted_iota(jnp.int32, shape, 0) == lax.broadcasted_iota(
                jnp.int32, shape, 1
            )
            h_ref[rows, cols] = jnp.where(
                same, jnp.broadcast_to(prec_ref[:, rows], shape), 0.0
            )

    def unit_rows(index):
        def start(chip, core, piece):
            return (chip * 2 + core) * n + piece * third

        late = jnp.where(index == 2, 2, index - 4 + (index == 3))
        rows = []
        for i in range(4):
            core, upper = i % 2, i // 2
            pair = jnp.where(
                index == 0, start(p, core, upper),
                jnp.where(
                    index == 1, start(near if upper else p, core, 0 if upper else 2),
                    start(near, core, 1 + upper),
                ),
            )
            far_rows = start(edge if upper else far, core, late)
            rows.append(jnp.where((index == 0) | (index == 1) | (index == 3), pair, far_rows))
        return rows

    def part_of(i):
        return pl.ds(pl.multiple_of(i * PART, PART), PART)

    def turn(rows, i, flag):
        weighted, pulled = weigh(all_ref, wr_ref, rows, third, part_of(i))
        gacc_ref[:, part_of(i)] += pulled * flag
        return weighted

    def multiply(turned, rows, i):
        value = turned[...]
        for t in range(half // TILE):
            there = pl.ds(t * TILE, TILE)
            h_ref[part_of(i), there] += jnp.dot(
                value, slabs(col_ref, None, rows, third, there),
                preferred_element_type=jnp.float32,
            )

    def compute(u):
        index = sum((u >= s).astype(jnp.int32) for s in begins) - 1

        def choose(values):
            out = values[0]
            for i in range(1, len(values)):
                out = jnp.where(index >= i, values[i], out)
            return out

        begin, span = choose(begins), choose([e - s for s, e in zip(begins, ends)])
        span = jnp.where((index >= 3) & (p != z) & ((z == 0) | (z == last)), span - pace, span)
        low = jnp.minimum((u - begin) * tiles // span, tiles)
        high = jnp.minimum((u - begin + 1) * tiles // span, tiles)
        rows = unit_rows(index)

        @pl.when(u == begin)
        def _():
            @pl.when(index == 0)
            def _():
                weights()
                partner_rows(p)

            @pl.when(index == 1)
            def _():
                partner_rows(near)

            @pl.when(index == 2)
            def _():
                partner_rows(far)
                partner_rows(edge)

            @pl.when((index >= 4) & (p != z))
            def _():
                remote(once, once, bf_s.at[0], adr.at[index - 4], rows=r).wait_recv()

            @pl.when(index != 2)
            def _():
                even[...] = turn(rows, 0, 1.0)

        def keep(i, _):
            for e in range(2):
                kept[part_of(2 * i + e), :] = turn(rows, 2 * i + e, 1.0)
            return 0

        def pair(i, _):
            multiply(even, rows, 2 * i)
            odd[...] = turn(rows, 2 * i + 1, 1.0)
            multiply(odd, rows, 2 * i + 1)
            more = i < tiles - 1
            even[...] = turn(
                rows, jnp.where(more, 2 * i + 2, 0), jnp.where(more, 1.0, 0.0)
            )
            return 0

        @pl.when(index == 2)
        def _():
            lax.fori_loop(low, high, keep, 0)

            @pl.when(u == ends[2] - 1)
            def _():
                pltpu.make_async_copy(kept, turned_out, lsem.at[3]).start()
                depth = 4 * third
                cut = PART * depth // half
                for i in range(half // depth):
                    h_ref[pl.ds(width + depth, cut), pl.ds(i * depth, depth)] = kept[
                        pl.ds(i * cut, cut), :
                    ].astype(jnp.float32)

        @pl.when(index != 2)
        def _():
            lax.fori_loop(low, high, pair, 0)

        @pl.when(u == ends[-1] - 1)
        def _():
            pltpu.make_async_copy(gacc_ref, pull_out, lsem.at[4]).start()

    def some(event, low, high):
        def one(i, _):
            event(i)
            return 0
        lax.fori_loop(low, high, one, 0)

    def step(u, _):
        @pl.when(u < begins[0])
        def _():
            per = -(-tiles // begins[0])
            some(prepare, jnp.minimum(u * per, tiles), jnp.minimum(u * per + per, tiles))

        @pl.when((u >= begins[0]) & (u < ends[-1]))
        def _():
            compute(u)

        @pl.when((p != z) & (u < items * nch))
        def _():
            column_event(u)

        @pl.when(u == 2)
        def _():
            share_stats()

        @pl.when(u < 2)
        def _():
            some(lambda j: own_sends(j, 0), 1 + AHEAD * u, 1 + AHEAD * (u + 1))

        @pl.when(u >= 2)
        def _():
            low = 1 + 2 * AHEAD + 3 * (u - 2)
            some(
                lambda j: own_sends(j, 0), jnp.minimum(low, nch), jnp.minimum(low + 3, nch)
            )

        @pl.when((u == 0) & side_first)
        def _():
            side_own()
        hops = jnp.where(side_down, last - z, z)

        @pl.when((u == 3 * hops + 4) & side_later)
        def _():
            side_event()
        for e in range(2):
            i = u - (4 + 2 * e) * pace

            @pl.when((i >= 0) & (i % (3 * pace) == 0) & (i < 3 * pace * PIECES))
            def _():
                gather_event(2 * (i // (3 * pace)) + e)

        corner = u - 4 * q - 1

        @pl.when((corner >= 0) & (corner < q) & (corner % pace == 0))
        def _():
            corner_event(corner // pace)

        @pl.when((p == z) & (u >= lag) & (u < lag + 2 * nch))
        def _():
            source_event(u - lag)

        @pl.when(((p == 0) | (p == last)) & (u >= LATE) & (u < LATE + items * nch))
        def _():
            pass_event(u - LATE)

        @pl.when(((p == 0) | (p == last)) & (u >= nch))
        def _():
            low = jnp.minimum(2 * (u - nch), u - LATE)
            some(deliver_event, low, jnp.minimum(2 * (u + 1 - nch), u + 1 - LATE))
        return 0

    lax.fori_loop(0, items * nch + LATE, step, 0)

    @pl.when(p != z)
    def _():
        remote(once, once, bf_s.at[0], adr.at[2], rows=r).wait_recv()

    for i, start in enumerate(unit_rows(jnp.int32(2))):
        held = col_ref[pl.ds(pl.multiple_of(start, 16), third), :]
        h_ref[pl.ds(width + i * third, third), :] = held.astype(jnp.float32)

    def sent(ref, sem):
        remote(ref, ref, sem, pr.at[3], rows=r).wait_send()

    for d in range(1, feat_count):
        sent(st_ref, ss.at[d])
    for d in range(1, row_count):
        sent(stat_ref.at[r], ts.at[d])
    for i in range(2):
        sent(x_ref, own_s.at[i])

        @pl.when(relays)
        def _():
            sent(x_ref.at[:, pl.ds(0, half)], relay_s.at[i])

        @pl.when(relays_all)
        def _():
            sent(x_ref.at[:, pl.ds(0, half)], extra_s.at[i])

    @pl.when(has_down & ((p == 0) | (p == z)))
    def _():
        sent(x_ref, own_s.at[2])

    @pl.when(has_up & ((p == last) | (p == z)))
    def _():
        sent(x_ref, own_s.at[3])
    for rel in range(4):
        sent(x_ref, part_s.at[rel])
    @pl.when(side_first)
    def _():
        sent(x_ref.at[pl.ds(0, m)], side_s.at[0])

    @pl.when(side_later & side_more)
    def _():
        sent(col_ref.at[pl.ds(0, 2 * m)], side_s.at[1])

    @pl.when(side_later & side_give)
    def _():
        sent(col_ref.at[pl.ds(0, 2 * m)], side_s.at[2])
    down = p > z
    for q in range(items):
        if q > 0:
            @pl.when((p == z) & has_down)
            def _():
                sent(x_ref, src_s.at[0, q])

            @pl.when((p == z) & has_up)
            def _():
                sent(x_ref, src_s.at[1, q])

        sends = (p != z) & ((down & has_down) | (~down & has_up))
        short = ((p == 0) | (p == last)) if q == items - 1 else p < 0

        @pl.when(sends & ~short)
        def _():
            sent(twice, bf_s.at[q])

        @pl.when(sends & short)
        def _():
            sent(col_ref.at[pl.ds(0, 2 * n - 2 * m)], bf_s.at[q])
        for edge, block, more in ((0, z + 1 + q, has_down), (last, z - 1 - q, has_up)):
            @pl.when((p == edge) & (block >= 0) & (block <= last))
            def _():
                sent(twice, ad_s.at[q])

                @pl.when(more)
                def _():
                    sent(twice, af_s.at[q])
    pltpu.make_async_copy(gacc_ref, pull_out, lsem.at[4]).wait()
    pltpu.make_async_copy(kept, turned_out, lsem.at[3]).wait()


def extra_rows(n, half):
    depth = 4 * n // 3
    return depth + PART * depth // half


def line_stage(features, labels, post, prec):
    row_count = lax.axis_size("rows")
    feat_count = lax.axis_size("feat")
    n, width = features.shape
    half = width // 2
    items = feat_count - 1
    nch = n // CHUNK
    dma = pltpu.SemaphoreType.DMA
    return pl.pallas_call(
        functools.partial(line_kernel, row_count, feat_count),
        out_shape=(
            pltpu.VMEM((width + extra_rows(n, half), half), jnp.float32),
            pltpu.HBM((width, 4 * n // 3), features.dtype),
            pltpu.HBM((8, width), jnp.float32),
        ),
        in_specs=[
            pl.BlockSpec(memory_space=pl.ANY), pl.BlockSpec(memory_space=pltpu.VMEM),
            pl.BlockSpec(memory_space=pltpu.VMEM), pl.BlockSpec(memory_space=pltpu.VMEM),
        ],
        out_specs=[pl.BlockSpec(memory_space=pltpu.VMEM)]
        + [pl.BlockSpec(memory_space=pl.ANY)] * 2,
        scratch_shapes=[
            pltpu.VMEM((row_count * n, width), features.dtype),
            pltpu.VMEM((row_count * n, half), features.dtype),
            pltpu.VMEM((2, row_count * n, 128), features.dtype),
            pltpu.VMEM((8, width), jnp.float32),
            pltpu.VMEM((width, 4 * n // 3), features.dtype),
            pltpu.VMEM((PART, 4 * n // 3), features.dtype),
            pltpu.VMEM((PART, 4 * n // 3), features.dtype),
            pltpu.VMEM((items, 2, n, half), features.dtype),
            pltpu.VMEM((16, 128), jnp.float32),
            pltpu.VMEM((row_count, feat_count, 16, 128), jnp.float32),
            dma((3, 2, PIECES)), dma((4,)), dma((items, 2, nch)), dma((items + 1, 2, nch)),
            dma((3,)),
            dma((4,)), dma((2,)), dma((2,)), dma((4,)), dma((2, items)), dma((items,)),
            dma((items,)), dma((items,)), dma((2,)), dma((3,)),
            dma((feat_count,)), dma((feat_count,)),
            dma((row_count,)), dma((row_count,)),
            dma((9,)),
        ],
        compiler_params=pltpu.CompilerParams(
            collective_id=0, has_side_effects=True, vmem_limit_bytes=28 * 1024 * 1024
        ),
        name="line_stage",
    )(features, labels, post, prec)


def last_kernel(
    h_ref, turned_ref, gacc_ref,
    out_ref, grad_ref, stage, turned, cols, gacc, grad, sem, lsem, tsem,
):
    width, half = out_ref.shape
    slots = stage.shape[0]
    count = width // PART

    def part_of(i):
        return pl.ds(pl.multiple_of(i * PART, PART), PART)

    def take(i):
        return pltpu.make_async_copy(
            turned_ref.at[part_of(i)], turned.at[part_of(i)], tsem.at[i]
        )

    def put(i):
        slot = lax.rem(i, slots)
        return pltpu.make_async_copy(stage.at[slot], out_ref.at[part_of(i)], sem.at[slot])

    for i in range(1, count):
        take(i).start()
    late = pltpu.make_async_copy(gacc_ref, gacc, lsem.at[1])
    late.start()
    depth = cols.shape[0]
    cut = PART * depth // half
    cols[...] = h_ref[pl.ds(width, depth), :].astype(cols.dtype)
    for i in range(half // depth):
        turned[pl.ds(i * cut, cut), :] = h_ref[
            pl.ds(width + depth, cut), pl.ds(i * depth, depth)
        ].astype(turned.dtype)

    def one(i, _):
        @pl.when(i >= slots)
        def _():
            put(i - slots).wait()
        @pl.when(i >= 1)
        def _():
            take(i).wait()
        slot = lax.rem(i, slots)
        value = turned[part_of(i), :]
        for t in range(half // TILE):
            there = pl.ds(t * TILE, TILE)
            stage[slot, :, there] = h_ref[part_of(i), there] + jnp.dot(
                value, cols[:, there], preferred_element_type=jnp.float32
            )
        put(i).start()
        return 0

    lax.fori_loop(0, count, one, 0)
    late.wait()
    grad[...] = jnp.sum(gacc[...], axis=0, keepdims=True)
    give = pltpu.make_async_copy(grad, grad_ref, lsem.at[2])
    give.start()
    for i in range(max(0, count - slots), count):
        put(i).wait()
    give.wait()


def last_stage(h, turned, gacc):
    width, half = turned.shape[0], h.shape[1]
    dma = pltpu.SemaphoreType.DMA
    h = pltpu.with_memory_space_constraint(h, pltpu.VMEM)
    kept = [pltpu.with_memory_space_constraint(a, pltpu.HBM) for a in (turned, gacc)]
    return pl.pallas_call(
        last_kernel,
        out_shape=(
            pltpu.HBM((width, half), jnp.float32),
            pltpu.HBM((1, width), jnp.float32),
        ),
        in_specs=[pl.BlockSpec(memory_space=pltpu.VMEM)]
        + [pl.BlockSpec(memory_space=pl.ANY)] * 2,
        out_specs=[pl.BlockSpec(memory_space=pl.ANY)] * 2,
        scratch_shapes=[
            pltpu.VMEM((3, PART, half), jnp.float32),
            pltpu.VMEM(turned.shape, turned.dtype),
            pltpu.VMEM((turned.shape[1], half), turned.dtype),
            pltpu.VMEM(gacc.shape, gacc.dtype),
            pltpu.VMEM((1, width), jnp.float32),
            dma((3,)), dma((3,)), dma((width // PART,)),
        ],
        compiler_params=pltpu.CompilerParams(vmem_limit_bytes=14 * 1024 * 1024),
        name="last_stage",
    )(h, *kept)


def paired(row_count, feat_count, n, width):
    half = width // 2
    rows = row_count * n
    held = 4 * width * half + 2 * rows * (width + half + 256) + 12 * n * half + 4 * n * width
    return (
        row_count == 2 * feat_count and (feat_count - 1).bit_length() == 2
        and feat_count & (feat_count - 1) == 0 and n % (3 * PIECES * CHUNK) == 0 and n // CHUNK >= 2 * AHEAD + 1
        and half % (4 * n // 3) == 0 and PART * (4 * n // 3) % (16 * half) == 0
        and n <= 1024 and half % TILE == 0 and held <= VMEM_BUDGET
    )


def by_lines(features, labels, posterior, prior_prec):
    n, width = features.shape
    held = line_stage(
        features, labels.reshape(1, n), posterior.reshape(width // 128, 128),
        prior_prec.reshape(1, width),
    )
    hessian, gradient = last_stage(*held)
    return (hessian, gradient.reshape(width))


def gather_kernel(
    row_count, feat_count, x_ref, st_ref, all_ref, col_ref, stat_ref,
    ring, zs, zr, ps, pr, ds, dr, cs, cr, cl, ss, sr, ts, tr, lsem,
):
    r = lax.axis_index("rows")
    f = lax.axis_index("feat")
    n, width = x_ref.shape
    half = width // 2
    col_width = col_ref.shape[1]
    unit = min(col_width, half)
    per_half = half // unit
    per_owner = col_width // unit
    chips = row_count // 2
    bits = chips.bit_length() - 1
    part = n // SPLIT

    def rows_of(device):
        return pl.ds(pl.multiple_of(device * n, n), n)

    def remote(src, dst, send, recv, **where):
        return pltpu.make_async_remote_copy(
            src_ref=src, dst_ref=dst, send_sem=send, recv_sem=recv,
            device_id=where, device_id_type=MESH,
        )

    sends = []

    def go(copy):
        copy.start()
        sends.append(copy)

    def ring_slice(step, h, k):
        rows, cols = pl.ds(k * part, part), pl.ds(h * half, half)
        return x_ref.at[rows, cols] if step == 0 else ring.at[step - 1, rows, cols]

    def ring_copy(step, h, k):
        to = lax.rem(f + (1 if h == 0 else feat_count - 1), feat_count)
        return remote(
            ring_slice(step, h, k),
            ring.at[step, pl.ds(k * part, part), pl.ds(h * half, half)],
            zs.at[step, h, k], zr.at[step, h, k], feat=to,
        )

    def column_sends(step, h, k, start):
        block = lax.rem(f + (feat_count - step if h == 0 else step), feat_count)
        for u in range(per_half):
            inner = h * half + u * unit
            if width % col_width == 0:
                owner = block * (width // col_width) + inner // col_width
                offset = inner % col_width
                slot = offset // unit
            else:
                owner = (block * width + inner) // col_width
                slot = ((block * width + inner) % col_width) // unit
                offset = pl.multiple_of(slot * unit, unit)
            src = ring_slice(step, h, k).at[:, pl.ds(u * unit, unit)]
            dst = col_ref.at[
                pl.ds(pl.multiple_of(r * n + k * part, part), part), pl.ds(offset, unit)
            ]
            send = cs.at[step, h, k, u]

            @pl.when(owner != r)
            def _():
                copy = remote(src, dst, send, cr.at[r, slot, k], rows=owner)
                copy.start() if start else copy.wait_send()

            if start:
                @pl.when(owner == r)
                def _():
                    pltpu.make_async_copy(src, dst, cl.at[slot, k]).start()

    def order(h):
        return list(range(bits)) if h == 0 else list(range(bits))[::-1]

    def spread(h, stage, mask):
        bit = 1 << order(h)[stage]
        origin = r ^ (2 * mask)
        cols = pl.ds(h * half, half)
        src = x_ref.at[:, cols] if mask == 0 else all_ref.at[rows_of(origin), cols]
        return remote(
            src, all_ref.at[rows_of(origin), cols],
            ps.at[h, mask | bit], pr.at[h, mask | bit], rows=r ^ (2 * bit),
        )

    def partner(h, mask):
        origin = r ^ (2 * mask)
        cols = pl.ds(h * half, half)
        src = x_ref.at[:, cols] if mask == 0 else all_ref.at[rows_of(origin), cols]
        return remote(
            src, all_ref.at[rows_of(origin), cols],
            ds.at[h, mask], dr.at[h, mask], rows=r ^ 1,
        )

    def masks_before(h, stage):
        found = [0]
        for b in order(h)[:stage]:
            found += [m | (1 << b) for m in found]
        return found

    for k in range(SPLIT):
        for h in range(2):
            go(ring_copy(0, h, k))
    stat_local = pltpu.make_async_copy(st_ref, stat_ref.at[r, f], lsem.at[0])
    stat_local.start()
    for d in range(1, feat_count):
        go(remote(
            st_ref, stat_ref.at[r, f], ss.at[d], sr.at[d],
            feat=lax.rem(f + d, feat_count),
        ))
    for stage in range(bits):
        for h in range(2):
            go(spread(h, stage, 0))
    for h in range(2):
        go(partner(h, 0))
    own = pltpu.make_async_copy(x_ref, all_ref.at[rows_of(r)], lsem.at[1])
    own.start()
    for k in range(SPLIT):
        for h in range(2):
            column_sends(0, h, k, True)

    stat_local.wait()
    for d in range(1, feat_count):
        remote(
            st_ref, stat_ref.at[r, lax.rem(f + feat_count - d, feat_count)],
            ss.at[d], sr.at[d], feat=f,
        ).wait_recv()
    for d in range(1, row_count):
        go(remote(
            stat_ref.at[r], stat_ref.at[r], ts.at[d], tr.at[d],
            rows=lax.rem(r + d, row_count),
        ))

    def relay(stage):
        for h in range(2):
            bit = 1 << order(h)[stage]
            for m in masks_before(h, stage):
                mask = m | bit
                cols = pl.ds(h * half, half)
                remote(
                    x_ref.at[:, cols], all_ref.at[rows_of(r ^ (2 * mask)), cols],
                    ps.at[h, mask], pr.at[h, mask], rows=r,
                ).wait_recv()
                for later in range(stage + 1, bits):
                    go(spread(h, later, mask))
                go(partner(h, mask))

    for step in range(1, feat_count):
        for k in range(SPLIT):
            for h in range(2):
                ring_copy(step - 1, h, k).wait_recv()
                if step < feat_count - 1:
                    go(ring_copy(step, h, k))
                column_sends(step, h, k, True)
        if step <= bits:
            relay(step - 1)
    for stage in range(feat_count - 1, bits):
        relay(stage)

    for h in range(2):
        for mask in range(chips):
            cols = pl.ds(h * half, half)
            remote(
                x_ref.at[:, cols], all_ref.at[rows_of(r ^ (2 * mask) ^ 1), cols],
                ds.at[h, mask], dr.at[h, mask], rows=r,
            ).wait_recv()
    for d in range(1, row_count):
        origin = lax.rem(r + row_count - d, row_count)
        remote(
            stat_ref.at[origin], stat_ref.at[origin], ts.at[d], tr.at[d], rows=r
        ).wait_recv()
        for slot in range(per_owner):
            for k in range(SPLIT):
                dst = col_ref.at[
                    pl.ds(pl.multiple_of(origin * n + k * part, part), part),
                    pl.ds(slot * unit, unit),
                ]
                remote(
                    x_ref.at[pl.ds(0, part), pl.ds(0, unit)], dst,
                    cs.at[0, 0, 0, 0], cr.at[origin, slot, k], rows=r,
                ).wait_recv()
    for slot in range(per_owner):
        for k in range(SPLIT):
            dst = col_ref.at[
                pl.ds(pl.multiple_of(r * n + k * part, part), part),
                pl.ds(slot * unit, unit),
            ]
            pltpu.make_async_copy(
                x_ref.at[pl.ds(0, part), pl.ds(0, unit)], dst, cl.at[slot, k]
            ).wait()
    own.wait()
    for copy in sends:
        copy.wait_send()
    for step in range(feat_count):
        for k in range(SPLIT):
            for h in range(2):
                column_sends(step, h, k, False)


def gather(features, stats):
    row_count = lax.axis_size("rows")
    feat_count = lax.axis_size("feat")
    n, width = features.shape
    half = width // 2
    col_width = width * feat_count // row_count
    unit = min(col_width, half)
    chips = row_count // 2
    dma = pltpu.SemaphoreType.DMA
    return pl.pallas_call(
        functools.partial(gather_kernel, row_count, feat_count),
        out_shape=(
            jax.ShapeDtypeStruct((row_count * n, width), features.dtype),
            jax.ShapeDtypeStruct((row_count * n, col_width), features.dtype),
            jax.ShapeDtypeStruct((row_count, feat_count) + stats.shape, stats.dtype),
        ),
        in_specs=[pl.BlockSpec(memory_space=pltpu.VMEM)] * 2,
        out_specs=[pl.BlockSpec(memory_space=pl.ANY)] * 3,
        scratch_shapes=[
            pltpu.VMEM((feat_count - 1, n, width), features.dtype),
            dma((feat_count - 1, 2, SPLIT)), dma((feat_count - 1, 2, SPLIT)),
            dma((2, chips)), dma((2, chips)),
            dma((2, chips)), dma((2, chips)),
            dma((feat_count, 2, SPLIT, half // unit)),
            dma((row_count, col_width // unit, SPLIT)),
            dma((col_width // unit, SPLIT)),
            dma((feat_count,)), dma((feat_count,)),
            dma((row_count,)), dma((row_count,)),
            dma((2,)),
        ],
        compiler_params=pltpu.CompilerParams(
            has_side_effects=True, vmem_limit_bytes=32 * 1024 * 1024
        ),
        name="gather",
    )(features, stats)


def per_device(features, labels, posterior, prior_prec):
    row_count = lax.axis_size("rows")
    feat_count = lax.axis_size("feat")
    row_index = lax.axis_index("rows")
    feat_index = lax.axis_index("feat")
    n, block_width = features.shape
    if paired(row_count, feat_count, n, block_width):
        return by_lines(features, labels, posterior, prior_prec)
    col_width = block_width * feat_count // row_count
    partial_value = jnp.dot(features, posterior, preferred_element_type=jnp.float32)
    padded = -(-n // 512) * 512
    stats = jnp.concatenate([
        jnp.pad(partial_value, (0, padded - n)),
        jnp.pad(labels.astype(jnp.float32), (0, padded - n)),
    ]).reshape(-1, 128)
    all_rows, column_rows, all_stats = gather(features, stats)
    all_stats = all_stats.reshape(row_count, feat_count, 2, padded)[..., :n]
    margins = jnp.sum(all_stats[:, :, 0], axis=1).reshape(-1)
    all_labels = all_stats[:, 0, 1].reshape(-1)
    chance = jax.nn.sigmoid(margins)
    weight = (chance * (1.0 - chance)).astype(jnp.bfloat16)
    residual = (all_labels - chance).astype(jnp.bfloat16)
    summed = jnp.dot(residual, all_rows, preferred_element_type=jnp.float32)
    gradient = summed - prior_prec * posterior.astype(jnp.float32)
    weighted = weight[:, None] * all_rows
    product = lax.dot_general(
        weighted, column_rows, (((0,), (0,)), ((), ())), preferred_element_type=jnp.float32
    )
    global_rows = feat_index * block_width + jnp.arange(block_width, dtype=jnp.int32)
    global_cols = row_index * col_width + jnp.arange(col_width, dtype=jnp.int32)
    on_diagonal = global_rows[:, None] == global_cols[None, :]
    hessian = product + jnp.where(on_diagonal, prior_prec[:, None], jnp.float32(0.0))
    return (hessian, gradient)


def solution(mesh):
    in_specs = (P("rows", "feat"), P("rows"), P("feat"), P("feat"))
    out_specs = (P("feat", "rows"), P("feat"))
    return jax.shard_map(
        per_device, mesh=mesh, in_specs=in_specs, out_specs=out_specs, check_vma=False
    )
```
